32 devices in a mesh: seq: 2 (over y), batch: 4 (over z), head: 4 (over x, core).
Axes of the slice: x: 2, y: 2, z: 4, core: 2. Of those that a mesh axis runs over, the one named last changes fastest.
Arguments:
- tokens: bfloat16 [4, 1024, 768], P('batch', ('seq', 'head')), may hold values from -6 to 6
- seg_ids: int32 [4, 1024], P('batch'), may hold values from 0 to 11, never falling along the last dimension, each value on 1 to 512 neighbouring positions
- pattern: int32 [12, 16], P('head'), may hold values 0 or 1
- omega: float32 [64, 256], replicated, may hold values from -5 to 5
- norm1_gain: float32 [768], replicated, may hold values from 0.5 to 1.5
- norm1_bias: float32 [768], replicated, may hold values from -1.5 to 1.5
- w_qkv: bfloat16 [768, 3, 768], P(None, None, 'head'), may hold values from -0.21875 to 0.21875
- w_out: bfloat16 [768, 768], P('head'), may hold values from -0.875 to 0.875
- norm2_gain: float32 [768], replicated, may hold values from 0.5 to 1.5
- norm2_bias: float32 [768], replicated, may hold values from -1.5 to 1.5
- w_up: bfloat16 [768, 3072], P(None, 'head'), may hold values from -0.21875 to 0.21875
- w_down: bfloat16 [3072, 768], P('head'), may hold values from -0.109375 to 0.109375
- out_grad: bfloat16 [4, 1024, 768], P('batch', ('seq', 'head')), may hold values from -6 to 6
Outputs:
- mixed: bfloat16 [4, 1024, 768], P('batch', ('seq', 'head'))
- grad_tokens: float32 [4, 1024, 768], P('batch', ('seq', 'head'))
- grad_norm1_gain: float32 [768], P(('seq', 'batch', 'head'))
- grad_norm1_bias: float32 [768], P(('seq', 'batch', 'head'))
- grad_w_qkv: float32 [768, 3, 768], P(('seq', 'batch'), None, 'head')
- grad_w_out: float32 [768, 768], P('head', ('seq', 'batch'))
- grad_norm2_gain: float32 [768], P(('seq', 'batch', 'head'))
- grad_norm2_bias: float32 [768], P(('seq', 'batch', 'head'))
- grad_w_up: float32 [768, 3072], P(('seq', 'batch'), 'head')
- grad_w_down: float32 [3072, 768], P('head', ('seq', 'batch'))
The draws below stay inside these ranges and needn't reach their ends.
Inputs may be any that keep to these rules, and one draw needn't show every extreme that they name: `seg_ids`: along a sequence the document numbers never fall; each document has 1 to 512 tokens and one has exactly that many.
All inputs are finite; a program needn't handle non-finite values. No bound on the sum of `pattern` on one device may be relied on, other than what follows from the above.
Results may differ from the reference program's by a relative error of at most 0.018.
Values may be sent and summed in bfloat16 or wider, within the bound.
A program may use at most 128 MiB of HBM per device.

```python
import math
import jax
import jax.numpy as jnp
import numpy as np
from jax import lax

D = 768
H = 12
DH = 64
M = 256
FF = 3072
BLK = 64
LEN = 1024
NB = 16
SEQS = 4


def plant(values, rng, smallest, high):
    shape = values.shape
    place = [jax.random.randint(jax.random.fold_in(rng, axis), (), 0, shape[axis]) for axis in range(len(shape))]
    values = values.at[tuple(place)].set(smallest)
    longest = shape.index(max(shape))
    place[longest] = (place[longest] + 1) % shape[longest]
    return values.at[tuple(place)].set(high)


def with_spikes(array, rng, source, target, shards_of, factor):
    def block_of(axis_at):
        return (jnp.arange(array.shape[axis_at]) // (array.shape[axis_at] // shards_of)).reshape((-1,) + (1,) * (array.ndim - 1 - axis_at))

    one_side = jax.random.permutation(rng, shards_of)[block_of(target)]
    far = (block_of(target) + shards_of // 2) % shards_of
    return jnp.where((block_of(source) == one_side) | (block_of(source) == far), factor * array, array)


def block_scale(stream_key, extent, pieces, smallest, top_value):
    level = 1.0
    for dim, blocks in pieces:
        heights = jax.random.uniform(jax.random.fold_in(jax.random.fold_in(stream_key, 6), dim), (blocks,), jnp.float32, smallest / len(pieces), top_value / len(pieces))
        level = level * jnp.repeat(jnp.exp(heights), extent[dim] // blocks).reshape((-1,) + (1,) * (len(extent) - 1 - dim))
    return level


def length_profile(count, total, limit, skew):
    portions = [(1 << 20) // math.isqrt(standing ** skew) + 1 for standing in range(2, count + 1)]
    surplus, counts = total - limit - (count - 1), [1] * (count - 1)
    while surplus > 0:
        free = [i for i in range(count - 1) if counts[i] < limit]
        pool, left = sum([portions[i] for i in free]), surplus
        for i in free:
            extra = min(limit - counts[i], max(1, left * portions[i] // pool), surplus)
            counts[i] = counts[i] + extra
            surplus = surplus - extra
    return np.array([limit] + counts)


def ragged(own_key, count, total, reach, slope):
    if count == 2:
        one = jax.random.randint(own_key, (), max(1, total - reach), min(reach, total - 1) + 1)
        return jnp.stack([one, total - one])
    sizes = jnp.asarray(length_profile(count, total, reach, slope), jnp.int32)
    couples = (count - 1) // 2
    giver, sink = sizes[1:1 + 2 * couples:2], sizes[2:2 + 2 * couples:2]
    slack = jnp.minimum(giver - 1, reach - sink)
    moved = jax.random.randint(jax.random.fold_in(own_key, 1), (couples,), 0, 1 << 20) % (slack + 1)
    sizes = sizes.at[1:1 + 2 * couples:2].set(giver - moved).at[2:2 + 2 * couples:2].set(sink + moved)
    return sizes[jax.random.permutation(jax.random.fold_in(own_key, 2), count)]


def gaussian(rng, extent, scale, bound, cuts=(), held_as=jnp.bfloat16):
    values = scale * jax.random.normal(rng, extent, jnp.float32)
    if cuts:
        values = values * block_scale(rng, extent, cuts, -0.22, 0.18)
    return jnp.clip(values, -bound, bound).astype(held_as)


def noise_with(rng, extent, scale, most, shards, heavy, dtype=jnp.bfloat16):
    result = scale * jax.random.normal(rng, extent, jnp.float32)
    if shards:
        result = result * block_scale(rng, extent, shards, -0.22, 0.18)
    return jnp.clip(with_spikes(result, jax.random.fold_in(rng, 3), *heavy), -most, most).astype(dtype)


def setup_inputs(seed: int = 0) -> dict:
    streams_of = jax.random.split(jax.random.key(seed), 14)
    return {
        "tokens": gaussian(streams_of[0], (SEQS, LEN, D), 1.0, 6.0, ((0, 4), (1, 8))),
        "seg_ids": jax.vmap(lambda own: jnp.searchsorted(jnp.cumsum(ragged(own, 12, LEN, LEN // 2, 2)), jnp.arange(LEN), side="right"))(jax.random.split(streams_of[1], SEQS)).reshape((SEQS, LEN)).astype(jnp.int32),
        "pattern": plant((jax.random.randint(streams_of[2], (H, NB), 0, 2) < 1).astype(jnp.int32), jax.random.fold_in(streams_of[2], 1), 0, 1),
        "omega": gaussian(streams_of[3], (DH, M), 1.0, 5.0, (), jnp.float32),
        "norm1_gain": jnp.clip(1.0 + 0.1 * jax.random.normal(streams_of[4], (D,), jnp.float32), 0.5, 1.5),
        "norm1_bias": gaussian(streams_of[5], (D,), 0.3, 1.5, (), jnp.float32),
        "w_qkv": gaussian(streams_of[6], (D, 3, D), D ** -0.5, 0.21875, ((2, 4),)),
        "w_out": gaussian(streams_of[7], (D, D), (D // 16) ** -0.5, 0.875, ((0, 4),)),
        "norm2_gain": jnp.clip(1.0 + 0.1 * jax.random.normal(streams_of[8], (D,), jnp.float32), 0.5, 1.5),
        "norm2_bias": gaussian(streams_of[9], (D,), 0.3, 1.5, (), jnp.float32),
        "w_up": gaussian(streams_of[10], (D, FF), D ** -0.5, 0.21875, ((1, 4),)),
        "w_down": gaussian(streams_of[11], (FF, D), FF ** -0.5, 0.109375, ((0, 4),)),
        "out_grad": noise_with(streams_of[12], (SEQS, LEN, D), 1.0, 6.0, ((0, 4), (1, 8)), (0, 2, 4, 2.0)),
    }


@jax.custom_vjp
def low(v):
    return lax.optimization_barrier(v.astype(jnp.bfloat16)).astype(jnp.float32)

@jax.custom_vjp
def low_back(v):
    return v

def low_keep(v):
    return (low(v), None)

def low_pass(kept, grad):
    return (grad,)

def back_keep(v):
    return (v, None)

def back_low(kept, grad):
    return (low(grad),)
low.defvjp(low_keep, low_pass)
low_back.defvjp(back_keep, back_low)

def layer_norm(values, gain, bias):
    center = values - lax.optimization_barrier(jnp.mean(values, axis=-1, keepdims=True))
    spread = lax.optimization_barrier(jnp.mean(center * center, axis=-1, keepdims=True))
    return center * lax.rsqrt(spread + 1e-05) * gain + bias

def feature_map(values, omega):
    depth = values.shape[-1]
    count = omega.shape[-1]
    scaled = values * depth ** (-0.25)
    projected = jnp.einsum('...td,dm->...tm', scaled, omega, precision=lax.Precision.HIGHEST)
    return jnp.exp(projected - 0.5 * lax.optimization_barrier(jnp.sum(scaled * scaled, axis=-1, keepdims=True))) / math.sqrt(count)

def chain(feat_keys, values, segment):
    batch, heads, length, count = feat_keys.shape
    blocks = length // BLK
    seg_blocks = segment.reshape(batch, blocks, BLK)
    tail_ids = seg_blocks[:, :, -1]
    in_tail = (seg_blocks == tail_ids[:, :, None]).astype(jnp.float32)
    weighted = feat_keys.reshape(batch, heads, blocks, BLK, count) * in_tail[:, None, :, :, None]
    block_v = jnp.einsum('shcjm,shcjd->shcmd', weighted, values.reshape(batch, heads, blocks, BLK, -1), precision=lax.Precision.HIGHEST)
    block_z = lax.optimization_barrier(jnp.sum(weighted, axis=3))
    positions = jnp.arange(blocks)
    linked = ((tail_ids[:, :, None] == tail_ids[:, None, :]) & (positions[:, None] >= positions[None, :])[None]).astype(jnp.float32)
    state_v = jnp.einsum('sbc,shcmd->shbmd', linked, block_v, precision=lax.Precision.HIGHEST)
    state_z = jnp.einsum('sbc,shcm->shbm', linked, block_z, precision=lax.Precision.HIGHEST)
    return (state_v, state_z, tail_ids)

def with_previous(current, first):
    earlier = jnp.concatenate([first[:, :, None], current[:, :, :-1]], axis=2)
    return jnp.concatenate([earlier, current], axis=3)

def attend(query, key_rows, value_rows, key_in, value_in, state_v_in, state_z_in, segment, seg_prev, tail_in, block_pattern, omega):
    batch, heads, length, depth = query.shape
    blocks = length // BLK
    feat_query = feature_map(query, omega)
    feat_keys = feature_map(key_rows, omega)
    feat_in = feature_map(key_in, omega)
    state_v, state_z, tail_ids = chain(feat_keys, value_rows, segment)
    carried = (tail_in[:, 1][:, None] == tail_ids).astype(jnp.float32)
    state_v = state_v + carried[:, None, :, None, None] * state_v_in[:, 1][:, :, None]
    state_z = state_z + carried[:, None, :, None] * state_z_in[:, 1][:, :, None]
    far_v = jnp.concatenate([state_v_in[:, 0][:, :, None], state_v_in[:, 1][:, :, None], state_v[:, :, :blocks - 2]], axis=2)
    far_z = jnp.concatenate([state_z_in[:, 0][:, :, None], state_z_in[:, 1][:, :, None], state_z[:, :, :blocks - 2]], axis=2)
    far_tail = jnp.concatenate([tail_in, tail_ids[:, :blocks - 2]], axis=1)
    seg_blocks = segment.reshape(batch, blocks, BLK)
    far_mask = (seg_blocks == far_tail[:, :, None]).astype(jnp.float32)
    query_feat_blocks = feat_query.reshape(batch, heads, blocks, BLK, -1)
    query_far = query_feat_blocks * far_mask[:, None, :, :, None]
    numer = jnp.einsum('shbim,shbmd->shbid', query_far, far_v, precision=lax.Precision.HIGHEST)
    denom = jnp.einsum('shbim,shbm->shbi', query_far, far_z, precision=lax.Precision.HIGHEST)
    query_blocks = query.reshape(batch, heads, blocks, BLK, depth)
    key_window = with_previous(key_rows.reshape(batch, heads, blocks, BLK, depth), key_in)
    value_window = with_previous(value_rows.reshape(batch, heads, blocks, BLK, depth), value_in)
    feat_window = with_previous(feat_keys.reshape(batch, heads, blocks, BLK, -1), feat_in)
    seg_earlier = jnp.concatenate([seg_prev[:, None], seg_blocks[:, :-1]], axis=1)
    seg_window = jnp.concatenate([seg_earlier, seg_blocks], axis=2)
    scores = jnp.einsum('shbid,shbjd->shbij', query_blocks, key_window, precision=lax.Precision.HIGHEST) / math.sqrt(depth)
    lowrank = jnp.einsum('shbim,shbjm->shbij', query_feat_blocks, feat_window, precision=lax.Precision.HIGHEST)
    row_pos = jnp.arange(BLK)[:, None]
    col_pos = jnp.arange(2 * BLK)[None, :]
    causal = (col_pos < BLK) | (col_pos - BLK <= row_pos)
    same_doc = seg_blocks[:, :, :, None] == seg_window[:, :, None, :]
    allowed = (same_doc & causal[None, None]).astype(jnp.float32)[:, None]
    exact = jnp.where(col_pos >= BLK, 1.0, block_pattern.astype(jnp.float32)[:, :, None, None])
    weights = allowed * (exact * jnp.exp(scores) + (1.0 - exact) * lowrank)
    numer = numer + jnp.einsum('shbij,shbjd->shbid', weights, value_window, precision=lax.Precision.HIGHEST)
    denom = denom + lax.optimization_barrier(jnp.sum(weights, axis=-1))
    return (numer / denom[..., None]).reshape(batch, heads, length, depth)

def forward(inputs, params, segment, pattern, omega):
    gain_one, bias_one, w_qkv, w_out, gain_two, bias_two, w_up, w_down = params
    batch, length, width = inputs.shape
    heads = w_qkv.shape[2] // DH
    normed_one = low(layer_norm(inputs, gain_one, bias_one))
    qkv = low(low_back(jnp.einsum('std,dce->stce', normed_one, w_qkv, precision=lax.Precision.HIGHEST)))

    def split_heads(part):
        return part.reshape(batch, length, heads, DH).transpose(0, 2, 1, 3)
    query, key_rows, value_rows = (split_heads(qkv[:, :, 0]), split_heads(qkv[:, :, 1]), split_heads(qkv[:, :, 2]))
    zero_block = jnp.zeros((batch, heads, BLK, DH), jnp.float32)
    zero_v = jnp.zeros((batch, 2, heads, omega.shape[1], DH), jnp.float32)
    zero_z = jnp.zeros((batch, 2, heads, omega.shape[1]), jnp.float32)
    seg_prev = jnp.full((batch, BLK), -1, jnp.int32)
    tail_in = jnp.full((batch, 2), -1, jnp.int32)
    attended = attend(query, key_rows, value_rows, zero_block, zero_block, zero_v, zero_z, segment, seg_prev, tail_in, pattern, omega)
    attended = low(attended.transpose(0, 2, 1, 3).reshape(batch, length, width))
    hidden_one = inputs + low_back(jnp.einsum('ste,ed->std', attended, w_out, precision=lax.Precision.HIGHEST))
    normed_two = low(layer_norm(hidden_one, gain_two, bias_two))
    upper = low_back(jnp.einsum('std,df->stf', normed_two, w_up, precision=lax.Precision.HIGHEST))
    activated = low(jax.nn.gelu(upper, approximate=True))
    return hidden_one + jnp.einsum('stf,fd->std', activated, w_down, precision=lax.Precision.HIGHEST)

def reference(tokens, seg_ids, pattern, omega, norm1_gain, norm1_bias, w_qkv, w_out, norm2_gain, norm2_bias, w_up, w_down, out_grad):
    params = tuple((item.astype(jnp.float32) for item in (norm1_gain, norm1_bias, w_qkv, w_out, norm2_gain, norm2_bias, w_up, w_down)))
    omega_f = omega.astype(jnp.float32)
    group = math.gcd(SEQS, max(1, 4096 // LEN))
    count = SEQS // group
    inputs = tokens.astype(jnp.float32).reshape(count, group, LEN, D)
    segments = seg_ids.reshape(count, group, LEN)
    cotangents = out_grad.astype(jnp.float32).reshape(count, group, LEN, D)

    def step(total, item):
        group_in, group_seg, group_cot = item

        def run(values, weights):
            return forward(values, weights, group_seg, pattern, omega_f)
        outputs, pull = jax.vjp(run, group_in, params)
        grad_in, grad_params = pull(group_cot)
        total = jax.tree.map(jnp.add, total, grad_params)
        return (total, (outputs.astype(jnp.bfloat16), grad_in))
    zeros = jax.tree.map(jnp.zeros_like, params)
    total, (outputs, grad_in) = lax.scan(step, zeros, (inputs, segments, cotangents))
    return (outputs.reshape(SEQS, LEN, D), grad_in.reshape(SEQS, LEN, D), total[0], total[1], total[2], total[3], total[4], total[5], total[6], total[7])
```

```python
import functools
import math
from types import SimpleNamespace

import jax
import jax.numpy as jnp
from jax import lax
from jax.experimental import pallas as pl
from jax.experimental.pallas import tpu as pltpu
from jax.sharding import PartitionSpec as P

DH = 64
BLK = 64
LANES = 128
TILE = 128
STATE = 80
F32 = jnp.float32
BF16 = jnp.bfloat16
MESH = pl.DeviceIdType.MESH


def nn(a, b):
    return lax.dot_general(a, b, (((1,), (0,)), ((), ())), preferred_element_type=F32)


def nt(a, b):
    return lax.dot_general(a, b, (((1,), (1,)), ((), ())), preferred_element_type=F32)


def tn(a, b):
    return lax.dot_general(a, b, (((0,), (0,)), ((), ())), preferred_element_type=F32)


def normalize(x):
    center = x - jnp.mean(x, axis=-1, keepdims=True)
    rstd = lax.rsqrt(jnp.mean(center * center, axis=-1, keepdims=True) + 1e-05)
    return center * rstd, rstd


def norm_back(grad, gain, xhat, rstd):
    g = grad * gain
    return rstd * (
        g - jnp.mean(g, axis=-1, keepdims=True) - xhat * jnp.mean(g * xhat, axis=-1, keepdims=True)
    )


def gelu_both(u):
    k0 = math.sqrt(2.0 / math.pi)
    u2 = u * u
    th = jnp.tanh(k0 * (u + 0.044715 * u2 * u))
    half = 0.5 * (1.0 + th)
    slope = half + 0.5 * u * (1.0 - th * th) * (k0 * (1.0 + 3.0 * 0.044715 * u2))
    return u * half, slope


class Plan:
    def __init__(self):
        self.shapes = []
        self.tree = {}

    def add(self, into=None, **buffers):
        into = self.tree if into is None else into
        for name, (shape, dtype) in buffers.items():
            into[name] = len(self.shapes)
            self.shapes.append(pltpu.VMEM(shape, dtype))

    def group(self, **groups):
        for name, buffers in groups.items():
            self.tree[name] = {}
            self.add(self.tree[name], **buffers)

    def semaphores(self, **counts):
        for name, n in counts.items():
            self.tree[name] = len(self.shapes)
            self.shapes.append(pltpu.SemaphoreType.DMA((n,)))

    def bind(self, refs):
        def walk(tree):
            return SimpleNamespace(
                **{k: walk(v) if isinstance(v, dict) else refs[v] for k, v in tree.items()}
            )

        return walk(self.tree)


def make_kernel(dims, n_in, n_out, plan):
    nh, ns, nb, T, R, D, E, FL, H, M, inner = dims
    nt_tiles = T // TILE
    half_rows = D // ns
    piece = D // (ns * nb)

    def kernel(*refs):
        (
            tok_hbm, seg_ref, pat_ref, omega_ref, g1_ref, b1_ref, wqkv_hbm, wout_hbm,
            g2_ref, b2_ref, wup_hbm, wdown_hbm, og_hbm,
        ) = refs[:n_in]
        (
            mixed_ref, gtok_ref, norm_ref, oqkv_ref, oout_ref, oup_ref, odown_ref,
        ) = refs[n_in : n_in + n_out]
        s = plan.bind(refs[n_in + n_out :])
        ssem, rsem, lsem = s.ssem, s.rsem, s.lsem
        used = {"r": 0, "l": 0}
        sends = []

        head = lax.axis_index("head")
        seq = lax.axis_index("seq")
        bat = lax.axis_index("batch")
        h1 = head + 1 - 2 * lax.rem(head, 2)
        h2 = lax.rem(head + 2, nh)
        h3 = lax.rem(h1 + 2, nh)
        other = 1 - seq

        def local(src, dst):
            k = used["l"]
            used["l"] += 1
            c = pltpu.make_async_copy(src, dst, lsem.at[k])
            c.start()
            return c

        def send(src, dst, **dev):
            k = used["r"]
            used["r"] += 1
            c = pltpu.make_async_remote_copy(
                src_ref=src, dst_ref=dst, send_sem=ssem.at[k], recv_sem=rsem.at[k],
                device_id=dev, device_id_type=MESH,
            )
            c.start()
            sends.append(c)
            return c

        def rows(slot, n=TILE):
            return pl.ds(pl.multiple_of(slot * n, n), n)

        c_tok = local(tok_hbm.at[0], s.tok.at[head])
        c_wqkv = local(wqkv_hbm, s.wqkv)
        c_wout = local(wout_hbm, s.wo.at[head])
        c_og = local(og_hbm.at[0], s.og.at[head])
        c_wup = local(wup_hbm, s.wup)
        c_wdown = local(wdown_hbm, s.wdown)
        barrier = pltpu.get_barrier_semaphore()
        peers = [dict(head=h1), dict(head=h2), dict(head=h3), dict(seq=other)]
        if inner:
            peers += [dict(batch=lax.rem(bat + d, nb)) for d in range(1, nb)]
        for dev in peers:
            pl.semaphore_signal(barrier, inc=1, device_id=dev, device_id_type=MESH)
        pl.semaphore_wait(barrier, len(peers))

        def gather_start(buf, chunks):
            n = buf.shape[1] // chunks
            out = []
            for i in range(chunks):
                part = buf.at[head, pl.ds(i * n, n)]
                across = send(part, part, head=h2)
                beside = send(part, part, head=h1)
                out.append((across, beside, i * n, n))
            return out

        def gather_forward(buf, started):
            out = []
            for across, _, lo, n in started:
                across.wait_recv()
                part = buf.at[h2, pl.ds(lo, n)]
                out.append(send(part, part, head=h1))
            return out

        c_tok.wait()
        ag_tok = gather_start(s.tok, 2)

        lane = lax.broadcasted_iota(jnp.int32, (1, LANES), 1)
        low = lane < DH
        ones_lanes = ((lane == DH) | (lane == DH + 1)).astype(F32)
        seg_all = seg_ref[...].astype(F32)
        first = seq == 0
        seg_half = jnp.where(first, seg_all[:, :T], seg_all[:, T : 2 * T])
        seg_prev = jnp.where(first, -1.0, seg_all[:, T - BLK : T])
        tail_one = jnp.where(first, -1.0, jnp.broadcast_to(seg_all[:, T - 1 : T], (1, LANES)))
        tail_two = jnp.where(
            first, -1.0, jnp.broadcast_to(seg_all[:, T - BLK - 1 : T - BLK], (1, LANES))
        )
        s.segrow[...] = jnp.broadcast_to(seg_half, (8, T))
        s.segcol[...] = jnp.transpose(jnp.broadcast_to(seg_half, (LANES, T)))
        segcol = s.segcol[...]
        row_id = lax.broadcasted_iota(jnp.int32, (T, LANES), 0)
        mask_one = (segcol == segcol[T - 1 : T, :]).astype(F32)
        mask_two = ((segcol == segcol[T - BLK - 1 : T - BLK, :]) & (row_id < T - BLK)).astype(F32)
        s.m1[...] = mask_one
        s.m0[...] = mask_two
        s.mfar[...] = jnp.where(
            row_id < BLK, (segcol == tail_two).astype(F32), (segcol == tail_one).astype(F32)
        )
        nblk = pat_ref.shape[1]
        per_half = T // BLK
        hot = (
            lax.broadcasted_iota(jnp.int32, (T, nblk), 1)
            == lax.broadcasted_iota(jnp.int32, (T, nblk), 0) // BLK + seq * per_half
        ).astype(F32)
        pat = pat_ref[...].astype(F32)
        for h in range(H):
            s.thr[h] = 3.0 - nn(
                (hot * pat[h : h + 1, :]).astype(BF16), jnp.ones((nblk, LANES), BF16)
            )
        wrow = lax.broadcasted_iota(jnp.int32, (TILE, 2 * TILE), 0)
        wcol = lax.broadcasted_iota(jnp.int32, (TILE, 2 * TILE), 1)
        dist = 2 + wrow // BLK - wcol // BLK
        kind = jnp.where(
            dist >= 2,
            1.0,
            jnp.where(dist == 1, 2.0, jnp.where((dist == 0) & (wcol - TILE <= wrow), 3.0, 0.0)),
        )
        for t in range(nt_tiles):
            col = segcol[t * TILE : (t + 1) * TILE, :]
            for side in range(2):
                tile = t - 1 + side
                if tile < 0:
                    continue
                same = col == s.segrow[0:1, tile * TILE : (tile + 1) * TILE]
                s.code[t, :, side * TILE : (side + 1) * TILE] = jnp.where(
                    same, kind[:, side * TILE : (side + 1) * TILE], 0.0
                )
        scale = DH ** (-0.25)
        om = omega_ref[...] * scale
        om_high = om.astype(BF16)
        s.omst[0:DH, :] = om_high
        s.omst[DH : 2 * DH, :] = (om - om_high.astype(F32)).astype(BF16)
        s.omtmp[...] = jnp.zeros((LANES, M), F32)
        s.omtmp[0:DH, :] = om
        s.omtmp[DH : DH + 8, :] = (
            lax.broadcasted_iota(jnp.int32, (8, M), 0) == 0
        ).astype(F32)
        s.omt[...] = jnp.transpose(s.omtmp[...]).astype(BF16)
        c_wqkv.wait()
        for c in range(3):
            for h in range(H):
                src = s.wqkv[c * E + h * DH : c * E + (h + 1) * DH, :]
                base = (c * H + h) * LANES
                s.wpad[base : base + DH, :] = src
                s.wpad[base + DH : base + 2 * DH, :] = src if c < 2 else jnp.zeros_like(src)
        c_wout.wait()
        for h in range(H):
            s.wopad[h * LANES : h * LANES + DH, :] = s.wo[head, h * DH : (h + 1) * DH, :]
            s.wopad[h * LANES + DH : (h + 1) * LANES, :] = jnp.zeros((DH, D), BF16)
        for h in range(H):
            for i in range(2):
                s.rin[h, i, STATE:LANES, :] = jnp.zeros((LANES - STATE, M), BF16)
                s.grin[h, i, STATE:LANES, :] = jnp.zeros((LANES - STATE, M), BF16)

        def features(twice):
            x = twice.astype(F32)
            square = jnp.sum(x * x, axis=-1, keepdims=True)
            projected = nn(twice, s.omst[...])
            return jnp.exp(projected - square * (scale * scale * 0.25)) * (1.0 / math.sqrt(M))

        gain1, bias1 = g1_ref[...], b1_ref[...]
        gain2, bias2 = g2_ref[...], b2_ref[...]

        def project(slot):
            xhat, _ = normalize(s.tok[slot].astype(F32))
            normed = (xhat * gain1 + bias1).astype(BF16)
            at = rows(slot)
            s.n1[at, :] = normed
            for c in range(3):
                out = nt(normed, s.wpad[c * H * LANES : (c + 1) * H * LANES, :])
                for h in range(H):
                    part = out[:, h * LANES : (h + 1) * LANES]
                    if c == 2:
                        s.v[h, at, :] = (part + ones_lanes).astype(BF16)
                    else:
                        low_part = part.astype(BF16)
                        (s.q, s.k)[c][h, at, :] = low_part
                        (s.fq, s.fk)[c][h, at, :] = features(low_part).astype(BF16)

        project(head)
        for _, beside, _, _ in ag_tok:
            beside.wait_recv()
        project(h1)
        fw_tok = gather_forward(s.tok, ag_tok)
        ag_wo = gather_start(s.wo, 1)
        project(h2)
        for c in fw_tok:
            c.wait_recv()
        project(h3)

        for h in range(H):
            fk = s.fk[h]
            v = s.v[h].astype(F32)
            v1 = (v * s.m1[...]).astype(BF16)
            v0 = (v * s.m0[...]).astype(BF16)
            s.v1[h] = v1
            s.v0[h] = v0
            s.rout[h, 0] = tn(v0, fk)[:STATE].astype(BF16)
            s.rout[h, 1] = tn(v1, fk)[:STATE].astype(BF16)
            kk = s.k[h, T - BLK : T, :].astype(F32)
            vv = v[T - BLK : T, :]
            s.kvout[h] = jnp.where(low, kk, pltpu.roll(vv, DH, 1)).astype(BF16)
        ex_kv = send(s.kvout, s.kvin, seq=other)
        ex_r = [
            send(s.rout.at[h], s.rin.at[h, :, pl.ds(0, STATE)], seq=other) for h in range(H)
        ]

        def attend(h, carry):
            for t in range(nt_tiles):
                lo, hi = t * TILE, (t + 1) * TILE
                w0 = max(0, lo - TILE)
                fq = s.fq[h, lo:hi, :]
                low_rank = nt(fq, s.fk[h, 0:hi, :])
                exact = jnp.exp(nt(s.q[h, lo:hi, :], s.k[h, w0:hi, :]) * (0.5 / math.sqrt(DH)))
                tiles = (hi - w0) // TILE
                code = s.code[t, :, (2 - tiles) * TILE :]
                thr = jnp.concatenate([s.thr[h, lo:hi, :]] * tiles, axis=1)
                near = jnp.where(
                    code >= thr, exact, jnp.where(code >= 1.0, low_rank[:, w0:], 0.0)
                )
                if w0 > 0:
                    col = jnp.concatenate([s.segcol[lo:hi, :]] * (w0 // TILE), axis=1)
                    far = jnp.where(col == s.segrow[0:1, 0:w0], low_rank[:, :w0], 0.0)
                    near = jnp.concatenate([far, near], axis=1)
                w = near.astype(BF16)
                s.w[h, lo:hi, 0:hi] = w
                s.acc[h, lo:hi, :] = nn(w, s.v[h, 0:hi, :])
            return carry

        lax.fori_loop(0, H, attend, 0)
        fw_wo = gather_forward(s.wo, ag_wo)
        c_og.wait()
        ag_og = gather_start(s.og, 1)

        ex_kv.wait_recv()
        for c in ex_r:
            c.wait_recv()

        def unpack(packed):
            x = packed.astype(F32)
            turned = pltpu.roll(x, DH, 1)
            twice = jnp.where(low, x, turned).astype(BF16)
            return twice, jnp.where(low, turned, 0.0)

        same_in = s.segcol[0:BLK, 0:BLK] == seg_prev
        for h in range(H):
            k_in, v_in = unpack(s.kvin[h])
            v_in = (v_in + ones_lanes).astype(BF16)
            f_in = features(k_in).astype(BF16)
            s.kin[h] = k_in
            s.vin[h] = v_in
            s.fin[h] = f_in
            q0 = s.q[h, 0:BLK, :]
            fq0 = s.fq[h, 0:BLK, :]
            exact = jnp.exp(nt(q0, k_in) * (0.5 / math.sqrt(DH)))
            low_rank = nt(fq0, f_in)
            use_exact = s.thr[h, 0:BLK, 0:BLK] < 2.5
            w_in = jnp.where(same_in, jnp.where(use_exact, exact, low_rank), 0.0).astype(BF16)
            s.win[h] = w_in
            far0 = jnp.where(
                s.mfar[0:BLK, :] > 0.5, nt(fq0, s.rin[h, 0]), 0.0
            )
            s.acc[h, 0:BLK, :] = s.acc[h, 0:BLK, :] + nn(w_in, v_in) + far0
            far1 = jnp.where(
                s.mfar[BLK:T, :] > 0.5, nt(s.fq[h, BLK:T, :], s.rin[h, 1]), 0.0
            )
            s.acc[h, BLK:T, :] = s.acc[h, BLK:T, :] + far1

        def divided(h, lo, hi):
            acc = s.acc[h, lo:hi, :]
            inv = 1.0 / acc[:, DH : DH + 1]
            return acc * inv, inv

        ag_at = []
        fw_at = []
        for t in range(nt_tiles):
            lo, hi = t * TILE, (t + 1) * TILE
            outs = [divided(h, lo, hi)[0] for h in range(H)]
            for h in range(0, H, 2):
                if h + 1 < H:
                    both = jnp.where(low, outs[h], pltpu.roll(outs[h + 1], DH, 1))
                    s.at[head, lo:hi, h * DH : (h + 2) * DH] = both.astype(BF16)
                else:
                    s.at[head, lo:hi, h * DH : (h + 1) * DH] = outs[h][:, :DH].astype(BF16)
            part = s.at.at[head, pl.ds(lo, TILE)]
            ag_at.append((send(part, part, head=h2), send(part, part, head=h1), lo, TILE))
        for c in fw_wo:
            c.wait_recv()
        for _, c, _, _ in ag_wo:
            c.wait_recv()
        fw_at = gather_forward(s.at, ag_at)
        fw_og = gather_forward(s.og, ag_og)
        for _, c, _, _ in ag_og:
            c.wait_recv()
        for c in fw_og:
            c.wait_recv()
        for _, c, _, _ in ag_at:
            c.wait_recv()
        for c in fw_at:
            c.wait_recv()
        c_wup.wait()
        c_wdown.wait()

        def scatter_sum(make, bufs):
            out, got = bufs.out, bufs.got
            out[0] = make(h3).astype(BF16)
            a = send(out.at[0], got.at[0], head=h1)
            mine = make(h2)
            a.wait_recv()
            out[1] = (mine + got[0].astype(F32)).astype(BF16)
            b = send(out.at[1], got.at[1], head=h2)
            out[2] = make(h1).astype(BF16)
            c = send(out.at[2], got.at[2], head=h1)
            return (b, c)

        def scatter_done(pending, bufs, own):
            got = bufs.got
            b, c = pending
            c.wait_recv()
            b.wait_recv()
            return own + got[1].astype(F32) + got[2].astype(F32)

        def feed(slot):
            at = rows(slot)
            hid = s.tok[slot].astype(F32)
            for j in range(nh):
                hid = hid + nn(s.at[j, at, :], s.wo[j])
            s.hid[at, :] = hid
            xhat, _ = normalize(hid)
            normed = (xhat * gain2 + bias2).astype(BF16)
            s.n2[at, :] = normed
            act, slope = gelu_both(nn(normed, s.wup[...]))
            s.act[at, :] = act.astype(BF16)
            gu = (nt(s.og[slot], s.wdown[...]) * slope).astype(BF16)
            s.gu[at, :] = gu
            return nt(gu, s.wup[...])

        pend = scatter_sum(feed, s.ra)
        own = feed(head)

        def weight_grad(name, left, right):
            a = left(pl.ds(pl.multiple_of(other * half_rows, LANES), half_rows))
            b = right()
            if inner:
                name.ys[...] = tn(a, b).astype(BF16)
                c = send(name.ys, name.yr, seq=other)
                a = left(pl.ds(pl.multiple_of(seq * half_rows, LANES), half_rows))
                name.own[...] = tn(a, b)
                return c
            return None

        def weight_cross(name, c):
            c.wait_recv()
            out = []
            for d in range(1, nb):
                at = rows(lax.rem(bat + d, nb), piece)
                name.zs[d - 1] = (
                    name.own[at, :] + name.yr[at, :].astype(F32)
                ).astype(BF16)
                out.append(
                    send(
                        name.zs.at[d - 1], name.zr.at[d - 1],
                        batch=lax.rem(bat + d, nb),
                    )
                )
            return out

        def weight_sum(name, cs):
            at = rows(bat, piece)
            total = name.own[at, :] + name.yr[at, :].astype(F32)
            for d, c in enumerate(cs):
                c.wait_recv()
                total = total + name.zr[d].astype(F32)
            return total

        def og_cols(at):
            return jnp.concatenate([s.og[j, :, at] for j in range(nh)], axis=0)

        if inner:
            y_down = weight_grad(s.wd, og_cols, lambda: s.act[...])

        grad2 = scatter_done(pend, s.ra, own)
        mine = rows(head)
        xhat2, rstd2 = normalize(s.hid[mine, :])
        s.ns[...] = jnp.zeros_like(s.ns)
        s.ns[2:3, :] = jnp.sum(grad2 * xhat2, axis=0, keepdims=True)
        s.ns[3:4, :] = jnp.sum(grad2, axis=0, keepdims=True)
        grad_hidden = s.og[head].astype(F32) + norm_back(grad2, gain2, xhat2, rstd2)
        s.gh[...] = grad_hidden
        s.gb[head] = grad_hidden.astype(BF16)
        ag_gb = gather_start(s.gb, 2)
        if inner:
            y_up = weight_grad(s.wu, lambda at: s.n2[:, at], lambda: s.gu[...])

        def divide_back(slot):
            at = rows(slot)
            ga = nt(s.gb[slot], s.wopad[...])
            for h in range(H):
                acc = s.acc[h, at, :]
                inv = 1.0 / acc[:, DH : DH + 1]
                gnum = ga[:, h * LANES : (h + 1) * LANES] * inv
                gden = -jnp.sum(gnum * acc, axis=-1, keepdims=True) * inv
                high = gden.astype(BF16).astype(F32)
                gnum = jnp.where(lane == DH, high, jnp.where(lane == DH + 1, gden - high, gnum))
                s.gn[h, at, :] = gnum.astype(BF16)

        divide_back(head)
        for _, c, _, _ in ag_gb:
            c.wait_recv()
        divide_back(h1)
        fw_gb = gather_forward(s.gb, ag_gb)
        divide_back(h2)
        for c in fw_gb:
            c.wait_recv()
        divide_back(h3)

        def feature_back(gfeat, feat, twice):
            x = nn((gfeat * feat.astype(F32)).astype(BF16), s.omt[...])
            return x - twice.astype(F32) * (x[:, DH : DH + 1] * (scale * scale))

        for h in range(H):
            gm = jnp.where(s.mfar[...] > 0.5, s.gn[h].astype(F32), 0.0).astype(BF16)
            s.gm[h] = gm
            s.grout[h, 0] = tn(gm[0:BLK, :], s.fq[h, 0:BLK, :])[:STATE].astype(BF16)
            s.grout[h, 1] = tn(gm[BLK:T, :], s.fq[h, BLK:T, :])[:STATE].astype(BF16)
            gn0 = s.gn[h, 0:BLK, :]
            q0 = s.q[h, 0:BLK, :]
            fq0 = s.fq[h, 0:BLK, :]
            gw = nt(gn0, s.vin[h])
            w_in = s.win[h]
            use_exact = s.thr[h, 0:BLK, 0:BLK] < 2.5
            gs = jnp.where(
                same_in & use_exact, gw * w_in.astype(F32) * (1.0 / math.sqrt(DH)), 0.0
            ).astype(BF16)
            gp = jnp.where(same_in & jnp.logical_not(use_exact), gw, 0.0).astype(BF16)
            gk = feature_back(tn(gp, fq0), s.fin[h], s.kin[h]) + tn(gs, q0)
            gv = tn(w_in, gn0)
            s.gkvout[h] = jnp.where(low, gk, pltpu.roll(gv, DH, 1)).astype(BF16)
            s.gfq0[h] = nn(gp, s.fin[h])
            s.gq0[h] = nn(gs, s.kin[h])
        ex_gkv = send(s.gkvout, s.gkvin, seq=other)
        ex_gr = [
            send(s.grout.at[h], s.grin.at[h, :, pl.ds(0, STATE)], seq=other) for h in range(H)
        ]

        if inner:
            z_down = weight_cross(s.wd, y_down)

        def attend_back(h, carry):
            for t in range(nt_tiles):
                lo, hi = t * TILE, (t + 1) * TILE
                w0 = max(0, lo - TILE)
                tiles = (hi - w0) // TILE
                gw = nt(s.gn[h, lo:hi, :], s.v[h, 0:hi, :])
                code = s.code[t, :, (2 - tiles) * TILE :]
                thr = jnp.concatenate([s.thr[h, lo:hi, :]] * tiles, axis=1)
                use_exact = code >= thr
                near = gw[:, w0:]
                gs = jnp.where(
                    use_exact,
                    near * s.w[h, lo:hi, w0:hi].astype(F32) * (1.0 / math.sqrt(DH)),
                    0.0,
                ).astype(BF16)
                gp = jnp.where((code >= 1.0) & (code < thr), near, 0.0)
                if w0 > 0:
                    col = jnp.concatenate([s.segcol[lo:hi, :]] * (w0 // TILE), axis=1)
                    far = jnp.where(col == s.segrow[0:1, 0:w0], gw[:, :w0], 0.0)
                    gp = jnp.concatenate([far, gp], axis=1)
                gp = gp.astype(BF16)
                s.gp[lo:hi, 0:hi] = gp
                s.gs[lo:hi, (2 - tiles) * TILE :] = gs
                gfq = nn(gp, s.fk[h, 0:hi, :])
                gq = nn(gs, s.k[h, w0:hi, :])
                gm = s.gm[h, lo:hi, :]
                if t == 0:
                    top = nn(gm[0:BLK], s.rin[h, 0]) + s.gfq0[h]
                    bottom = nn(gm[BLK:], s.rin[h, 1])
                    gfq = gfq + jnp.concatenate([top, bottom], axis=0)
                    gq = gq + jnp.concatenate(
                        [s.gq0[h], jnp.zeros((TILE - BLK, LANES), F32)], axis=0
                    )
                else:
                    gfq = gfq + nn(gm, s.rin[h, 1])
                gq = gq + feature_back(gfq, s.fq[h, lo:hi, :], s.q[h, lo:hi, :])
                s.gq[h, lo:hi, :] = gq
            for t in range(nt_tiles):
                lo, hi = t * TILE, (t + 1) * TILE
                s.gfk[h, lo:hi, :] = tn(s.gp[lo:T, lo:hi], s.fq[h, lo:T, :])
                s.gv[h, lo:hi, :] = tn(s.w[h, lo:T, lo:hi], s.gn[h, lo:T, :])
                gk = tn(s.gs[lo:hi, TILE:], s.q[h, lo:hi, :])
                if t + 1 < nt_tiles:
                    gk = gk + tn(s.gs[hi : hi + TILE, :TILE], s.q[h, hi : hi + TILE, :])
                s.gk[h, lo:hi, :] = gk
            return carry

        lax.fori_loop(0, H, attend_back, 0)

        def gb_cols(at):
            return jnp.concatenate([s.gb[j, :, at] for j in range(nh)], axis=0)

        if inner:
            y_out = weight_grad(s.wo_g, gb_cols, lambda: s.at[head])
            z_up = weight_cross(s.wu, y_up)

        ex_gkv.wait_recv()
        for c in ex_gr:
            c.wait_recv()

        def finish(h, carry):
            v1, v0 = s.v1[h], s.v0[h]
            r0 = jnp.where(first, s.grin[h, 0].astype(F32), 0.0).astype(BF16)
            r1 = jnp.where(first, s.grin[h, 1].astype(F32), 0.0).astype(BF16)
            gfk = s.gfk[h] + nn(v0, r0) + nn(v1, r1)
            fk = s.fk[h]
            gv = s.gv[h] + s.m0[...] * nt(fk, r0) + s.m1[...] * nt(fk, r1)
            gk = s.gk[h] + feature_back(gfk, fk, s.k[h])
            s.gk[h] = gk
            s.gv[h] = gv
            back = jnp.where(first, s.gkvin[h].astype(F32), 0.0)
            s.gk[h, T - BLK : T, :] = s.gk[h, T - BLK : T, :] + back
            s.gv[h, T - BLK : T, :] = s.gv[h, T - BLK : T, :] + pltpu.roll(back, DH, 1)
            return carry

        lax.fori_loop(0, H, finish, 0)
        parts = [(n, h) for n in (s.gq, s.gk, s.gv) for h in range(H)]
        for i in range(0, len(parts), 2):
            (na, ha) = parts[i]
            a = na[ha]
            if i + 1 < len(parts):
                (nb_, hb) = parts[i + 1]
                a = jnp.where(low, a, pltpu.roll(nb_[hb], DH, 1))
                s.gqkv[:, i * DH : (i + 2) * DH] = a.astype(BF16)
            else:
                s.gqkv[:, i * DH : (i + 1) * DH] = a[:, :DH].astype(BF16)

        if inner:
            y_qkv = weight_grad(s.wx, lambda at: s.n1[:, at], lambda: s.gqkv[...])

        pend = scatter_sum(lambda slot: nn(s.gqkv[rows(slot), :], s.wqkv[...]), s.rb)
        own = nn(s.gqkv[mine, :], s.wqkv[...])
        if inner:
            z_out = weight_cross(s.wo_g, y_out)

        pend_mixed = scatter_sum(lambda slot: nn(s.act[rows(slot), :], s.wdown[...]), s.rc)
        own_mixed = nn(s.act[mine, :], s.wdown[...])

        grad1 = scatter_done(pend, s.rb, own)
        xhat1, rstd1 = normalize(s.tok[head].astype(F32))
        s.ns[0:1, :] = jnp.sum(grad1 * xhat1, axis=0, keepdims=True)
        s.ns[1:2, :] = jnp.sum(grad1, axis=0, keepdims=True)
        gtok_ref[0] = s.gh[...] + norm_back(grad1, gain1, xhat1, rstd1)

        if inner:
            n_z = [
                send(s.ns, s.nz.at[d - 1], batch=lax.rem(bat + d, nb)) for d in range(1, nb)
            ]
            z_qkv = weight_cross(s.wx, y_qkv)
        mixed_ref[0] = (s.hid[mine, :] + scatter_done(pend_mixed, s.rc, own_mixed)).astype(BF16)

        if inner:
            total = s.ns[...]
            for d, c in enumerate(n_z):
                c.wait_recv()
                total = total + s.nz[d]
            s.ns2[...] = total
            c = send(s.ns2, s.ny, seq=other)
            odown_ref[...] = weight_sum(s.wd, z_down)
            oup_ref[...] = weight_sum(s.wu, z_up)
            c.wait_recv()
            s.ns3[...] = total + s.ny[...]
            n_h = [send(s.ns3, s.nh.at[i], head=d) for i, d in enumerate((h1, h2, h3))]
            s.otmp[...] = jnp.zeros_like(s.otmp)
            s.otmp[0:piece, 0:E] = weight_sum(s.wo_g, z_out)
            oout_ref[...] = jnp.transpose(s.otmp[...])[:E, :piece]
            total = s.ns3[...]
            for i, c in enumerate(n_h):
                c.wait_recv()
                total = total + s.nh[i]
            width = D // (ns * nb * nh)
            start = ((seq * nb + bat) * nh + head) * width
            pick = (
                lax.broadcasted_iota(jnp.int32, (D, LANES), 0)
                == lax.broadcasted_iota(jnp.int32, (D, LANES), 1) + start
            ).astype(F32)
            norm_ref[...] = lax.dot_general(
                total, pick, (((1,), (0,)), ((), ())),
                precision=lax.Precision.HIGHEST, preferred_element_type=F32,
            )
            gx = weight_sum(s.wx, z_qkv)
            for c in range(3):
                oqkv_ref[c] = gx[:, c * E : (c + 1) * E]
        else:
            norm_ref[...] = s.ns[...]
            odown_ref[...] = tn(og_cols(slice(0, D)), s.act[...])
            oup_ref[...] = tn(s.n2[...], s.gu[...])
            oout_ref[...] = tn(gb_cols(slice(0, D)), s.at[head])
            oqkv_ref[...] = tn(s.n1[...], s.gqkv[...])
        for c in sends:
            c.wait_send()

    return kernel


def build(dims):
    nh, ns, nb, T, R, D, E, FL, H, M, inner = dims
    plan = Plan()
    piece = D // (ns * nb)
    half = D // ns
    plan.add(
        tok=((nh, R, D), BF16),
        og=((nh, R, D), BF16),
        wqkv=((3 * E, D), BF16),
        wo=((nh, E, D), BF16),
        wup=((D, FL), BF16),
        wdown=((FL, D), BF16),
        wpad=((3 * H * LANES, D), BF16),
        wopad=((H * LANES, D), BF16),
        segrow=((8, T), F32),
        segcol=((T, LANES), F32),
        m0=((T, LANES), F32),
        m1=((T, LANES), F32),
        mfar=((T, LANES), F32),
        thr=((H, T, LANES), F32),
        code=((T // TILE, TILE, 2 * TILE), F32),
        omst=((2 * DH, M), BF16),
        omtmp=((LANES, M), F32),
        omt=((M, LANES), BF16),
        n1=((T, D), BF16),
        q=((H, T, LANES), BF16),
        k=((H, T, LANES), BF16),
        v=((H, T, LANES), BF16),
        v0=((H, T, LANES), BF16),
        v1=((H, T, LANES), BF16),
        gn=((H, T, LANES), BF16),
        gm=((H, T, LANES), BF16),
        fq=((H, T, M), BF16),
        fk=((H, T, M), BF16),
        rout=((H, 2, STATE, M), BF16),
        grout=((H, 2, STATE, M), BF16),
        rin=((H, 2, LANES, M), BF16),
        grin=((H, 2, LANES, M), BF16),
        kvout=((H, BLK, LANES), BF16),
        kvin=((H, BLK, LANES), BF16),
        gkvout=((H, BLK, LANES), BF16),
        gkvin=((H, BLK, LANES), BF16),
        kin=((H, BLK, LANES), BF16),
        vin=((H, BLK, LANES), BF16),
        fin=((H, BLK, M), BF16),
        win=((H, BLK, BLK), BF16),
        gfq0=((H, BLK, M), F32),
        gq0=((H, BLK, LANES), F32),
        w=((H, T, T), BF16),
        acc=((H, T, LANES), F32),
        at=((nh, T, E), BF16),
        hid=((T, D), F32),
        n2=((T, D), BF16),
        act=((T, FL), BF16),
        gu=((T, FL), BF16),
        gh=((R, D), F32),
        gb=((nh, R, D), BF16),
        gp=((T, T), BF16),
        gs=((T, 2 * TILE), BF16),
        gfk=((H, T, M), F32),
        gq=((H, T, LANES), F32),
        gk=((H, T, LANES), F32),
        gv=((H, T, LANES), F32),
        gqkv=((T, 3 * E), BF16),
        ns=((8, D), F32),
    )
    pair = dict(out=((3, R, D), BF16), got=((3, R, D), BF16))
    plan.group(ra=pair, rb=pair, rc=pair)
    if inner:

        def weight(width):
            return dict(
                ys=((half, width), BF16),
                yr=((half, width), BF16),
                own=((half, width), F32),
                zs=((nb - 1, piece, width), BF16),
                zr=((nb - 1, piece, width), BF16),
            )

        plan.group(wd=weight(FL), wu=weight(FL), wo_g=weight(E), wx=weight(3 * E))
        plan.add(
            ns2=((8, D), F32),
            ns3=((8, D), F32),
            nz=((nb - 1, 8, D), F32),
            ny=((8, D), F32),
            nh=((3, 8, D), F32),
            otmp=((LANES, 2 * LANES), F32),
        )
    plan.semaphores(ssem=96, rsem=96, lsem=8)

    if inner:
        grads = [(3, piece, E), (E, piece), (piece, FL), (piece, FL)]
        norm = (8, LANES)
    else:
        grads = [(D, 3 * E), (D, E), (D, FL), (D, FL)]
        norm = (8, D)
    outs = [((1, R, D), BF16), ((1, R, D), F32), (norm, F32)] + [(g, F32) for g in grads]
    hbm = pl.BlockSpec(memory_space=pl.ANY)
    vmem = pl.BlockSpec(memory_space=pltpu.VMEM)
    in_specs = [hbm, vmem, vmem, vmem, vmem, vmem, hbm, hbm, vmem, vmem, hbm, hbm, hbm]
    kernel = make_kernel(dims, len(in_specs), len(outs), plan)
    return pl.pallas_call(
        kernel,
        out_shape=[jax.ShapeDtypeStruct(shape, dtype) for shape, dtype in outs],
        in_specs=in_specs,
        out_specs=[vmem] * len(outs),
        scratch_shapes=plan.shapes,
        compiler_params=pltpu.CompilerParams(
            collective_id=0, has_side_effects=True, vmem_limit_bytes=60 << 20
        ),
        name="block",
    )


def per_device(
    mesh_shape,
    tokens,
    seg_ids,
    pattern,
    omega,
    norm1_gain,
    norm1_bias,
    w_qkv,
    w_out,
    norm2_gain,
    norm2_bias,
    w_up,
    w_down,
    out_grad,
):
    nh, ns, nb = mesh_shape
    rows, D = tokens.shape[1:]
    T = seg_ids.shape[1] // ns
    E = w_qkv.shape[2]
    FL = w_up.shape[1]
    piece = D // (ns * nb)
    inner = piece % 16 == 0
    dims = (nh, ns, nb, T, rows, D, E, FL, E // DH, omega.shape[1], inner)
    w_flat = jnp.transpose(w_qkv, (1, 2, 0)).reshape(3 * E, D)
    row = lambda a: a.reshape(1, D)
    mixed, grad_tokens, norms, g_qkv, g_out, g_up, g_down = build(dims)(
        tokens, seg_ids, pattern, omega, row(norm1_gain), row(norm1_bias), w_flat, w_out,
        row(norm2_gain), row(norm2_bias), w_up, w_down, out_grad,
    )
    if inner:
        width = D // (ns * nb * nh)
        norms = norms[:, :width]
        g_qkv = jnp.transpose(g_qkv, (1, 0, 2))
        g_down = g_down.T
    else:
        group = ("seq", "batch")
        scatter = functools.partial(lax.psum_scatter, scatter_dimension=0, tiled=True)
        norms = lax.psum_scatter(
            norms[:4], ("seq", "batch", "head"), scatter_dimension=1, tiled=True
        )
        g_qkv = scatter(g_qkv, group).reshape(piece, 3, E)
        g_out = scatter(g_out, group).T
        g_up = scatter(g_up, group)
        g_down = scatter(g_down, group).T
    return (
        mixed, grad_tokens, norms[0], norms[1], g_qkv, g_out, norms[2], norms[3], g_up, g_down,
    )


def solution(mesh):
    placed = (
        P("batch", ("seq", "head"), None),
        P("batch", None),
        P("head", None),
        P(),
        P(),
        P(),
        P(None, None, "head"),
        P("head", None),
        P(),
        P(),
        P(None, "head"),
        P("head", None),
        P("batch", ("seq", "head"), None),
    )
    shape = (mesh.shape["head"], mesh.shape["seq"], mesh.shape["batch"])
    return jax.shard_map(
        functools.partial(per_device, shape),
        mesh=mesh,
        in_specs=placed,
        out_specs=(
            P("batch", ("seq", "head"), None),
            P("batch", ("seq", "head"), None),
            P(("seq", "batch", "head")),
            P(("seq", "batch", "head")),
            P(("seq", "batch"), None, "head"),
            P("head", ("seq", "batch")),
            P(("seq", "batch", "head")),
            P(("seq", "batch", "head")),
            P(("seq", "batch"), "head"),
            P("head", ("seq", "batch")),
        ),
        check_vma=False,
    )
```

```python
import functools
import math
from types import SimpleNamespace

import jax
import jax.numpy as jnp
from jax import lax
from jax.experimental import pallas as pl
from jax.experimental.pallas import tpu as pltpu
from jax.sharding import PartitionSpec as P

DH = 64
BLK = 64
LANES = 128
TILE = 128
STATE = 80
F32 = jnp.float32
BF16 = jnp.bfloat16
MESH = pl.DeviceIdType.MESH


def nn(a, b):
    return lax.dot_general(a, b, (((1,), (0,)), ((), ())), preferred_element_type=F32)


def nt(a, b):
    return lax.dot_general(a, b, (((1,), (1,)), ((), ())), preferred_element_type=F32)


def tn(a, b):
    return lax.dot_general(a, b, (((0,), (0,)), ((), ())), preferred_element_type=F32)


def normalize(x):
    center = x - jnp.mean(x, axis=-1, keepdims=True)
    rstd = lax.rsqrt(jnp.mean(center * center, axis=-1, keepdims=True) + 1e-05)
    return center * rstd, rstd


def norm_back(grad, gain, xhat, rstd):
    g = grad * gain
    return rstd * (
        g - jnp.mean(g, axis=-1, keepdims=True) - xhat * jnp.mean(g * xhat, axis=-1, keepdims=True)
    )


def gelu_both(u):
    k0 = math.sqrt(2.0 / math.pi)
    u2 = u * u
    th = jnp.tanh(k0 * (u + 0.044715 * u2 * u))
    half = 0.5 * (1.0 + th)
    slope = half + 0.5 * u * (1.0 - th * th) * (k0 * (1.0 + 3.0 * 0.044715 * u2))
    return u * half, slope


class Plan:
    def __init__(self):
        self.shapes = []
        self.tree = {}

    def add(self, into=None, **buffers):
        into = self.tree if into is None else into
        for name, (shape, dtype) in buffers.items():
            into[name] = len(self.shapes)
            self.shapes.append(pltpu.VMEM(shape, dtype))

    def group(self, **groups):
        for name, buffers in groups.items():
            self.tree[name] = {}
            self.add(self.tree[name], **buffers)

    def semaphores(self, **counts):
        for name, n in counts.items():
            self.tree[name] = len(self.shapes)
            self.shapes.append(pltpu.SemaphoreType.DMA((n,)))

    def bind(self, refs):
        def walk(tree):
            return SimpleNamespace(
                **{k: walk(v) if isinstance(v, dict) else refs[v] for k, v in tree.items()}
            )

        return walk(self.tree)


def make_kernel(dims, n_in, n_out, plan):
    nh, ns, nb, T, R, D, E, FL, H, M, inner = dims
    nt_tiles = T // TILE
    half_rows = D // ns
    piece = D // (ns * nb)

    def kernel(*refs):
        (
            tok_hbm, seg_ref, pat_ref, omega_ref, g1_ref, b1_ref, wqkv_hbm, wout_hbm,
            g2_ref, b2_ref, wup_hbm, wdown_hbm, og_hbm,
        ) = refs[:n_in]
        (
            mixed_ref, gtok_ref, norm_ref, oqkv_ref, oout_ref, oup_ref, odown_ref,
        ) = refs[n_in : n_in + n_out]
        s = plan.bind(refs[n_in + n_out :])
        ssem, rsem, lsem = s.ssem, s.rsem, s.lsem
        used = {"r": 0, "l": 0}
        sends = []

        head = lax.axis_index("head")
        seq = lax.axis_index("seq")
        bat = lax.axis_index("batch")
        h1 = head + 1 - 2 * lax.rem(head, 2)
        h2 = lax.rem(head + 2, nh)
        h3 = lax.rem(h1 + 2, nh)
        other = 1 - seq

        def local(src, dst):
            k = used["l"]
            used["l"] += 1
            c = pltpu.make_async_copy(src, dst, lsem.at[k])
            c.start()
            return c

        def send(src, dst, **dev):
            k = used["r"]
            used["r"] += 1
            c = pltpu.make_async_remote_copy(
                src_ref=src, dst_ref=dst, send_sem=ssem.at[k], recv_sem=rsem.at[k],
                device_id=dev, device_id_type=MESH,
            )
            c.start()
            sends.append(c)
            return c

        def rows(slot, n=TILE):
            return pl.ds(pl.multiple_of(slot * n, n), n)

        c_tok = local(tok_hbm.at[0], s.tok.at[head])
        c_wqkv = local(wqkv_hbm, s.wqkv)
        c_wout = local(wout_hbm, s.wo.at[head])
        c_og = local(og_hbm.at[0], s.og.at[head])
        c_wup = local(wup_hbm, s.wup)
        c_wdown = local(wdown_hbm, s.wdown)
        barrier = pltpu.get_barrier_semaphore()
        peers = [dict(head=h1), dict(head=h2), dict(head=h3), dict(seq=other)]
        if inner:
            peers += [dict(batch=lax.rem(bat + d, nb)) for d in range(1, nb)]
        for dev in peers:
            pl.semaphore_signal(barrier, inc=1, device_id=dev, device_id_type=MESH)
        pl.semaphore_wait(barrier, len(peers))

        def gather_start(buf, chunks):
            n = buf.shape[1] // chunks
            out = []
            for i in range(chunks):
                part = buf.at[head, pl.ds(i * n, n)]
                across = send(part, part, head=h2)
                beside = send(part, part, head=h1)
                out.append((across, beside, i * n, n))
            return out

        def gather_forward(buf, started):
            out = []
            for across, _, lo, n in started:
                across.wait_recv()
                part = buf.at[h2, pl.ds(lo, n)]
                out.append(send(part, part, head=h1))
            return out

        c_tok.wait()
        ag_tok = gather_start(s.tok, 2)

        lane = lax.broadcasted_iota(jnp.int32, (1, LANES), 1)
        low = lane < DH
        ones_lanes = ((lane == DH) | (lane == DH + 1)).astype(F32)
        seg_all = seg_ref[...].astype(F32)
        first = seq == 0
        seg_half = jnp.where(first, seg_all[:, :T], seg_all[:, T : 2 * T])
        seg_prev = jnp.where(first, -1.0, seg_all[:, T - BLK : T])
        tail_one = jnp.where(first, -1.0, jnp.broadcast_to(seg_all[:, T - 1 : T], (1, LANES)))
        tail_two = jnp.where(
            first, -1.0, jnp.broadcast_to(seg_all[:, T - BLK - 1 : T - BLK], (1, LANES))
        )
        s.segrow[...] = jnp.broadcast_to(seg_half, (8, T))
        s.segcol[...] = jnp.transpose(jnp.broadcast_to(seg_half, (LANES, T)))
        segcol = s.segcol[...]
        row_id = lax.broadcasted_iota(jnp.int32, (T, LANES), 0)
        mask_two = ((segcol == segcol[T - BLK - 1 : T - BLK, :]) & (row_id < T - BLK)).astype(F32)
        prev_col = jnp.transpose(jnp.broadcast_to(seg_prev, (LANES, BLK)))
        s.mprev[...] = (prev_col == tail_one).astype(F32)
        link = (tail_one == tail_two).astype(F32)
        s.link[...] = jnp.broadcast_to(jnp.concatenate([link] * (M // LANES), axis=1), (8, M))
        s.m0[...] = mask_two
        s.mfar[...] = jnp.where(
            row_id < BLK, (segcol == tail_two).astype(F32), (segcol == tail_one).astype(F32)
        )
        nblk = pat_ref.shape[1]
        per_half = T // BLK
        hot = (
            lax.broadcasted_iota(jnp.int32, (T, nblk), 1)
            == lax.broadcasted_iota(jnp.int32, (T, nblk), 0) // BLK + seq * per_half
        ).astype(F32)
        pat = pat_ref[...].astype(F32)
        for h in range(H):
            s.thr[h] = 3.0 - nn(
                (hot * pat[h : h + 1, :]).astype(BF16), jnp.ones((nblk, LANES), BF16)
            )
        wrow = lax.broadcasted_iota(jnp.int32, (TILE, 2 * TILE), 0)
        wcol = lax.broadcasted_iota(jnp.int32, (TILE, 2 * TILE), 1)
        dist = 2 + wrow // BLK - wcol // BLK
        kind = jnp.where(
            dist >= 2,
            1.0,
            jnp.where(dist == 1, 2.0, jnp.where((dist == 0) & (wcol - TILE <= wrow), 3.0, 0.0)),
        )
        for t in range(nt_tiles):
            col = segcol[t * TILE : (t + 1) * TILE, :]
            for side in range(2):
                tile = t - 1 + side
                if tile < 0:
                    continue
                same = col == s.segrow[0:1, tile * TILE : (tile + 1) * TILE]
                s.code[t, :, side * TILE : (side + 1) * TILE] = jnp.where(
                    same, kind[:, side * TILE : (side + 1) * TILE], 0.0
                )
        scale = DH ** (-0.25)
        om = omega_ref[...] * scale
        om_high = om.astype(BF16)
        s.omst[0:DH, :] = om_high
        s.omst[DH : 2 * DH, :] = (om - om_high.astype(F32)).astype(BF16)
        s.omtmp[...] = jnp.zeros((LANES, M), F32)
        s.omtmp[0:DH, :] = om
        s.omtmp[DH : DH + 8, :] = (
            lax.broadcasted_iota(jnp.int32, (8, M), 0) == 0
        ).astype(F32)
        s.omt[...] = jnp.transpose(s.omtmp[...]).astype(BF16)
        c_wqkv.wait()
        for c in range(3):
            for h in range(H):
                src = s.wqkv[c * E + h * DH : c * E + (h + 1) * DH, :]
                base = (c * H + h) * LANES
                s.wpad[base : base + DH, :] = src
                s.wpad[base + DH : base + 2 * DH, :] = src if c < 2 else jnp.zeros_like(src)
        c_wout.wait()
        for h in range(H):
            s.wopad[h * LANES : h * LANES + DH, :] = s.wo[head, h * DH : (h + 1) * DH, :]
            s.wopad[h * LANES + DH : (h + 1) * LANES, :] = jnp.zeros((DH, D), BF16)
        for h in range(H):
            s.rin[h, STATE:LANES, :] = jnp.zeros((LANES - STATE, M), BF16)
            s.grin[h, STATE:LANES, :] = jnp.zeros((LANES - STATE, M), BF16)

        def features(twice):
            x = twice.astype(F32)
            square = jnp.sum(x * x, axis=-1, keepdims=True)
            projected = nn(twice, s.omst[...])
            return jnp.exp(projected - square * (scale * scale * 0.25)) * (1.0 / math.sqrt(M))

        gain1, bias1 = g1_ref[...].reshape(1, D), b1_ref[...].reshape(1, D)
        gain2, bias2 = g2_ref[...].reshape(1, D), b2_ref[...].reshape(1, D)

        def project(slot):
            xhat, _ = normalize(s.tok[slot].astype(F32))
            normed = (xhat * gain1 + bias1).astype(BF16)
            at = rows(slot)
            s.n1[at, :] = normed
            for c in range(3):
                out = nt(normed, s.wpad[c * H * LANES : (c + 1) * H * LANES, :])
                for h in range(H):
                    part = out[:, h * LANES : (h + 1) * LANES]
                    if c == 2:
                        s.v[h, at, :] = (part + ones_lanes).astype(BF16)
                    else:
                        low_part = part.astype(BF16)
                        (s.q, s.k)[c][h, at, :] = low_part
                        (s.fq, s.fk)[c][h, at, :] = features(low_part).astype(BF16)

        project(head)
        for _, beside, _, _ in ag_tok:
            beside.wait_recv()
        project(h1)
        fw_tok = gather_forward(s.tok, ag_tok)
        ag_wo = gather_start(s.wo, 1)
        project(h2)
        for c in fw_tok:
            c.wait_recv()
        project(h3)

        for h in range(H):
            fk = s.fk[h]
            v = s.v[h].astype(F32)
            v0 = (v * s.m0[...]).astype(BF16)
            s.v0[h] = v0
            s.rout[h] = tn(v0, fk)[:STATE].astype(BF16)
            kk = s.k[h, T - BLK : T, :].astype(F32)
            vv = v[T - BLK : T, :]
            s.kvout[h] = jnp.where(low, kk, pltpu.roll(vv, DH, 1)).astype(BF16)
        ex_kv = send(s.kvout, s.kvin, seq=other)
        ex_r = send(s.rout, s.rin.at[:, pl.ds(0, STATE)], seq=other)
        c_og.wait()
        ag_og = gather_start(s.og, 1)

        def attend(h, carry):
            for t in range(nt_tiles):
                lo, hi = t * TILE, (t + 1) * TILE
                w0 = max(0, lo - TILE)
                fq = s.fq[h, lo:hi, :]
                low_rank = nt(fq, s.fk[h, 0:hi, :])
                exact = jnp.exp(nt(s.q[h, lo:hi, :], s.k[h, w0:hi, :]) * (0.5 / math.sqrt(DH)))
                tiles = (hi - w0) // TILE
                code = s.code[t, :, (2 - tiles) * TILE :]
                thr = jnp.concatenate([s.thr[h, lo:hi, :]] * tiles, axis=1)
                near = jnp.where(
                    code >= thr, exact, jnp.where(code >= 1.0, low_rank[:, w0:], 0.0)
                )
                if w0 > 0:
                    col = jnp.concatenate([s.segcol[lo:hi, :]] * (w0 // TILE), axis=1)
                    far = jnp.where(col == s.segrow[0:1, 0:w0], low_rank[:, :w0], 0.0)
                    near = jnp.concatenate([far, near], axis=1)
                w = near.astype(BF16)
                s.w[h, lo:hi, 0:hi] = w
                s.acc[h, lo:hi, :] = nn(w, s.v[h, 0:hi, :])
            return carry

        lax.fori_loop(0, H, attend, 0)
        fw_wo = gather_forward(s.wo, ag_wo)

        if inner:
            for j in range(nh):
                lo = j * TILE
                s.n1t[:, lo : lo + TILE] = jnp.transpose(s.n1[lo : lo + TILE, :])

        ex_kv.wait_recv()
        ex_r.wait_recv()

        def unpack(packed):
            x = packed.astype(F32)
            turned = pltpu.roll(x, DH, 1)
            twice = jnp.where(low, x, turned).astype(BF16)
            return twice, jnp.where(low, turned, 0.0)

        same_in = s.segcol[0:BLK, 0:BLK] == seg_prev
        for h in range(H):
            k_in, v_in = unpack(s.kvin[h])
            v_in = (v_in + ones_lanes).astype(BF16)
            f_in = features(k_in).astype(BF16)
            s.kin[h] = k_in
            s.vin[h] = v_in
            s.fin[h] = f_in
            q0 = s.q[h, 0:BLK, :]
            fq0 = s.fq[h, 0:BLK, :]
            exact = jnp.exp(nt(q0, k_in) * (0.5 / math.sqrt(DH)))
            low_rank = nt(fq0, f_in)
            use_exact = s.thr[h, 0:BLK, 0:BLK] < 2.5
            w_in = jnp.where(same_in, jnp.where(use_exact, exact, low_rank), 0.0).astype(BF16)
            s.win[h] = w_in
            state = s.rin[h]
            later = state.astype(F32) * s.link[0:1, :] + tn(
                (v_in.astype(F32) * s.mprev[...]).astype(BF16), f_in
            )
            s.rlater[h] = later.astype(BF16)
            far0 = jnp.where(s.mfar[0:BLK, :] > 0.5, nt(fq0, state), 0.0)
            s.acc[h, 0:BLK, :] = s.acc[h, 0:BLK, :] + nn(w_in, v_in) + far0
            far1 = jnp.where(
                s.mfar[BLK:T, :] > 0.5, nt(s.fq[h, BLK:T, :], s.rlater[h]), 0.0
            )
            s.acc[h, BLK:T, :] = s.acc[h, BLK:T, :] + far1

        def divided(h, lo, hi):
            acc = s.acc[h, lo:hi, :]
            inv = 1.0 / acc[:, DH : DH + 1]
            return acc * inv, inv

        ag_at = []
        fw_at = []
        for t in range(nt_tiles):
            lo, hi = t * TILE, (t + 1) * TILE
            outs = [divided(h, lo, hi)[0] for h in range(H)]
            for h in range(0, H, 2):
                if h + 1 < H:
                    both = jnp.where(low, outs[h], pltpu.roll(outs[h + 1], DH, 1))
                    s.at[head, lo:hi, h * DH : (h + 2) * DH] = both.astype(BF16)
                else:
                    s.at[head, lo:hi, h * DH : (h + 1) * DH] = outs[h][:, :DH].astype(BF16)
            part = s.at.at[head, pl.ds(lo, TILE)]
            ag_at.append((send(part, part, head=h2), send(part, part, head=h1), lo, TILE))
        for c in fw_wo:
            c.wait_recv()
        for _, c, _, _ in ag_wo:
            c.wait_recv()
        fw_at = gather_forward(s.at, ag_at)
        fw_og = gather_forward(s.og, ag_og)
        for _, c, _, _ in ag_og:
            c.wait_recv()
        for c in fw_og:
            c.wait_recv()
        for _, c, _, _ in ag_at:
            c.wait_recv()
        for c in fw_at:
            c.wait_recv()
        c_wup.wait()
        c_wdown.wait()
        if inner:
            for j in range(nh):
                lo = j * TILE
                s.ogt[:, lo : lo + TILE] = jnp.transpose(s.og[j])

        def scatter_beside(make, bufs):
            bufs.out[0] = make(h3).astype(BF16)
            a = send(bufs.out.at[0], bufs.got.at[0], head=h1)
            bufs.mine[...] = make(h2)
            return a

        def scatter_across(bufs, a):
            a.wait_recv()
            bufs.out[1] = (bufs.mine[...] + bufs.got[0].astype(F32)).astype(BF16)
            return send(bufs.out.at[1], bufs.got.at[1], head=h2)

        def scatter_last(make, bufs):
            bufs.out[2] = make(h1).astype(BF16)
            return send(bufs.out.at[2], bufs.got.at[2], head=h1)

        def scatter_done(bufs, b, c):
            c.wait_recv()
            part = bufs.got[2].astype(F32)
            b.wait_recv()
            return part + bufs.got[1].astype(F32)

        def feed(slot):
            at = rows(slot)
            hid = s.tok[slot].astype(F32)
            for j in range(nh):
                hid = hid + nn(s.at[j, at, :], s.wo[j])
            s.hid[at, :] = hid
            xhat, _ = normalize(hid)
            normed = (xhat * gain2 + bias2).astype(BF16)
            s.n2[at, :] = normed
            act, slope = gelu_both(nn(normed, s.wup[...]))
            s.act[at, :] = act.astype(BF16)
            gu = (nt(s.og[slot], s.wdown[...]) * slope).astype(BF16)
            s.gu[at, :] = gu
            return nt(gu, s.wup[...])

        ra_a = scatter_beside(feed, s.ra)
        ra_b = scatter_across(s.ra, ra_a)
        ra_c = scatter_last(feed, s.ra)
        own = feed(head)

        b1 = bat + 1 - 2 * lax.rem(bat, 2)
        b2 = lax.rem(bat + 2, nb)
        b3 = lax.rem(b1 + 2, nb)
        there = pl.ds(pl.multiple_of(other * half_rows, LANES), half_rows)
        here = pl.ds(pl.multiple_of(seq * half_rows, LANES), half_rows)

        def y_send(g):
            g.y = send(g.ys, g.yr, seq=other)

        def y_other(g, left, right):
            g.ys[...] = nn(left[there, :], right).astype(BF16)

        def y_own(g, left, right):
            g.own[...] = nn(left[here, :], right)

        def with_y(g, index):
            at = rows(index, piece)
            return g.own[at, :] + g.yr[at, :].astype(F32)

        def za_send(g):
            g.y.wait_recv()
            for i, index in enumerate((b1, b3)):
                g.zas[i] = with_y(g, index).astype(BF16)
            g.za = send(g.zas, g.zar, batch=b1)

        def zb_send(g):
            g.za.wait_recv()
            g.zbs[...] = (with_y(g, b2) + g.zar[1].astype(F32)).astype(BF16)
            g.zb = send(g.zbs, g.zbr, batch=b2)

        def weight_sum(g):
            total = with_y(g, bat) + g.zar[0].astype(F32)
            g.zb.wait_recv()
            return total + g.zbr[...].astype(F32)

        def zd_send(g):
            g.y.wait_recv()
            g.zd = []
            for i, index in enumerate((b2, b1, b3)):
                g.zds[i] = with_y(g, index).astype(BF16)
                g.zd.append(send(g.zds.at[i], g.zdr.at[i], batch=index))

        def weight_sum_direct(g):
            total = with_y(g, bat)
            for i in (1, 2, 0):
                g.zd[i].wait_recv()
                total = total + g.zdr[i].astype(F32)
            return total

        def both(index):
            return [rows(half * nb + index, piece) for half in range(ns)]

        def first_za(g, left, right):
            g.own[...] = nn(left[...], right)
            for i, index in enumerate((b1, b3)):
                for half, at in enumerate(both(index)):
                    g.zas[i, half] = g.own[at, :].astype(BF16)
            g.za = send(g.zas, g.zar, batch=b1)

        def first_zb(g):
            g.za.wait_recv()
            for half, at in enumerate(both(b2)):
                g.zbs[half] = (g.own[at, :] + g.zar[1, half].astype(F32)).astype(BF16)
            g.zb = send(g.zbs, g.zbr, batch=b2)

        def first_part(g, half):
            at = rows(half * nb + bat, piece)
            return g.own[at, :] + g.zar[0, half].astype(F32) + g.zbr[half].astype(F32)

        def first_y(g):
            g.zb.wait_recv()
            g.ys[...] = first_part(g, other).astype(BF16)
            g.y = send(g.ys, g.yr, seq=other)

        def first_sum(g):
            total = first_part(g, seq)
            g.y.wait_recv()
            return total + g.yr[...].astype(F32)

        def columns(ref, i, groups):
            width = ref.shape[-1] // groups
            return ref[:, i * width : (i + 1) * width]

        if inner:
            ups, qkvs = [s.u0, s.u1], [s.x0, s.x1, s.x2]
            y_other(s.d1, s.ogt, columns(s.act, 1, 2))
            y_send(s.d1)
            first_za(s.d0, s.ogt, columns(s.act, 0, 2))
            y_own(s.d1, s.ogt, columns(s.act, 1, 2))

        grad2 = own + scatter_done(s.ra, ra_b, ra_c)
        mine = rows(head)
        xhat2, rstd2 = normalize(s.hid[mine, :])
        s.ns[...] = jnp.zeros_like(s.ns)
        s.ns[2:3, :] = jnp.sum(grad2 * xhat2, axis=0, keepdims=True)
        s.ns[3:4, :] = jnp.sum(grad2, axis=0, keepdims=True)
        grad_hidden = s.og[head].astype(F32) + norm_back(grad2, gain2, xhat2, rstd2)
        s.gh[...] = grad_hidden
        s.gb[head] = grad_hidden.astype(BF16)
        ag_gb = gather_start(s.gb, 2)
        if inner:
            for j in range(nh):
                lo = j * TILE
                s.n2t[:, lo : lo + TILE] = jnp.transpose(s.n2[lo : lo + TILE, :])
            y_other(s.u0, s.n2t, columns(s.gu, 0, 2))
            y_send(s.u0)
            y_other(s.u1, s.n2t, columns(s.gu, 1, 2))

        def lower(slot):
            return nn(s.act[rows(slot), :], s.wdown[...])

        rc_a = scatter_beside(lower, s.rc)
        rc_c = scatter_last(lower, s.rc)

        def divide_back(slot):
            at = rows(slot)
            ga = nt(s.gb[slot], s.wopad[...])
            for h in range(H):
                acc = s.acc[h, at, :]
                inv = 1.0 / acc[:, DH : DH + 1]
                gnum = ga[:, h * LANES : (h + 1) * LANES] * inv
                gden = -jnp.sum(gnum * acc, axis=-1, keepdims=True) * inv
                high = gden.astype(BF16).astype(F32)
                gnum = jnp.where(lane == DH, high, jnp.where(lane == DH + 1, gden - high, gnum))
                s.gn[h, at, :] = gnum.astype(BF16)

        divide_back(head)
        for _, c, _, _ in ag_gb:
            c.wait_recv()
        divide_back(h1)
        if inner:
            first_zb(s.d0)
            za_send(s.d1)
        fw_gb = gather_forward(s.gb, ag_gb)
        divide_back(h2)
        for c in fw_gb:
            c.wait_recv()
        divide_back(h3)

        def feature_back(gfeat, feat, twice):
            x = nn((gfeat * feat.astype(F32)).astype(BF16), s.omt[...])
            return x - twice.astype(F32) * (x[:, DH : DH + 1] * (scale * scale))

        for h in range(H):
            gm = jnp.where(s.mfar[...] > 0.5, s.gn[h].astype(F32), 0.0).astype(BF16)
            s.gm[h] = gm
            glater = tn(gm[BLK:T, :], s.fq[h, BLK:T, :])
            gstate = tn(gm[0:BLK, :], s.fq[h, 0:BLK, :]) + glater * s.link[0:1, :]
            s.grout[h] = gstate[:STATE].astype(BF16)
            glater = glater.astype(BF16)
            v_last = (s.vin[h].astype(F32) * s.mprev[...]).astype(BF16)
            gn0 = s.gn[h, 0:BLK, :]
            q0 = s.q[h, 0:BLK, :]
            fq0 = s.fq[h, 0:BLK, :]
            gw = nt(gn0, s.vin[h])
            w_in = s.win[h]
            use_exact = s.thr[h, 0:BLK, 0:BLK] < 2.5
            gs = jnp.where(
                same_in & use_exact, gw * w_in.astype(F32) * (1.0 / math.sqrt(DH)), 0.0
            ).astype(BF16)
            gp = jnp.where(same_in & jnp.logical_not(use_exact), gw, 0.0).astype(BF16)
            gfeat = tn(gp, fq0) + nn(v_last, glater)
            gk = feature_back(gfeat, s.fin[h], s.kin[h]) + tn(gs, q0)
            gv = tn(w_in, gn0) + s.mprev[...] * nt(s.fin[h], glater)
            s.gkvout[h] = jnp.where(low, gk, pltpu.roll(gv, DH, 1)).astype(BF16)
            s.gfq0[h] = nn(gp, s.fin[h])
            s.gq0[h] = nn(gs, s.kin[h])
        ex_gkv = send(s.gkvout, s.gkvin, seq=other)
        ex_gr = send(s.grout, s.grin.at[:, pl.ds(0, STATE)], seq=other)

        rc_b = scatter_across(s.rc, rc_a)
        if inner:
            y_send(s.u1)
            for i, g in enumerate(ups):
                y_own(g, s.n2t, columns(s.gu, i, 2))

        def attend_back(h):
            for t in range(nt_tiles):
                lo, hi = t * TILE, (t + 1) * TILE
                w0 = max(0, lo - TILE)
                tiles = (hi - w0) // TILE
                gw = nt(s.gn[h, lo:hi, :], s.v[h, 0:hi, :])
                code = s.code[t, :, (2 - tiles) * TILE :]
                thr = jnp.concatenate([s.thr[h, lo:hi, :]] * tiles, axis=1)
                use_exact = code >= thr
                near = gw[:, w0:]
                gs = jnp.where(
                    use_exact,
                    near * s.w[h, lo:hi, w0:hi].astype(F32) * (1.0 / math.sqrt(DH)),
                    0.0,
                ).astype(BF16)
                gp = jnp.where((code >= 1.0) & (code < thr), near, 0.0)
                if w0 > 0:
                    col = jnp.concatenate([s.segcol[lo:hi, :]] * (w0 // TILE), axis=1)
                    far = jnp.where(col == s.segrow[0:1, 0:w0], gw[:, :w0], 0.0)
                    gp = jnp.concatenate([far, gp], axis=1)
                gp = gp.astype(BF16)
                s.gp[lo:hi, 0:hi] = gp
                s.gs[lo:hi, (2 - tiles) * TILE :] = gs
                gfq = nn(gp, s.fk[h, 0:hi, :])
                gq = nn(gs, s.k[h, w0:hi, :])
                gm = s.gm[h, lo:hi, :]
                if t == 0:
                    top = nn(gm[0:BLK], s.rin[h]) + s.gfq0[h]
                    bottom = nn(gm[BLK:], s.rlater[h])
                    gfq = gfq + jnp.concatenate([top, bottom], axis=0)
                    gq = gq + jnp.concatenate(
                        [s.gq0[h], jnp.zeros((TILE - BLK, LANES), F32)], axis=0
                    )
                else:
                    gfq = gfq + nn(gm, s.rlater[h])
                gq = gq + feature_back(gfq, s.fq[h, lo:hi, :], s.q[h, lo:hi, :])
                s.gq[h, lo:hi, :] = gq
            for t in range(nt_tiles):
                lo, hi = t * TILE, (t + 1) * TILE
                s.gfk[h, lo:hi, :] = tn(s.gp[lo:T, lo:hi], s.fq[h, lo:T, :])
                s.gv[h, lo:hi, :] = tn(s.w[h, lo:T, lo:hi], s.gn[h, lo:T, :])
                gk = tn(s.gs[lo:hi, TILE:], s.q[h, lo:hi, :])
                if t + 1 < nt_tiles:
                    gk = gk + tn(s.gs[hi : hi + TILE, :TILE], s.q[h, hi : hi + TILE, :])
                s.gk[h, lo:hi, :] = gk

        for h in range(H):
            attend_back(h)
            if inner and h == 1:
                za_send(s.u0)
        if inner:
            zb_send(s.d1)
            first_y(s.d0)
            for j in range(nh):
                lo = j * TILE
                s.gbt[:, lo : lo + TILE] = jnp.transpose(s.gb[j])
            y_other(s.o0, s.gbt, s.at[head])
            y_send(s.o0)

        ex_gkv.wait_recv()
        ex_gr.wait_recv()

        def finish(h, carry):
            state = jnp.where(first, s.grin[h].astype(F32), 0.0).astype(BF16)
            gfk = s.gfk[h] + nn(s.v0[h], state)
            fk = s.fk[h]
            gv = s.gv[h] + s.m0[...] * nt(fk, state)
            gk = s.gk[h] + feature_back(gfk, fk, s.k[h])
            s.gk[h] = gk
            s.gv[h] = gv
            back = jnp.where(first, s.gkvin[h].astype(F32), 0.0)
            s.gk[h, T - BLK : T, :] = s.gk[h, T - BLK : T, :] + back
            s.gv[h, T - BLK : T, :] = s.gv[h, T - BLK : T, :] + pltpu.roll(back, DH, 1)
            return carry

        lax.fori_loop(0, H, finish, 0)
        parts = [(n, h) for n in (s.gq, s.gk, s.gv) for h in range(H)]
        for i in range(0, len(parts), 2):
            (na, ha) = parts[i]
            a = na[ha]
            if i + 1 < len(parts):
                (nb_, hb) = parts[i + 1]
                a = jnp.where(low, a, pltpu.roll(nb_[hb], DH, 1))
                s.gqkv[:, i * DH : (i + 2) * DH] = a.astype(BF16)
            else:
                s.gqkv[:, i * DH : (i + 1) * DH] = a[:, :DH].astype(BF16)

        if inner:
            for i, g in enumerate(qkvs):
                y_other(g, s.n1t, columns(s.gqkv, i, 3))
                y_send(g)

        def first_grad(slot):
            return nn(s.gqkv[rows(slot), :], s.wqkv[...])

        rb_a = scatter_beside(first_grad, s.rb)
        rb_b = scatter_across(s.rb, rb_a)
        if inner:
            zb_send(s.u0)
        rb_c = scatter_last(first_grad, s.rb)
        own = first_grad(head)
        if inner:
            za_send(s.u1)
            y_own(s.o0, s.gbt, s.at[head])
            for i, g in enumerate(qkvs):
                y_own(g, s.n1t, columns(s.gqkv, i, 3))
            zd_send(s.o0)
        own_mixed = s.hid[mine, :] + lower(head)

        grad1 = own + scatter_done(s.rb, rb_b, rb_c)
        xhat1, rstd1 = normalize(s.tok[head].astype(F32))
        s.ns[0:1, :] = jnp.sum(grad1 * xhat1, axis=0, keepdims=True)
        s.ns[1:2, :] = jnp.sum(grad1, axis=0, keepdims=True)
        gtok_ref[0] = s.gh[...] + norm_back(grad1, gain1, xhat1, rstd1)

        if inner:
            n_h = [send(s.ns, s.nh.at[i], head=d) for i, d in enumerate((h1, h2, h3))]
            zd_send(s.x0)
            zb_send(s.u1)
            total = s.ns[...]
            for i, c in enumerate(n_h):
                c.wait_recv()
                total = total + s.nh[i]
            s.ns2[...] = total
            n_y = send(s.ns2, s.ny, seq=other)
            zd_send(s.x1)
        mixed_ref[0] = (own_mixed + scatter_done(s.rc, rc_b, rc_c)).astype(BF16)
        if inner:
            n_y.wait_recv()
            s.ns3[...] = s.ns2[...] + s.ny[...]
            n_z = [
                send(s.ns3, s.nz.at[d - 1], batch=lax.rem(bat + d, nb)) for d in range(1, nb)
            ]
            zd_send(s.x2)
            wide = FL // 2
            odown_ref[:, :wide] = first_sum(s.d0)
            odown_ref[:, wide:] = weight_sum(s.d1)
            oup_ref[:, :wide] = weight_sum(s.u0)
            oup_ref[:, wide:] = weight_sum(s.u1)
            s.otmp[...] = jnp.zeros_like(s.otmp)
            s.otmp[0:piece, 0:E] = weight_sum_direct(s.o0)
            oout_ref[...] = jnp.transpose(s.otmp[...])[:E, :piece]
            total = s.ns3[...]
            for i, c in enumerate(n_z):
                c.wait_recv()
                total = total + s.nz[i]
            width = D // (ns * nb * nh)
            start = ((seq * nb + bat) * nh + head) * width
            pick = (
                lax.broadcasted_iota(jnp.int32, (D, LANES), 0)
                == lax.broadcasted_iota(jnp.int32, (D, LANES), 1) + start
            ).astype(F32)
            norm_ref[...] = lax.dot_general(
                total, pick, (((1,), (0,)), ((), ())),
                precision=lax.Precision.HIGHEST, preferred_element_type=F32,
            )
            for i, g in enumerate(qkvs):
                oqkv_ref[i] = weight_sum_direct(g)
        else:

            def joined(ref):
                return jnp.concatenate([ref[j] for j in range(nh)], axis=0)

            norm_ref[...] = s.ns[...]
            odown_ref[...] = tn(joined(s.og), s.act[...])
            oup_ref[...] = tn(s.n2[...], s.gu[...])
            oout_ref[...] = tn(joined(s.gb), s.at[head])
            oqkv_ref[...] = tn(s.n1[...], s.gqkv[...])
        for c in sends:
            c.wait_send()

    return kernel


def build(dims):
    nh, ns, nb, T, R, D, E, FL, H, M, inner = dims
    plan = Plan()
    piece = D // (ns * nb)
    half = D // ns
    plan.add(
        tok=((nh, R, D), BF16),
        og=((nh, R, D), BF16),
        wqkv=((3 * E, D), BF16),
        wo=((nh, E, D), BF16),
        wup=((D, FL), BF16),
        wdown=((FL, D), BF16),
        wpad=((3 * H * LANES, D), BF16),
        wopad=((H * LANES, D), BF16),
        segrow=((8, T), F32),
        segcol=((T, LANES), F32),
        m0=((T, LANES), F32),
        mprev=((BLK, LANES), F32),
        link=((8, M), F32),
        mfar=((T, LANES), F32),
        thr=((H, T, LANES), F32),
        code=((T // TILE, TILE, 2 * TILE), F32),
        omst=((2 * DH, M), BF16),
        omtmp=((LANES, M), F32),
        omt=((M, LANES), BF16),
        n1=((T, D), BF16),
        q=((H, T, LANES), BF16),
        k=((H, T, LANES), BF16),
        v=((H, T, LANES), BF16),
        v0=((H, T, LANES), BF16),
        gn=((H, T, LANES), BF16),
        gm=((H, T, LANES), BF16),
        fq=((H, T, M), BF16),
        fk=((H, T, M), BF16),
        rout=((H, STATE, M), BF16),
        grout=((H, STATE, M), BF16),
        rin=((H, LANES, M), BF16),
        grin=((H, LANES, M), BF16),
        rlater=((H, LANES, M), BF16),
        kvout=((H, BLK, LANES), BF16),
        kvin=((H, BLK, LANES), BF16),
        gkvout=((H, BLK, LANES), BF16),
        gkvin=((H, BLK, LANES), BF16),
        kin=((H, BLK, LANES), BF16),
        vin=((H, BLK, LANES), BF16),
        fin=((H, BLK, M), BF16),
        win=((H, BLK, BLK), BF16),
        gfq0=((H, BLK, M), F32),
        gq0=((H, BLK, LANES), F32),
        w=((H, T, T), BF16),
        acc=((H, T, LANES), F32),
        at=((nh, T, E), BF16),
        hid=((T, D), F32),
        n2=((T, D), BF16),
        act=((T, FL), BF16),
        gu=((T, FL), BF16),
        gh=((R, D), F32),
        gb=((nh, R, D), BF16),
        gp=((T, T), BF16),
        gs=((T, 2 * TILE), BF16),
        gfk=((H, T, M), F32),
        gq=((H, T, LANES), F32),
        gk=((H, T, LANES), F32),
        gv=((H, T, LANES), F32),
        gqkv=((T, 3 * E), BF16),
        ns=((8, D), F32),
    )
    pair = dict(out=((3, R, D), BF16), got=((3, R, D), BF16), mine=((R, D), F32))
    plan.group(ra=pair, rb=pair, rc=pair)
    if inner:

        def weight(width):
            return dict(
                ys=((half, width), BF16),
                yr=((half, width), BF16),
                own=((half, width), F32),
                zas=((2, piece, width), BF16),
                zar=((2, piece, width), BF16),
                zbs=((piece, width), BF16),
                zbr=((piece, width), BF16),
            )

        def weight_direct(width):
            return dict(
                ys=((half, width), BF16),
                yr=((half, width), BF16),
                own=((half, width), F32),
                zds=((nb - 1, piece, width), BF16),
                zdr=((nb - 1, piece, width), BF16),
            )

        def weight_first(width):
            return dict(
                own=((D, width), F32),
                zas=((2, ns, piece, width), BF16),
                zar=((2, ns, piece, width), BF16),
                zbs=((ns, piece, width), BF16),
                zbr=((ns, piece, width), BF16),
                ys=((piece, width), BF16),
                yr=((piece, width), BF16),
            )

        wide = weight(FL // 2)
        plan.group(d0=weight_first(FL // 2), d1=wide, u0=wide, u1=wide)
        narrow = weight_direct(E)
        plan.group(o0=narrow, x0=narrow, x1=narrow, x2=narrow)
        turned = ((D, T), BF16)
        plan.add(n1t=turned, n2t=turned, ogt=turned, gbt=turned)
        plan.add(
            ns2=((8, D), F32),
            ns3=((8, D), F32),
            nz=((nb - 1, 8, D), F32),
            ny=((8, D), F32),
            nh=((3, 8, D), F32),
            otmp=((LANES, 2 * LANES), F32),
        )
    plan.semaphores(ssem=96, rsem=96, lsem=8)

    if inner:
        grads = [(3, piece, E), (E, piece), (piece, FL), (piece, FL)]
        norm = (8, LANES)
    else:
        grads = [(D, 3 * E), (D, E), (D, FL), (D, FL)]
        norm = (8, D)
    outs = [((1, R, D), BF16), ((1, R, D), F32), (norm, F32)] + [(g, F32) for g in grads]
    hbm = pl.BlockSpec(memory_space=pltpu.HBM)
    vmem = pl.BlockSpec(memory_space=pltpu.VMEM)
    in_specs = [hbm, vmem, vmem, vmem, vmem, vmem, hbm, hbm, vmem, vmem, hbm, hbm, hbm]
    kernel = make_kernel(dims, len(in_specs), len(outs), plan)
    return pl.pallas_call(
        kernel,
        out_shape=[jax.ShapeDtypeStruct(shape, dtype) for shape, dtype in outs],
        in_specs=in_specs,
        out_specs=[vmem] * len(outs),
        scratch_shapes=plan.shapes,
        compiler_params=pltpu.CompilerParams(
            collective_id=0, has_side_effects=True, vmem_limit_bytes=60 << 20
        ),
        name="block",
    )


def hand_over(width, *arrays):
    count = len(arrays) - 1

    def kernel(*refs):
        ins, norm_ref = refs[:count], refs[count]
        outs, norm_outs = refs[count + 1 : 2 * count + 1], refs[2 * count + 1 :]
        for a, b in zip(ins, outs):
            b[...] = a[...]
        for i, out in enumerate(norm_outs):
            out[...] = norm_ref[i, :width]

    vmem = pl.BlockSpec(memory_space=pltpu.VMEM)
    return pl.pallas_call(
        kernel,
        out_shape=[jax.ShapeDtypeStruct(a.shape, a.dtype) for a in arrays[:-1]]
        + [jax.ShapeDtypeStruct((width,), F32)] * 4,
        in_specs=[vmem] * len(arrays),
        out_specs=[vmem] * (count + 4),
        name="hand_over",
    )(*arrays)


def per_device(
    mesh_shape,
    tokens,
    seg_ids,
    pattern,
    omega,
    norm1_gain,
    norm1_bias,
    w_qkv,
    w_out,
    norm2_gain,
    norm2_bias,
    w_up,
    w_down,
    out_grad,
):
    nh, ns, nb = mesh_shape
    rows, D = tokens.shape[1:]
    T = seg_ids.shape[1] // ns
    E = w_qkv.shape[2]
    FL = w_up.shape[1]
    piece = D // (ns * nb)
    inner = piece % 16 == 0 and nb == 4
    dims = (nh, ns, nb, T, rows, D, E, FL, E // DH, omega.shape[1], inner)
    w_flat = jnp.transpose(w_qkv, (1, 2, 0)).reshape(3 * E, D)
    mixed, grad_tokens, norms, g_qkv, g_out, g_up, g_down = build(dims)(
        tokens, seg_ids, pattern, omega, norm1_gain, norm1_bias, w_flat, w_out,
        norm2_gain, norm2_bias, w_up, w_down, out_grad,
    )
    if inner:
        width = D // (ns * nb * nh)
        mixed, grad_tokens, g_qkv, g_out, g_up, g_down, *norms = hand_over(
            width, mixed, grad_tokens, g_qkv, g_out, g_up, g_down, norms
        )
        g_qkv = jnp.transpose(g_qkv, (1, 0, 2))
        g_down = g_down.T
    else:
        group = ("seq", "batch")
        scatter = functools.partial(lax.psum_scatter, scatter_dimension=0, tiled=True)
        norms = lax.psum_scatter(
            norms[:4], ("seq", "batch", "head"), scatter_dimension=1, tiled=True
        )
        g_qkv = scatter(g_qkv, group).reshape(piece, 3, E)
        g_out = scatter(g_out, group).T
        g_up = scatter(g_up, group)
        g_down = scatter(g_down, group).T
    return (
        mixed, grad_tokens, norms[0], norms[1], g_qkv, g_out, norms[2], norms[3], g_up, g_down,
    )


def solution(mesh):
    placed = (
        P("batch", ("seq", "head"), None),
        P("batch", None),
        P("head", None),
        P(),
        P(),
        P(),
        P(None, None, "head"),
        P("head", None),
        P(),
        P(),
        P(None, "head"),
        P("head", None),
        P("batch", ("seq", "head"), None),
    )
    shape = (mesh.shape["head"], mesh.shape["seq"], mesh.shape["batch"])
    return jax.shard_map(
        functools.partial(per_device, shape),
        mesh=mesh,
        in_specs=placed,
        out_specs=(
            P("batch", ("seq", "head"), None),
            P("batch", ("seq", "head"), None),
            P(("seq", "batch", "head")),
            P(("seq", "batch", "head")),
            P(("seq", "batch"), None, "head"),
            P("head", ("seq", "batch")),
            P(("seq", "batch", "head")),
            P(("seq", "batch", "head")),
            P(("seq", "batch"), "head"),
            P("head", ("seq", "batch")),
        ),
        check_vma=False,
    )
```

```python
import functools
import math
from types import SimpleNamespace

import jax
import jax.numpy as jnp
from jax import lax
from jax.experimental import pallas as pl
from jax.experimental.pallas import tpu as pltpu
from jax.sharding import PartitionSpec as P

DH = 64
BLK = 64
LANES = 128
TILE = 128
STATE = 80
F32 = jnp.float32
BF16 = jnp.bfloat16
MESH = pl.DeviceIdType.MESH


def nn(a, b):
    return lax.dot_general(a, b, (((1,), (0,)), ((), ())), preferred_element_type=F32)


def nt(a, b):
    return lax.dot_general(a, b, (((1,), (1,)), ((), ())), preferred_element_type=F32)


def tn(a, b):
    return lax.dot_general(a, b, (((0,), (0,)), ((), ())), preferred_element_type=F32)


def normalize(x):
    center = x - jnp.mean(x, axis=-1, keepdims=True)
    rstd = lax.rsqrt(jnp.mean(center * center, axis=-1, keepdims=True) + 1e-05)
    return center * rstd, rstd


def norm_back(grad, gain, xhat, rstd):
    g = grad * gain
    return rstd * (
        g - jnp.mean(g, axis=-1, keepdims=True) - xhat * jnp.mean(g * xhat, axis=-1, keepdims=True)
    )


def gelu_both(u):
    k0 = math.sqrt(2.0 / math.pi)
    u2 = u * u
    th = jnp.tanh(k0 * (u + 0.044715 * u2 * u))
    half = 0.5 * (1.0 + th)
    slope = half + 0.5 * u * (1.0 - th * th) * (k0 * (1.0 + 3.0 * 0.044715 * u2))
    return u * half, slope


class Plan:
    def __init__(self):
        self.shapes = []
        self.tree = {}

    def add(self, into=None, **buffers):
        into = self.tree if into is None else into
        for name, (shape, dtype) in buffers.items():
            into[name] = len(self.shapes)
            self.shapes.append(pltpu.VMEM(shape, dtype))

    def group(self, **groups):
        for name, buffers in groups.items():
            self.tree[name] = {}
            self.add(self.tree[name], **buffers)

    def semaphores(self, **counts):
        for name, n in counts.items():
            self.tree[name] = len(self.shapes)
            self.shapes.append(pltpu.SemaphoreType.DMA((n,)))

    def bind(self, refs):
        def walk(tree):
            return SimpleNamespace(
                **{k: walk(v) if isinstance(v, dict) else refs[v] for k, v in tree.items()}
            )

        return walk(self.tree)


def make_kernel(dims, n_in, n_out, plan):
    nh, ns, nb, T, R, D, E, FL, H, M, inner = dims
    nt_tiles = T // TILE
    half_rows = D // ns
    piece = D // (ns * nb)

    def kernel(*refs):
        (
            tok_hbm, seg_ref, pat_ref, omega_ref, g1_ref, b1_ref, wqkv_hbm, wout_hbm,
            g2_ref, b2_ref, wup_hbm, wdown_hbm, og_hbm,
        ) = refs[:n_in]
        (
            mixed_ref, gtok_ref, norm_ref, oqkv_ref, oout_ref, oup_ref, odown_ref,
        ) = refs[n_in : n_in + n_out]
        s = plan.bind(refs[n_in + n_out :])
        ssem, rsem, lsem = s.ssem, s.rsem, s.lsem
        used = {"r": 0, "l": 0}
        sends = []

        head = lax.axis_index("head")
        seq = lax.axis_index("seq")
        bat = lax.axis_index("batch")
        h1 = head + 1 - 2 * lax.rem(head, 2)
        h2 = lax.rem(head + 2, nh)
        h3 = lax.rem(h1 + 2, nh)
        other = 1 - seq

        def local(src, dst):
            k = used["l"]
            used["l"] += 1
            c = pltpu.make_async_copy(src, dst, lsem.at[k])
            c.start()
            return c

        def send(src, dst, **dev):
            k = used["r"]
            used["r"] += 1
            c = pltpu.make_async_remote_copy(
                src_ref=src, dst_ref=dst, send_sem=ssem.at[k], recv_sem=rsem.at[k],
                device_id=dev, device_id_type=MESH,
            )
            c.start()
            sends.append(c)
            return c

        def prepare(src, dst, **dev):
            k = used["r"]
            used["r"] += 1
            return pltpu.make_async_remote_copy(
                src_ref=src, dst_ref=dst, send_sem=ssem.at[k], recv_sem=rsem.at[k],
                device_id=dev, device_id_type=MESH,
            )

        def rows(slot, n=TILE):
            return pl.ds(pl.multiple_of(slot * n, n), n)

        c_tok = local(tok_hbm.at[0], s.tok.at[head])
        c_wqkv = local(wqkv_hbm, s.wqkv)
        c_wout = local(wout_hbm, s.wo.at[head])
        c_og = local(og_hbm.at[0], s.og.at[head])
        c_wup = local(wup_hbm, s.wup)
        c_wdown = local(wdown_hbm, s.wdown)
        barrier = pltpu.get_barrier_semaphore()
        peers = [dict(head=h1), dict(head=h2), dict(head=h3), dict(seq=other)]
        if inner:
            peers += [dict(batch=lax.rem(bat + d, nb)) for d in range(1, nb)]
        for dev in peers:
            pl.semaphore_signal(barrier, inc=1, device_id=dev, device_id_type=MESH)
        pl.semaphore_wait(barrier, len(peers))

        def gather_start(buf, chunks):
            n = buf.shape[1] // chunks
            out = []
            for i in range(chunks):
                part = buf.at[head, pl.ds(i * n, n)]
                across = send(part, part, head=h2)
                beside = send(part, part, head=h1)
                out.append((across, beside, i * n, n))
            return out

        def gather_forward(buf, started):
            out = []
            for across, _, lo, n in started:
                across.wait_recv()
                part = buf.at[h2, pl.ds(lo, n)]
                out.append(send(part, part, head=h1))
            return out

        c_tok.wait()
        ag_tok = gather_start(s.tok, 2)

        lane = lax.broadcasted_iota(jnp.int32, (1, LANES), 1)
        low = lane < DH
        ones_lanes = ((lane == DH) | (lane == DH + 1)).astype(F32)
        seg_all = seg_ref[...].astype(F32)
        first = seq == 0
        seg_half = jnp.where(first, seg_all[:, :T], seg_all[:, T : 2 * T])
        seg_prev = jnp.where(first, -1.0, seg_all[:, T - BLK : T])
        tail_one = jnp.where(first, -1.0, jnp.broadcast_to(seg_all[:, T - 1 : T], (1, LANES)))
        tail_two = jnp.where(
            first, -1.0, jnp.broadcast_to(seg_all[:, T - BLK - 1 : T - BLK], (1, LANES))
        )
        s.segrow[...] = jnp.broadcast_to(seg_half, (8, T))
        s.segcol[...] = jnp.transpose(jnp.broadcast_to(seg_half, (LANES, T)))
        segcol = s.segcol[...]
        row_id = lax.broadcasted_iota(jnp.int32, (T, LANES), 0)
        mask_two = ((segcol == segcol[T - BLK - 1 : T - BLK, :]) & (row_id < T - BLK)).astype(F32)
        prev_col = jnp.transpose(jnp.broadcast_to(seg_prev, (LANES, BLK)))
        s.mprev[...] = (prev_col == tail_one).astype(F32)
        link = (tail_one == tail_two).astype(F32)
        s.link[...] = jnp.broadcast_to(jnp.concatenate([link] * (M // LANES), axis=1), (8, M))
        s.m0[...] = mask_two
        s.mfar[...] = jnp.where(
            row_id < BLK, (segcol == tail_two).astype(F32), (segcol == tail_one).astype(F32)
        )
        nblk = pat_ref.shape[1]
        per_half = T // BLK
        hot = (
            lax.broadcasted_iota(jnp.int32, (T, nblk), 1)
            == lax.broadcasted_iota(jnp.int32, (T, nblk), 0) // BLK + seq * per_half
        ).astype(F32)
        pat = pat_ref[...].astype(F32)
        for h in range(H):
            s.thr[h] = 3.0 - nn(
                (hot * pat[h : h + 1, :]).astype(BF16), jnp.ones((nblk, LANES), BF16)
            )
        wrow = lax.broadcasted_iota(jnp.int32, (TILE, 2 * TILE), 0)
        wcol = lax.broadcasted_iota(jnp.int32, (TILE, 2 * TILE), 1)
        dist = 2 + wrow // BLK - wcol // BLK
        kind = jnp.where(
            dist >= 2,
            1.0,
            jnp.where(dist == 1, 2.0, jnp.where((dist == 0) & (wcol - TILE <= wrow), 3.0, 0.0)),
        )
        for t in range(nt_tiles):
            col = segcol[t * TILE : (t + 1) * TILE, :]
            for side in range(2):
                tile = t - 1 + side
                if tile < 0:
                    continue
                same = col == s.segrow[0:1, tile * TILE : (tile + 1) * TILE]
                s.code[t, :, side * TILE : (side + 1) * TILE] = jnp.where(
                    same, kind[:, side * TILE : (side + 1) * TILE], 0.0
                )
        scale = DH ** (-0.25)
        om = omega_ref[...] * scale
        om_high = om.astype(BF16)
        s.omst[0:DH, :] = om_high
        s.omst[DH : 2 * DH, :] = (om - om_high.astype(F32)).astype(BF16)
        s.omtmp[...] = jnp.zeros((LANES, M), F32)
        s.omtmp[0:DH, :] = om
        s.omtmp[DH : DH + 8, :] = (
            lax.broadcasted_iota(jnp.int32, (8, M), 0) == 0
        ).astype(F32)
        s.omt[...] = jnp.transpose(s.omtmp[...]).astype(BF16)
        c_wqkv.wait()
        for c in range(3):
            for h in range(H):
                src = s.wqkv[c * E + h * DH : c * E + (h + 1) * DH, :]
                base = (c * H + h) * LANES
                s.wpad[base : base + DH, :] = src
                s.wpad[base + DH : base + 2 * DH, :] = src if c < 2 else jnp.zeros_like(src)
        c_wout.wait()
        for h in range(H):
            s.wopad[h * LANES : h * LANES + DH, :] = s.wo[head, h * DH : (h + 1) * DH, :]
            s.wopad[h * LANES + DH : (h + 1) * LANES, :] = jnp.zeros((DH, D), BF16)
        for h in range(H):
            s.rin[h, STATE:LANES, :] = jnp.zeros((LANES - STATE, M), BF16)
            s.grin[h, STATE:LANES, :] = jnp.zeros((LANES - STATE, M), BF16)

        def features(twice):
            x = twice.astype(F32)
            square = jnp.sum(x * x, axis=-1, keepdims=True)
            projected = nn(twice, s.omst[...])
            return jnp.exp(projected - square * (scale * scale * 0.25)) * (1.0 / math.sqrt(M))

        gain1, bias1 = g1_ref[...].reshape(1, D), b1_ref[...].reshape(1, D)
        gain2, bias2 = g2_ref[...].reshape(1, D), b2_ref[...].reshape(1, D)

        def project(slot):
            xhat, _ = normalize(s.tok[slot].astype(F32))
            normed = (xhat * gain1 + bias1).astype(BF16)
            at = rows(slot)
            s.n1[at, :] = normed
            for c in range(3):
                out = nt(normed, s.wpad[c * H * LANES : (c + 1) * H * LANES, :])
                for h in range(H):
                    part = out[:, h * LANES : (h + 1) * LANES]
                    if c == 2:
                        s.v[h, at, :] = (part + ones_lanes).astype(BF16)
                    else:
                        low_part = part.astype(BF16)
                        (s.q, s.k)[c][h, at, :] = low_part
                        (s.fq, s.fk)[c][h, at, :] = features(low_part).astype(BF16)

        project(head)
        for _, beside, _, _ in ag_tok:
            beside.wait_recv()
        project(h1)
        fw_tok = gather_forward(s.tok, ag_tok)
        ag_wo = gather_start(s.wo, 1)
        project(h2)
        for c in fw_tok:
            c.wait_recv()
        project(h3)

        for h in range(H):
            fk = s.fk[h]
            v = s.v[h].astype(F32)
            v0 = (v * s.m0[...]).astype(BF16)
            s.v0[h] = v0
            s.rout[h] = tn(v0, fk)[:STATE].astype(BF16)
            kk = s.k[h, T - BLK : T, :].astype(F32)
            vv = v[T - BLK : T, :]
            s.kvout[h] = jnp.where(low, kk, pltpu.roll(vv, DH, 1)).astype(BF16)
        ex_kv = send(s.kvout, s.kvin, seq=other)
        ex_r = send(s.rout, s.rin.at[:, pl.ds(0, STATE)], seq=other)
        c_og.wait()
        ag_og = gather_start(s.og, 1)

        def attend(h, carry):
            for t in range(nt_tiles):
                lo, hi = t * TILE, (t + 1) * TILE
                w0 = max(0, lo - TILE)
                fq = s.fq[h, lo:hi, :]
                low_rank = nt(fq, s.fk[h, 0:hi, :])
                exact = jnp.exp(nt(s.q[h, lo:hi, :], s.k[h, w0:hi, :]) * (0.5 / math.sqrt(DH)))
                tiles = (hi - w0) // TILE
                code = s.code[t, :, (2 - tiles) * TILE :]
                thr = jnp.concatenate([s.thr[h, lo:hi, :]] * tiles, axis=1)
                near = jnp.where(
                    code >= thr, exact, jnp.where(code >= 1.0, low_rank[:, w0:], 0.0)
                )
                if w0 > 0:
                    col = jnp.concatenate([s.segcol[lo:hi, :]] * (w0 // TILE), axis=1)
                    far = jnp.where(col == s.segrow[0:1, 0:w0], low_rank[:, :w0], 0.0)
                    near = jnp.concatenate([far, near], axis=1)
                w = near.astype(BF16)
                s.w[h, lo:hi, 0:hi] = w
                s.acc[h, lo:hi, :] = nn(w, s.v[h, 0:hi, :])
            return carry

        lax.fori_loop(0, H, attend, 0)
        fw_wo = gather_forward(s.wo, ag_wo)

        if inner:
            for j in range(nh):
                lo = j * TILE
                s.n1t[:, lo : lo + TILE] = jnp.transpose(s.n1[lo : lo + TILE, :])

        ex_kv.wait_recv()
        ex_r.wait_recv()

        def unpack(packed):
            x = packed.astype(F32)
            turned = pltpu.roll(x, DH, 1)
            twice = jnp.where(low, x, turned).astype(BF16)
            return twice, jnp.where(low, turned, 0.0)

        same_in = s.segcol[0:BLK, 0:BLK] == seg_prev
        for h in range(H):
            k_in, v_in = unpack(s.kvin[h])
            v_in = (v_in + ones_lanes).astype(BF16)
            f_in = features(k_in).astype(BF16)
            s.kin[h] = k_in
            s.vin[h] = v_in
            s.fin[h] = f_in
            q0 = s.q[h, 0:BLK, :]
            fq0 = s.fq[h, 0:BLK, :]
            exact = jnp.exp(nt(q0, k_in) * (0.5 / math.sqrt(DH)))
            low_rank = nt(fq0, f_in)
            use_exact = s.thr[h, 0:BLK, 0:BLK] < 2.5
            w_in = jnp.where(same_in, jnp.where(use_exact, exact, low_rank), 0.0).astype(BF16)
            s.win[h] = w_in
            state = s.rin[h]
            later = state.astype(F32) * s.link[0:1, :] + tn(
                (v_in.astype(F32) * s.mprev[...]).astype(BF16), f_in
            )
            s.rlater[h] = later.astype(BF16)
            far0 = jnp.where(s.mfar[0:BLK, :] > 0.5, nt(fq0, state), 0.0)
            s.acc[h, 0:BLK, :] = s.acc[h, 0:BLK, :] + nn(w_in, v_in) + far0
            far1 = jnp.where(
                s.mfar[BLK:T, :] > 0.5, nt(s.fq[h, BLK:T, :], s.rlater[h]), 0.0
            )
            s.acc[h, BLK:T, :] = s.acc[h, BLK:T, :] + far1

        def divided(h, lo, hi):
            acc = s.acc[h, lo:hi, :]
            inv = 1.0 / acc[:, DH : DH + 1]
            return acc * inv, inv

        order = (0, 2, 1, 3)
        ag_at = {}
        for t in order:
            lo, hi = t * TILE, (t + 1) * TILE
            outs = [divided(h, lo, hi)[0] for h in range(H)]
            for h in range(0, H, 2):
                if h + 1 < H:
                    both = jnp.where(low, outs[h], pltpu.roll(outs[h + 1], DH, 1))
                    s.at[head, lo:hi, h * DH : (h + 2) * DH] = both.astype(BF16)
                else:
                    s.at[head, lo:hi, h * DH : (h + 1) * DH] = outs[h][:, :DH].astype(BF16)
            part = s.at.at[head, pl.ds(lo, TILE)]
            ag_at[t] = (send(part, part, head=h2), send(part, part, head=h1))
        for c in fw_wo:
            c.wait_recv()
        for _, c, _, _ in ag_wo:
            c.wait_recv()
        fw_og = gather_forward(s.og, ag_og)
        for _, c, _, _ in ag_og:
            c.wait_recv()
        for c in fw_og:
            c.wait_recv()
        c_wup.wait()
        c_wdown.wait()
        if inner:
            for j in range(nh):
                lo = j * TILE
                s.ogt[:, lo : lo + TILE] = jnp.transpose(s.og[j])
        fw_at = {}

        def forward_attended(t):
            ag_at[t][0].wait_recv()
            part = s.at.at[h2, pl.ds(t * TILE, TILE)]
            fw_at[t] = send(part, part, head=h1)

        def scatter_beside(make, bufs):
            bufs.out[0] = make(h3).astype(BF16)
            a = send(bufs.out.at[0], bufs.got.at[0], head=h1)
            bufs.mine[...] = make(h2)
            return a

        def scatter_across(bufs, a):
            a.wait_recv()
            bufs.out[1] = (bufs.mine[...] + bufs.got[0].astype(F32)).astype(BF16)
            return send(bufs.out.at[1], bufs.got.at[1], head=h2)

        def scatter_last(make, bufs):
            bufs.out[2] = make(h1).astype(BF16)
            return send(bufs.out.at[2], bufs.got.at[2], head=h1)

        def scatter_done(bufs, b, c):
            c.wait_recv()
            part = bufs.got[2].astype(F32)
            b.wait_recv()
            return part + bufs.got[1].astype(F32)

        def feed(slot):
            ag_at[slot][1].wait_recv()
            fw_at[slot].wait_recv()
            at = slice(slot * TILE, (slot + 1) * TILE)
            hid = s.tok[slot].astype(F32)
            for j in range(nh):
                hid = hid + nn(s.at[j, at, :], s.wo[j])
            s.hid[at, :] = hid
            xhat, _ = normalize(hid)
            normed = (xhat * gain2 + bias2).astype(BF16)
            s.n2[at, :] = normed
            act, slope = gelu_both(nn(normed, s.wup[...]))
            s.act[at, :] = act.astype(BF16)
            gu = (nt(s.og[slot], s.wdown[...]) * slope).astype(BF16)
            s.gu[at, :] = gu
            s.ra.part[slot] = nt(gu, s.wup[...])

        core = lax.rem(head, 2)
        ra_a = {
            t: prepare(s.ra.out.at[t], s.ra.got.at[t], head=h1) for t in range(nh)
        }
        ra_b = prepare(s.ra.bout, s.ra.bgot, head=h2)

        def to_core(t):
            @pl.when(core != t % 2)
            def _():
                s.ra.out[t] = s.ra.part[t].astype(BF16)
                ra_a[t].start()

        def to_chip(t):
            @pl.when(h2 == t)
            def _():
                ra_a[t].wait_recv()
                s.ra.bout[...] = (s.ra.part[t] + s.ra.got[t].astype(F32)).astype(BF16)
                ra_b.start()

        forward_attended(order[0])
        for i, t in enumerate(order):
            if i + 1 < nh:
                forward_attended(order[i + 1])
            feed(t)
            to_core(t)
            if i > 0:
                to_chip(order[i - 1])
        to_chip(order[-1])

        b1 = bat + 1 - 2 * lax.rem(bat, 2)
        b2 = lax.rem(bat + 2, nb)
        b3 = lax.rem(b1 + 2, nb)
        there = pl.ds(pl.multiple_of(other * half_rows, LANES), half_rows)
        here = pl.ds(pl.multiple_of(seq * half_rows, LANES), half_rows)

        def y_send(g):
            right = g.right()
            g.ys[...] = nn(g.left[there, :], right).astype(BF16)
            g.y = send(g.ys, g.yr, seq=other)
            g.own[...] = nn(g.left[here, :], right)

        def with_y(g, index):
            at = rows(index, piece)
            return g.own[at, :] + g.yr[at, :].astype(F32)

        def za_send(g):
            g.y.wait_recv()
            for i, index in enumerate((b1, b3)):
                g.zas[i] = with_y(g, index).astype(BF16)
            g.za = send(g.zas, g.zar, batch=b1)

        def zb_send(g):
            g.za.wait_recv()
            g.zbs[...] = (with_y(g, b2) + g.zar[1].astype(F32)).astype(BF16)
            g.zb = send(g.zbs, g.zbr, batch=b2)

        def weight_sum(g):
            total = with_y(g, bat) + g.zar[0].astype(F32)
            g.zb.wait_recv()
            return total + g.zbr[...].astype(F32)

        def zd_send(g):
            g.y.wait_recv()
            g.zd = []
            for i, index in enumerate((b2, b1, b3)):
                g.zds[i] = with_y(g, index).astype(BF16)
                g.zd.append(send(g.zds.at[i], g.zdr.at[i], batch=index))

        def weight_sum_direct(g):
            total = with_y(g, bat)
            for i in (1, 2, 0):
                g.zd[i].wait_recv()
                total = total + g.zdr[i].astype(F32)
            return total

        def both(index):
            return [rows(half * nb + index, piece) for half in range(ns)]

        def first_za(g):
            g.own[...] = nn(g.left[...], g.right())
            for i, index in enumerate((b1, b3)):
                for half, at in enumerate(both(index)):
                    g.zas[i, half] = g.own[at, :].astype(BF16)
            g.za = send(g.zas, g.zar, batch=b1)

        def first_zb(g):
            g.za.wait_recv()
            for half, at in enumerate(both(b2)):
                g.zbs[half] = (g.own[at, :] + g.zar[1, half].astype(F32)).astype(BF16)
            g.zb = send(g.zbs, g.zbr, batch=b2)

        def first_part(g, half):
            at = rows(half * nb + bat, piece)
            return g.own[at, :] + g.zar[0, half].astype(F32) + g.zbr[half].astype(F32)

        def first_y(g):
            g.zb.wait_recv()
            g.ys[...] = first_part(g, other).astype(BF16)
            g.y = send(g.ys, g.yr, seq=other)

        def first_sum(g):
            total = first_part(g, seq)
            g.y.wait_recv()
            return total + g.yr[...].astype(F32)

        def collect(g):
            if hasattr(g, "zdr"):
                return weight_sum_direct(g)
            return weight_sum(g) if g.zbs.shape[0] == piece else first_sum(g)

        def chunks(groups, left, ref):
            width = ref.shape[-1] // len(groups)
            for i, g in enumerate(groups):
                g.left = left
                g.right = lambda i=i: ref[:, i * width : (i + 1) * width]

        steps = {}
        if inner:
            downs, ups, qkvs = (s.d0, s.d1), (s.u0, s.u1), (s.x0, s.x1, s.x2)
            chunks(downs, s.ogt, s.act)
            chunks(ups, s.n2t, s.gu)
            chunks((s.o0,), s.gbt, s.at.at[head])
            chunks(qkvs, s.n1t, s.gqkv)
            steps = {
                0: [(first_za, s.d1)],
                1: [(y_send, s.d0)],
                5: [(y_send, s.u0)],
                6: [(first_za, s.u1)],
                7: [(first_zb, s.d1)],
                9: [(za_send, s.d0)],
                15: [(first_zb, s.u1)],
                17: [(y_send, s.o0)],
                19: [(za_send, s.u0)],
                21: [(y_send, s.x0)],
                24: [(zb_send, s.d0)],
                27: [(za_send, s.o0), (y_send, s.x1)],
                28: [(zb_send, s.u0), (za_send, s.x0)],
                29: [(y_send, s.x2), (zb_send, s.o0), (zd_send, s.x1)],
                30: [(first_y, s.d1)],
                31: [(za_send, s.x2)],
                34: [(zb_send, s.x0)],
                36: [(first_y, s.u1)],
                37: [(zb_send, s.x2)],
            }

        def run(*numbers):
            for number in numbers:
                for step, group in steps.get(number, ()):
                    step(group)

        run(0, 1)
        for t in range(nh):

            @pl.when(head == t)
            def _():
                ra_a[t].wait_recv()

        ra_b.wait_recv()
        run(2)
        grad2 = s.ra.part[head] + s.ra.got[head].astype(F32) + s.ra.bgot[...].astype(F32)
        mine = rows(head)
        xhat2, rstd2 = normalize(s.hid[mine, :])
        s.ns[...] = jnp.zeros_like(s.ns)
        s.ns[2:3, :] = jnp.sum(grad2 * xhat2, axis=0, keepdims=True)
        s.ns[3:4, :] = jnp.sum(grad2, axis=0, keepdims=True)
        grad_hidden = s.og[head].astype(F32) + norm_back(grad2, gain2, xhat2, rstd2)
        s.gh[...] = grad_hidden
        s.gb[head] = grad_hidden.astype(BF16)
        run(3)
        ag_gb = gather_start(s.gb, 2)
        run(4)
        if inner:
            for j in range(nh):
                lo = j * TILE
                s.n2t[:, lo : lo + TILE] = jnp.transpose(s.n2[lo : lo + TILE, :])
        run(5, 6)

        def lower(slot):
            return nn(s.act[rows(slot), :], s.wdown[...])

        rc_a = scatter_beside(lower, s.rc)
        rc_c = scatter_last(lower, s.rc)
        run(7)

        def divide_back(slot):
            at = rows(slot)
            ga = nt(s.gb[slot], s.wopad[...])
            for h in range(H):
                acc = s.acc[h, at, :]
                inv = 1.0 / acc[:, DH : DH + 1]
                gnum = ga[:, h * LANES : (h + 1) * LANES] * inv
                gden = -jnp.sum(gnum * acc, axis=-1, keepdims=True) * inv
                high = gden.astype(BF16).astype(F32)
                gnum = jnp.where(lane == DH, high, jnp.where(lane == DH + 1, gden - high, gnum))
                s.gn[h, at, :] = gnum.astype(BF16)

        divide_back(head)
        for _, c, _, _ in ag_gb:
            c.wait_recv()
        divide_back(h1)
        run(8)
        fw_gb = gather_forward(s.gb, ag_gb)
        divide_back(h2)
        for c in fw_gb:
            c.wait_recv()
        run(9)
        divide_back(h3)
        run(10)

        def feature_back(gfeat, feat, twice):
            x = nn((gfeat * feat.astype(F32)).astype(BF16), s.omt[...])
            return x - twice.astype(F32) * (x[:, DH : DH + 1] * (scale * scale))

        for h in range(H):
            gm = jnp.where(s.mfar[...] > 0.5, s.gn[h].astype(F32), 0.0).astype(BF16)
            s.gm[h] = gm
            glater = tn(gm[BLK:T, :], s.fq[h, BLK:T, :])
            gstate = tn(gm[0:BLK, :], s.fq[h, 0:BLK, :]) + glater * s.link[0:1, :]
            s.grout[h] = gstate[:STATE].astype(BF16)
            glater = glater.astype(BF16)
            v_last = (s.vin[h].astype(F32) * s.mprev[...]).astype(BF16)
            gn0 = s.gn[h, 0:BLK, :]
            q0 = s.q[h, 0:BLK, :]
            fq0 = s.fq[h, 0:BLK, :]
            gw = nt(gn0, s.vin[h])
            w_in = s.win[h]
            use_exact = s.thr[h, 0:BLK, 0:BLK] < 2.5
            gs = jnp.where(
                same_in & use_exact, gw * w_in.astype(F32) * (1.0 / math.sqrt(DH)), 0.0
            ).astype(BF16)
            gp = jnp.where(same_in & jnp.logical_not(use_exact), gw, 0.0).astype(BF16)
            gfeat = tn(gp, fq0) + nn(v_last, glater)
            gk = feature_back(gfeat, s.fin[h], s.kin[h]) + tn(gs, q0)
            gv = tn(w_in, gn0) + s.mprev[...] * nt(s.fin[h], glater)
            s.gkvout[h] = jnp.where(low, gk, pltpu.roll(gv, DH, 1)).astype(BF16)
            s.gfq0[h] = nn(gp, s.fin[h])
            s.gq0[h] = nn(gs, s.kin[h])
        run(11)
        ex_gkv = send(s.gkvout, s.gkvin, seq=other)
        ex_gr = send(s.grout, s.grin.at[:, pl.ds(0, STATE)], seq=other)

        run(12)
        rc_b = scatter_across(s.rc, rc_a)
        run(13)

        def attend_back(h):
            for t in range(nt_tiles):
                lo, hi = t * TILE, (t + 1) * TILE
                w0 = max(0, lo - TILE)
                tiles = (hi - w0) // TILE
                gw = nt(s.gn[h, lo:hi, :], s.v[h, 0:hi, :])
                code = s.code[t, :, (2 - tiles) * TILE :]
                thr = jnp.concatenate([s.thr[h, lo:hi, :]] * tiles, axis=1)
                use_exact = code >= thr
                near = gw[:, w0:]
                gs = jnp.where(
                    use_exact,
                    near * s.w[h, lo:hi, w0:hi].astype(F32) * (1.0 / math.sqrt(DH)),
                    0.0,
                ).astype(BF16)
                gp = jnp.where((code >= 1.0) & (code < thr), near, 0.0)
                if w0 > 0:
                    col = jnp.concatenate([s.segcol[lo:hi, :]] * (w0 // TILE), axis=1)
                    far = jnp.where(col == s.segrow[0:1, 0:w0], gw[:, :w0], 0.0)
                    gp = jnp.concatenate([far, gp], axis=1)
                gp = gp.astype(BF16)
                s.gp[lo:hi, 0:hi] = gp
                s.gs[lo:hi, (2 - tiles) * TILE :] = gs
                gfq = nn(gp, s.fk[h, 0:hi, :])
                gq = nn(gs, s.k[h, w0:hi, :])
                gm = s.gm[h, lo:hi, :]
                if t == 0:
                    top = nn(gm[0:BLK], s.rin[h]) + s.gfq0[h]
                    bottom = nn(gm[BLK:], s.rlater[h])
                    gfq = gfq + jnp.concatenate([top, bottom], axis=0)
                    gq = gq + jnp.concatenate(
                        [s.gq0[h], jnp.zeros((TILE - BLK, LANES), F32)], axis=0
                    )
                else:
                    gfq = gfq + nn(gm, s.rlater[h])
                gq = gq + feature_back(gfq, s.fq[h, lo:hi, :], s.q[h, lo:hi, :])
                s.gq[h, lo:hi, :] = gq
            for t in range(nt_tiles):
                lo, hi = t * TILE, (t + 1) * TILE
                s.gfk[h, lo:hi, :] = tn(s.gp[lo:T, lo:hi], s.fq[h, lo:T, :])
                s.gv[h, lo:hi, :] = tn(s.w[h, lo:T, lo:hi], s.gn[h, lo:T, :])
                gk = tn(s.gs[lo:hi, TILE:], s.q[h, lo:hi, :])
                if t + 1 < nt_tiles:
                    gk = gk + tn(s.gs[hi : hi + TILE, :TILE], s.q[h, hi : hi + TILE, :])
                s.gk[h, lo:hi, :] = gk

        for h in range(H):
            attend_back(h)
            run(14 + min(h, 2))
        if inner:
            for j in range(nh):
                lo = j * TILE
                s.gbt[:, lo : lo + TILE] = jnp.transpose(s.gb[j])
        run(17)

        ex_gkv.wait_recv()
        ex_gr.wait_recv()
        run(18)

        def finish(h, carry):
            state = jnp.where(first, s.grin[h].astype(F32), 0.0).astype(BF16)
            gfk = s.gfk[h] + nn(s.v0[h], state)
            fk = s.fk[h]
            gv = s.gv[h] + s.m0[...] * nt(fk, state)
            gk = s.gk[h] + feature_back(gfk, fk, s.k[h])
            s.gk[h] = gk
            s.gv[h] = gv
            back = jnp.where(first, s.gkvin[h].astype(F32), 0.0)
            s.gk[h, T - BLK : T, :] = s.gk[h, T - BLK : T, :] + back
            s.gv[h, T - BLK : T, :] = s.gv[h, T - BLK : T, :] + pltpu.roll(back, DH, 1)
            return carry

        lax.fori_loop(0, H, finish, 0)
        parts = [(n, h) for n in (s.gq, s.gk, s.gv) for h in range(H)]
        for i in range(0, len(parts), 2):
            (na, ha) = parts[i]
            a = na[ha]
            if i + 1 < len(parts):
                (nb_, hb) = parts[i + 1]
                a = jnp.where(low, a, pltpu.roll(nb_[hb], DH, 1))
                s.gqkv[:, i * DH : (i + 2) * DH] = a.astype(BF16)
            else:
                s.gqkv[:, i * DH : (i + 1) * DH] = a[:, :DH].astype(BF16)

        run(19, 20, 21, 22)

        def first_grad(slot):
            return nn(s.gqkv[rows(slot), :], s.wqkv[...])

        rb_a = scatter_beside(first_grad, s.rb)
        run(23)
        rb_b = scatter_across(s.rb, rb_a)
        run(24)
        rb_c = scatter_last(first_grad, s.rb)
        run(25)
        own = first_grad(head)
        run(26)
        own_mixed = s.hid[mine, :] + lower(head)

        run(27, 28)
        grad1 = own + scatter_done(s.rb, rb_b, rb_c)
        run(29)
        xhat1, rstd1 = normalize(s.tok[head].astype(F32))
        s.ns[0:1, :] = jnp.sum(grad1 * xhat1, axis=0, keepdims=True)
        s.ns[1:2, :] = jnp.sum(grad1, axis=0, keepdims=True)
        gtok_ref[0] = s.gh[...] + norm_back(grad1, gain1, xhat1, rstd1)

        if inner:
            run(30)
            n_h = [send(s.ns, s.nh.at[i], head=d) for i, d in enumerate((h1, h2, h3))]
            run(31)
            total = s.ns[...]
            for i, c in enumerate(n_h):
                c.wait_recv()
                total = total + s.nh[i]
            s.ns2[...] = total
            run(32)
            n_y = send(s.ns2, s.ny, seq=other)
            run(33)
        mixed_ref[0] = (own_mixed + scatter_done(s.rc, rc_b, rc_c)).astype(BF16)
        if inner:
            run(34)
            n_y.wait_recv()
            run(35)
            s.ns3[...] = s.ns2[...] + s.ny[...]
            n_z = [
                send(s.ns3, s.nz.at[d - 1], batch=lax.rem(bat + d, nb)) for d in range(1, nb)
            ]
            run(36, 37)
            wide = FL // 2
            for i in range(2):
                odown_ref[:, i * wide : (i + 1) * wide] = collect(downs[i])
                oup_ref[:, i * wide : (i + 1) * wide] = collect(ups[i])
            s.otmp[...] = jnp.zeros_like(s.otmp)
            s.otmp[0:piece, 0:E] = collect(s.o0)
            oout_ref[...] = jnp.transpose(s.otmp[...])[:E, :piece]
            total = s.ns3[...]
            for i, c in enumerate(n_z):
                c.wait_recv()
                total = total + s.nz[i]
            width = D // (ns * nb * nh)
            start = ((seq * nb + bat) * nh + head) * width
            pick = (
                lax.broadcasted_iota(jnp.int32, (D, LANES), 0)
                == lax.broadcasted_iota(jnp.int32, (D, LANES), 1) + start
            ).astype(F32)
            norm_ref[...] = lax.dot_general(
                total, pick, (((1,), (0,)), ((), ())),
                precision=lax.Precision.HIGHEST, preferred_element_type=F32,
            )
            for i, g in enumerate(qkvs):
                oqkv_ref[i] = collect(g)
        else:

            def joined(ref):
                return jnp.concatenate([ref[j] for j in range(nh)], axis=0)

            norm_ref[...] = s.ns[...]
            odown_ref[...] = tn(joined(s.og), s.act[...])
            oup_ref[...] = tn(s.n2[...], s.gu[...])
            oout_ref[...] = tn(joined(s.gb), s.at[head])
            oqkv_ref[...] = tn(s.n1[...], s.gqkv[...])
        for t in range(nh):

            @pl.when(core != t % 2)
            def _():
                ra_a[t].wait_send()

        ra_b.wait_send()
        for c in sends:
            c.wait_send()

    return kernel


def build(dims):
    nh, ns, nb, T, R, D, E, FL, H, M, inner = dims
    plan = Plan()
    piece = D // (ns * nb)
    half = D // ns
    plan.add(
        tok=((nh, R, D), BF16),
        og=((nh, R, D), BF16),
        wqkv=((3 * E, D), BF16),
        wo=((nh, E, D), BF16),
        wup=((D, FL), BF16),
        wdown=((FL, D), BF16),
        wpad=((3 * H * LANES, D), BF16),
        wopad=((H * LANES, D), BF16),
        segrow=((8, T), F32),
        segcol=((T, LANES), F32),
        m0=((T, LANES), F32),
        mprev=((BLK, LANES), F32),
        link=((8, M), F32),
        mfar=((T, LANES), F32),
        thr=((H, T, LANES), F32),
        code=((T // TILE, TILE, 2 * TILE), F32),
        omst=((2 * DH, M), BF16),
        omtmp=((LANES, M), F32),
        omt=((M, LANES), BF16),
        n1=((T, D), BF16),
        q=((H, T, LANES), BF16),
        k=((H, T, LANES), BF16),
        v=((H, T, LANES), BF16),
        v0=((H, T, LANES), BF16),
        gn=((H, T, LANES), BF16),
        gm=((H, T, LANES), BF16),
        fq=((H, T, M), BF16),
        fk=((H, T, M), BF16),
        rout=((H, STATE, M), BF16),
        grout=((H, STATE, M), BF16),
        rin=((H, LANES, M), BF16),
        grin=((H, LANES, M), BF16),
        rlater=((H, LANES, M), BF16),
        kvout=((H, BLK, LANES), BF16),
        kvin=((H, BLK, LANES), BF16),
        gkvout=((H, BLK, LANES), BF16),
        gkvin=((H, BLK, LANES), BF16),
        kin=((H, BLK, LANES), BF16),
        vin=((H, BLK, LANES), BF16),
        fin=((H, BLK, M), BF16),
        win=((H, BLK, BLK), BF16),
        gfq0=((H, BLK, M), F32),
        gq0=((H, BLK, LANES), F32),
        w=((H, T, T), BF16),
        acc=((H, T, LANES), F32),
        at=((nh, T, E), BF16),
        hid=((T, D), F32),
        n2=((T, D), BF16),
        act=((T, FL), BF16),
        gu=((T, FL), BF16),
        gh=((R, D), F32),
        gb=((nh, R, D), BF16),
        gp=((T, T), BF16),
        gs=((T, 2 * TILE), BF16),
        gfk=((H, T, M), F32),
        gq=((H, T, LANES), F32),
        gk=((H, T, LANES), F32),
        gv=((H, T, LANES), F32),
        gqkv=((T, 3 * E), BF16),
        ns=((8, D), F32),
    )
    pair = dict(out=((3, R, D), BF16), got=((3, R, D), BF16), mine=((R, D), F32))
    plan.group(rb=pair, rc=pair)
    plan.group(
        ra=dict(
            part=((nh, R, D), F32),
            out=((nh, R, D), BF16),
            got=((nh, R, D), BF16),
            bout=((R, D), BF16),
            bgot=((R, D), BF16),
        )
    )
    if inner:

        def weight(width):
            return dict(
                ys=((half, width), BF16),
                yr=((half, width), BF16),
                own=((half, width), F32),
                zas=((2, piece, width), BF16),
                zar=((2, piece, width), BF16),
                zbs=((piece, width), BF16),
                zbr=((piece, width), BF16),
            )

        def weight_direct(width):
            return dict(
                ys=((half, width), BF16),
                yr=((half, width), BF16),
                own=((half, width), F32),
                zds=((nb - 1, piece, width), BF16),
                zdr=((nb - 1, piece, width), BF16),
            )

        def weight_first(width):
            return dict(
                own=((D, width), F32),
                zas=((2, ns, piece, width), BF16),
                zar=((2, ns, piece, width), BF16),
                zbs=((ns, piece, width), BF16),
                zbr=((ns, piece, width), BF16),
                ys=((piece, width), BF16),
                yr=((piece, width), BF16),
            )

        wide, narrow = FL // 2, E
        plan.group(
            d0=weight(wide),
            d1=weight_first(wide),
            u0=weight(wide),
            u1=weight_first(wide),
            o0=weight(narrow),
            x0=weight(narrow),
            x1=weight_direct(narrow),
            x2=weight(narrow),
        )
        turned = ((D, T), BF16)
        plan.add(n1t=turned, n2t=turned, ogt=turned, gbt=turned)
        plan.add(
            ns2=((8, D), F32),
            ns3=((8, D), F32),
            nz=((nb - 1, 8, D), F32),
            ny=((8, D), F32),
            nh=((3, 8, D), F32),
            otmp=((LANES, 2 * LANES), F32),
        )
    plan.semaphores(ssem=96, rsem=96, lsem=8)

    if inner:
        grads = [(3, piece, E), (E, piece), (piece, FL), (piece, FL)]
        norm = (8, LANES)
    else:
        grads = [(D, 3 * E), (D, E), (D, FL), (D, FL)]
        norm = (8, D)
    outs = [((1, R, D), BF16), ((1, R, D), F32), (norm, F32)] + [(g, F32) for g in grads]
    hbm = pl.BlockSpec(memory_space=pltpu.HBM)
    vmem = pl.BlockSpec(memory_space=pltpu.VMEM)
    in_specs = [hbm, vmem, vmem, vmem, vmem, vmem, hbm, hbm, vmem, vmem, hbm, hbm, hbm]
    kernel = make_kernel(dims, len(in_specs), len(outs), plan)
    return pl.pallas_call(
        kernel,
        out_shape=[jax.ShapeDtypeStruct(shape, dtype) for shape, dtype in outs],
        in_specs=in_specs,
        out_specs=[vmem] * len(outs),
        scratch_shapes=plan.shapes,
        compiler_params=pltpu.CompilerParams(
            collective_id=0, has_side_effects=True, vmem_limit_bytes=60 << 20
        ),
        name="block",
    )


def hand_over(width, *arrays):
    count = len(arrays) - 1

    def kernel(*refs):
        ins, norm_ref = refs[:count], refs[count]
        outs, norm_outs = refs[count + 1 : 2 * count + 1], refs[2 * count + 1 :]
        for a, b in zip(ins, outs):
            b[...] = a[...]
        for i, out in enumerate(norm_outs):
            out[...] = norm_ref[i, :width]

    vmem = pl.BlockSpec(memory_space=pltpu.VMEM)
    return pl.pallas_call(
        kernel,
        out_shape=[jax.ShapeDtypeStruct(a.shape, a.dtype) for a in arrays[:-1]]
        + [jax.ShapeDtypeStruct((width,), F32)] * 4,
        in_specs=[vmem] * len(arrays),
        out_specs=[vmem] * (count + 4),
        name="hand_over",
    )(*arrays)


def per_device(
    mesh_shape,
    tokens,
    seg_ids,
    pattern,
    omega,
    norm1_gain,
    norm1_bias,
    w_qkv,
    w_out,
    norm2_gain,
    norm2_bias,
    w_up,
    w_down,
    out_grad,
):
    nh, ns, nb = mesh_shape
    rows, D = tokens.shape[1:]
    T = seg_ids.shape[1] // ns
    E = w_qkv.shape[2]
    FL = w_up.shape[1]
    piece = D // (ns * nb)
    inner = piece % 16 == 0 and nb == 4
    dims = (nh, ns, nb, T, rows, D, E, FL, E // DH, omega.shape[1], inner)
    w_flat = jnp.transpose(w_qkv, (1, 2, 0)).reshape(3 * E, D)
    mixed, grad_tokens, norms, g_qkv, g_out, g_up, g_down = build(dims)(
        tokens, seg_ids, pattern, omega, norm1_gain, norm1_bias, w_flat, w_out,
        norm2_gain, norm2_bias, w_up, w_down, out_grad,
    )
    if inner:
        width = D // (ns * nb * nh)
        mixed, grad_tokens, g_qkv, g_out, g_up, g_down, *norms = hand_over(
            width, mixed, grad_tokens, g_qkv, g_out, g_up, g_down, norms
        )
        g_qkv = jnp.transpose(g_qkv, (1, 0, 2))
        g_down = g_down.T
    else:
        group = ("seq", "batch")
        scatter = functools.partial(lax.psum_scatter, scatter_dimension=0, tiled=True)
        norms = lax.psum_scatter(
            norms[:4], ("seq", "batch", "head"), scatter_dimension=1, tiled=True
        )
        g_qkv = scatter(g_qkv, group).reshape(piece, 3, E)
        g_out = scatter(g_out, group).T
        g_up = scatter(g_up, group)
        g_down = scatter(g_down, group).T
    return (
        mixed, grad_tokens, norms[0], norms[1], g_qkv, g_out, norms[2], norms[3], g_up, g_down,
    )


def solution(mesh):
    placed = (
        P("batch", ("seq", "head"), None),
        P("batch", None),
        P("head", None),
        P(),
        P(),
        P(),
        P(None, None, "head"),
        P("head", None),
        P(),
        P(),
        P(None, "head"),
        P("head", None),
        P("batch", ("seq", "head"), None),
    )
    shape = (mesh.shape["head"], mesh.shape["seq"], mesh.shape["batch"])
    return jax.shard_map(
        functools.partial(per_device, shape),
        mesh=mesh,
        in_specs=placed,
        out_specs=(
            P("batch", ("seq", "head"), None),
            P("batch", ("seq", "head"), None),
            P(("seq", "batch", "head")),
            P(("seq", "batch", "head")),
            P(("seq", "batch"), None, "head"),
            P("head", ("seq", "batch")),
            P(("seq", "batch", "head")),
            P(("seq", "batch", "head")),
            P(("seq", "batch"), "head"),
            P("head", ("seq", "batch")),
        ),
        check_vma=False,
    )
```

```python
import functools
import math
from types import SimpleNamespace

import jax
import jax.numpy as jnp
from jax import lax
from jax.experimental import pallas as pl
from jax.experimental.pallas import tpu as pltpu
from jax.sharding import PartitionSpec as P

DH = 64
BLK = 64
LANES = 128
TILE = 128
STATE = 80
F32 = jnp.float32
BF16 = jnp.bfloat16
MESH = pl.DeviceIdType.MESH


def nn(a, b):
    return lax.dot_general(a, b, (((1,), (0,)), ((), ())), preferred_element_type=F32)


def nt(a, b):
    return lax.dot_general(a, b, (((1,), (1,)), ((), ())), preferred_element_type=F32)


def tn(a, b):
    return lax.dot_general(a, b, (((0,), (0,)), ((), ())), preferred_element_type=F32)


def normalize(x):
    center = x - jnp.mean(x, axis=-1, keepdims=True)
    rstd = lax.rsqrt(jnp.mean(center * center, axis=-1, keepdims=True) + 1e-05)
    return center * rstd, rstd


def norm_back(grad, gain, xhat, rstd):
    g = grad * gain
    return rstd * (
        g - jnp.mean(g, axis=-1, keepdims=True) - xhat * jnp.mean(g * xhat, axis=-1, keepdims=True)
    )


def gelu_both(u):
    k0 = math.sqrt(2.0 / math.pi)
    u2 = u * u
    th = jnp.tanh(k0 * (u + 0.044715 * u2 * u))
    half = 0.5 * (1.0 + th)
    slope = half + 0.5 * u * (1.0 - th * th) * (k0 * (1.0 + 3.0 * 0.044715 * u2))
    return u * half, slope


class Plan:
    def __init__(self):
        self.shapes = []
        self.tree = {}

    def add(self, into=None, **buffers):
        into = self.tree if into is None else into
        for name, (shape, dtype) in buffers.items():
            into[name] = len(self.shapes)
            self.shapes.append(pltpu.VMEM(shape, dtype))

    def group(self, **groups):
        for name, buffers in groups.items():
            self.tree[name] = {}
            self.add(self.tree[name], **buffers)

    def semaphores(self, **counts):
        for name, n in counts.items():
            self.tree[name] = len(self.shapes)
            self.shapes.append(pltpu.SemaphoreType.DMA((n,)))

    def bind(self, refs):
        def walk(tree):
            return SimpleNamespace(
                **{k: walk(v) if isinstance(v, dict) else refs[v] for k, v in tree.items()}
            )

        return walk(self.tree)


def make_kernel(dims, n_in, n_out, plan):
    nh, ns, nb, T, R, D, E, FL, H, M, inner = dims
    nt_tiles = T // TILE
    half_rows = D // ns
    piece = D // (ns * nb)

    def kernel(*refs):
        (
            tok_hbm, seg_hbm, pat_hbm, omega_hbm, g1_hbm, b1_hbm, wqkv_hbm, wout_hbm,
            g2_hbm, b2_hbm, wup_hbm, wdown_hbm, og_hbm,
        ) = refs[:n_in]
        (
            mixed_ref, gtok_ref, norm_ref, oqkv_ref, oout_ref, oup_ref, odown_ref,
        ) = refs[n_in : n_in + n_out]
        s = plan.bind(refs[n_in + n_out :])
        seg_ref, pat_ref, omega_ref = s.seg, s.pat, s.omega
        g1_ref, b1_ref, g2_ref, b2_ref = s.g1, s.b1, s.g2, s.b2
        ssem, rsem, lsem = s.ssem, s.rsem, s.lsem
        used = {"r": 0, "l": 0}
        sends = []

        head = lax.axis_index("head")
        seq = lax.axis_index("seq")
        bat = lax.axis_index("batch")
        h1 = head + 1 - 2 * lax.rem(head, 2)
        h2 = lax.rem(head + 2, nh)
        h3 = lax.rem(h1 + 2, nh)
        other = 1 - seq

        def local(src, dst):
            k = used["l"]
            used["l"] += 1
            c = pltpu.make_async_copy(src, dst, lsem.at[k])
            c.start()
            return c

        written = []

        def write(src, dst):
            written.append(local(src, dst))

        def send(src, dst, **dev):
            k = used["r"]
            used["r"] += 1
            c = pltpu.make_async_remote_copy(
                src_ref=src, dst_ref=dst, send_sem=ssem.at[k], recv_sem=rsem.at[k],
                device_id=dev, device_id_type=MESH,
            )
            c.start()
            sends.append(c)
            return c

        def prepare(src, dst, **dev):
            k = used["r"]
            used["r"] += 1
            return pltpu.make_async_remote_copy(
                src_ref=src, dst_ref=dst, send_sem=ssem.at[k], recv_sem=rsem.at[k],
                device_id=dev, device_id_type=MESH,
            )

        def rows(slot, n=TILE):
            return pl.ds(pl.multiple_of(slot * n, n), n)

        b1 = bat + 1 - 2 * lax.rem(bat, 2)
        barrier = pltpu.get_barrier_semaphore()
        peers = [dict(head=h1), dict(head=h2), dict(head=h3), dict(seq=other)]
        if inner:
            peers += [dict(batch=lax.rem(bat + d, nb)) for d in range(1, nb)]
        else:
            peers += [dict(batch=b1)]
        for dev in peers:
            pl.semaphore_signal(barrier, inc=1, device_id=dev, device_id_type=MESH)
        c_tok = local(tok_hbm.at[0], s.tok.at[head])
        c_wout = local(wout_hbm, s.wo.at[head])
        c_og = local(og_hbm.at[0], s.og.at[head])
        c_wqkv = local(wqkv_hbm, s.wqkv)
        small = [
            local(a, b)
            for a, b in (
                (seg_hbm, seg_ref), (pat_hbm, pat_ref), (omega_hbm, omega_ref),
                (g1_hbm, g1_ref), (b1_hbm, b1_ref), (g2_hbm, g2_ref), (b2_hbm, b2_ref),
            )
        ]
        c_wup = local(wup_hbm, s.wup)
        c_wdown = local(wdown_hbm, s.wdown)
        pl.semaphore_wait(barrier, len(peers))

        def gather_start(buf, chunks):
            n = buf.shape[1] // chunks
            out = []
            for i in range(chunks):
                part = buf.at[head, pl.ds(i * n, n)]
                across = send(part, part, head=h2)
                beside = send(part, part, head=h1)
                out.append((across, beside, i * n, n))
            return out

        def gather_forward(buf, started):
            out = []
            for across, _, lo, n in started:
                across.wait_recv()
                part = buf.at[h2, pl.ds(lo, n)]
                out.append(send(part, part, head=h1))
            return out

        c_tok.wait()
        ag_tok = gather_start(s.tok, 2)
        c_wout.wait()
        cut = E // 2
        half_wo = pl.ds(pl.multiple_of(lax.rem(bat, 2) * cut, cut), cut)
        part = s.wo.at[head, half_wo]
        wo_across = send(part, part, head=h2)
        wo_beside = send(s.wo.at[head], s.wo.at[head], head=h1)
        c_og.wait()
        ag_og = gather_start(s.og, 1)

        for c in small:
            c.wait()
        lane = lax.broadcasted_iota(jnp.int32, (1, LANES), 1)
        low = lane < DH
        ones_lanes = ((lane == DH) | (lane == DH + 1)).astype(F32)
        seg_all = seg_ref[...].astype(F32)
        first = seq == 0
        seg_half = jnp.where(first, seg_all[:, :T], seg_all[:, T : 2 * T])
        seg_prev = jnp.where(first, -1.0, seg_all[:, T - BLK : T])
        tail_one = jnp.where(first, -1.0, jnp.broadcast_to(seg_all[:, T - 1 : T], (1, LANES)))
        tail_two = jnp.where(
            first, -1.0, jnp.broadcast_to(seg_all[:, T - BLK - 1 : T - BLK], (1, LANES))
        )
        s.segrow[...] = jnp.broadcast_to(seg_half, (8, T))
        s.segcol[...] = jnp.transpose(jnp.broadcast_to(seg_half, (LANES, T)))
        segcol = s.segcol[...]
        row_id = lax.broadcasted_iota(jnp.int32, (T, LANES), 0)
        mask_two = ((segcol == segcol[T - BLK - 1 : T - BLK, :]) & (row_id < T - BLK)).astype(F32)
        prev_col = jnp.transpose(jnp.broadcast_to(seg_prev, (LANES, BLK)))
        s.mprev[...] = (prev_col == tail_one).astype(F32)
        link = (tail_one == tail_two).astype(F32)
        s.link[...] = jnp.broadcast_to(jnp.concatenate([link] * (M // LANES), axis=1), (8, M))
        s.m0[...] = mask_two
        s.mfar[...] = jnp.where(
            row_id < BLK, (segcol == tail_two).astype(F32), (segcol == tail_one).astype(F32)
        )
        nblk = pat_ref.shape[1]
        per_half = T // BLK
        hot = (
            lax.broadcasted_iota(jnp.int32, (T, nblk), 1)
            == lax.broadcasted_iota(jnp.int32, (T, nblk), 0) // BLK + seq * per_half
        ).astype(F32)
        pat = pat_ref[...].astype(F32)
        for h in range(H):
            s.thr[h] = 3.0 - nn(
                (hot * pat[h : h + 1, :]).astype(BF16), jnp.ones((nblk, LANES), BF16)
            )
        wrow = lax.broadcasted_iota(jnp.int32, (TILE, 2 * TILE), 0)
        wcol = lax.broadcasted_iota(jnp.int32, (TILE, 2 * TILE), 1)
        dist = 2 + wrow // BLK - wcol // BLK
        kind = jnp.where(
            dist >= 2,
            1.0,
            jnp.where(dist == 1, 2.0, jnp.where((dist == 0) & (wcol - TILE <= wrow), 3.0, 0.0)),
        )
        for t in range(nt_tiles):
            col = segcol[t * TILE : (t + 1) * TILE, :]
            for side in range(2):
                tile = t - 1 + side
                if tile < 0:
                    continue
                same = col == s.segrow[0:1, tile * TILE : (tile + 1) * TILE]
                s.code[t, :, side * TILE : (side + 1) * TILE] = jnp.where(
                    same, kind[:, side * TILE : (side + 1) * TILE], 0.0
                )
        scale = DH ** (-0.25)
        om = omega_ref[...] * scale
        om_high = om.astype(BF16)
        s.omst[0:DH, :] = om_high
        s.omst[DH : 2 * DH, :] = (om - om_high.astype(F32)).astype(BF16)
        s.omtmp[...] = jnp.zeros((LANES, M), F32)
        s.omtmp[0:DH, :] = om
        s.omtmp[DH : DH + 8, :] = (
            lax.broadcasted_iota(jnp.int32, (8, M), 0) == 0
        ).astype(F32)
        s.omt[...] = jnp.transpose(s.omtmp[...]).astype(BF16)
        c_wqkv.wait()
        for c in range(3):
            for h in range(H):
                src = s.wqkv[c * E + h * DH : c * E + (h + 1) * DH, :]
                base = (c * H + h) * LANES
                s.wpad[base : base + DH, :] = src
                s.wpad[base + DH : base + 2 * DH, :] = src if c < 2 else jnp.zeros_like(src)
        for h in range(H):
            s.wopad[h * LANES : h * LANES + DH, :] = s.wo[head, h * DH : (h + 1) * DH, :]
            s.wopad[h * LANES + DH : (h + 1) * LANES, :] = jnp.zeros((DH, D), BF16)
        for h in range(H):
            s.rin[h, STATE:LANES, :] = jnp.zeros((LANES - STATE, M), BF16)
            s.grin[h, STATE:LANES, :] = jnp.zeros((LANES - STATE, M), BF16)

        def features(twice):
            x = twice.astype(F32)
            square = jnp.sum(x * x, axis=-1, keepdims=True)
            projected = nn(twice, s.omst[...])
            return jnp.exp(projected - square * (scale * scale * 0.25)) * (1.0 / math.sqrt(M))

        gain1, bias1 = g1_ref[...].reshape(1, D), b1_ref[...].reshape(1, D)
        gain2, bias2 = g2_ref[...].reshape(1, D), b2_ref[...].reshape(1, D)

        def project(slot):
            xhat, _ = normalize(s.tok[slot].astype(F32))
            normed = (xhat * gain1 + bias1).astype(BF16)
            at = rows(slot)
            s.n1[at, :] = normed
            for c in range(3):
                out = nt(normed, s.wpad[c * H * LANES : (c + 1) * H * LANES, :])
                for h in range(H):
                    part = out[:, h * LANES : (h + 1) * LANES]
                    if c == 2:
                        s.v[h, at, :] = (part + ones_lanes).astype(BF16)
                    else:
                        low_part = part.astype(BF16)
                        (s.q, s.k)[c][h, at, :] = low_part
                        (s.fq, s.fk)[c][h, at, :] = features(low_part).astype(BF16)

        project(head)
        for _, beside, _, _ in ag_tok:
            beside.wait_recv()
        project(h1)
        fw_tok = gather_forward(s.tok, ag_tok)
        project(h2)
        for c in fw_tok:
            c.wait_recv()
        project(h3)

        for h in range(H):
            kk = s.k[h, T - BLK : T, :].astype(F32)
            vv = s.v[h, T - BLK : T, :].astype(F32)
            s.kvout[h] = jnp.where(low, kk, pltpu.roll(vv, DH, 1)).astype(BF16)
        ex_kv = send(s.kvout, s.kvin, seq=other)
        ex_r = []
        for h in range(H):
            v0 = (s.v[h].astype(F32) * s.m0[...]).astype(BF16)
            s.v0[h] = v0
            s.rout[h] = tn(v0, s.fk[h])[:STATE].astype(BF16)
            ex_r.append(send(s.rout.at[h], s.rin.at[h, pl.ds(0, STATE)], seq=other))

        wo_across.wait_recv()
        part = s.wo.at[h2, half_wo]
        wo_batch = send(part, part, batch=b1)

        def attend(h, carry):
            for t in range(nt_tiles):
                lo, hi = t * TILE, (t + 1) * TILE
                w0 = max(0, lo - TILE)
                fq = s.fq[h, lo:hi, :]
                low_rank = nt(fq, s.fk[h, 0:hi, :])
                exact = jnp.exp(nt(s.q[h, lo:hi, :], s.k[h, w0:hi, :]) * (0.5 / math.sqrt(DH)))
                tiles = (hi - w0) // TILE
                code = s.code[t, :, (2 - tiles) * TILE :]
                thr = jnp.concatenate([s.thr[h, lo:hi, :]] * tiles, axis=1)
                near = jnp.where(
                    code >= thr, exact, jnp.where(code >= 1.0, low_rank[:, w0:], 0.0)
                )
                if w0 > 0:
                    col = jnp.concatenate([s.segcol[lo:hi, :]] * (w0 // TILE), axis=1)
                    far = jnp.where(col == s.segrow[0:1, 0:w0], low_rank[:, :w0], 0.0)
                    near = jnp.concatenate([far, near], axis=1)
                w = near.astype(BF16)
                s.w[h, lo:hi, 0:hi] = w
                s.acc[h, lo:hi, :] = nn(w, s.v[h, 0:hi, :])
            return carry

        lax.fori_loop(0, H, attend, 0)

        if inner:
            for j in range(nh):
                lo = j * TILE
                s.n1t[:, lo : lo + TILE] = jnp.transpose(s.n1[lo : lo + TILE, :])

        ex_kv.wait_recv()

        def unpack(packed):
            x = packed.astype(F32)
            turned = pltpu.roll(x, DH, 1)
            twice = jnp.where(low, x, turned).astype(BF16)
            return twice, jnp.where(low, turned, 0.0)

        same_in = s.segcol[0:BLK, 0:BLK] == seg_prev
        for h in range(H):
            k_in, v_in = unpack(s.kvin[h])
            v_in = (v_in + ones_lanes).astype(BF16)
            f_in = features(k_in).astype(BF16)
            s.kin[h] = k_in
            s.vin[h] = v_in
            s.fin[h] = f_in
            q0 = s.q[h, 0:BLK, :]
            fq0 = s.fq[h, 0:BLK, :]
            exact = jnp.exp(nt(q0, k_in) * (0.5 / math.sqrt(DH)))
            low_rank = nt(fq0, f_in)
            use_exact = s.thr[h, 0:BLK, 0:BLK] < 2.5
            w_in = jnp.where(same_in, jnp.where(use_exact, exact, low_rank), 0.0).astype(BF16)
            s.win[h] = w_in
            s.acc[h, 0:BLK, :] = s.acc[h, 0:BLK, :] + nn(w_in, v_in)
            s.last[h] = tn((v_in.astype(F32) * s.mprev[...]).astype(BF16), f_in)
        for h in range(H):
            ex_r[h].wait_recv()
            state = s.rin[h]
            s.rlater[h] = (state.astype(F32) * s.link[0:1, :] + s.last[h]).astype(BF16)
            far0 = jnp.where(s.mfar[0:BLK, :] > 0.5, nt(s.fq[h, 0:BLK, :], state), 0.0)
            s.acc[h, 0:BLK, :] = s.acc[h, 0:BLK, :] + far0
            far1 = jnp.where(
                s.mfar[BLK:T, :] > 0.5, nt(s.fq[h, BLK:T, :], s.rlater[h]), 0.0
            )
            s.acc[h, BLK:T, :] = s.acc[h, BLK:T, :] + far1

        def divided(h, lo, hi):
            acc = s.acc[h, lo:hi, :]
            inv = 1.0 / acc[:, DH : DH + 1]
            return acc * inv, inv

        order = (0, 2, 1, 3)
        ag_at = {}
        for t in order:
            lo, hi = t * TILE, (t + 1) * TILE
            outs = [divided(h, lo, hi)[0] for h in range(H)]
            for h in range(0, H, 2):
                if h + 1 < H:
                    both = jnp.where(low, outs[h], pltpu.roll(outs[h + 1], DH, 1))
                    s.at[head, lo:hi, h * DH : (h + 2) * DH] = both.astype(BF16)
                else:
                    s.at[head, lo:hi, h * DH : (h + 1) * DH] = outs[h][:, :DH].astype(BF16)
            part = s.at.at[head, pl.ds(lo, TILE)]
            ag_at[t] = (send(part, part, head=h2), send(part, part, head=h1))
        wo_batch.wait_recv()
        fw_wo = send(s.wo.at[h2], s.wo.at[h2], head=h1)
        fw_og = gather_forward(s.og, ag_og)
        wo_beside.wait_recv()
        fw_wo.wait_recv()
        for _, c, _, _ in ag_og:
            c.wait_recv()
        for c in fw_og:
            c.wait_recv()
        c_wup.wait()
        c_wdown.wait()
        if inner:
            for j in range(nh):
                lo = j * TILE
                s.ogt[:, lo : lo + TILE] = jnp.transpose(s.og[j])
        fw_at = {}

        def forward_attended(t):
            ag_at[t][0].wait_recv()
            part = s.at.at[h2, pl.ds(t * TILE, TILE)]
            fw_at[t] = send(part, part, head=h1)

        def scatter_beside(make, bufs):
            bufs.out[0] = make(h3).astype(BF16)
            a = send(bufs.out.at[0], bufs.got.at[0], head=h1)
            bufs.mine[...] = make(h2)
            return a

        def scatter_across(bufs, a):
            a.wait_recv()
            bufs.out[1] = (bufs.mine[...] + bufs.got[0].astype(F32)).astype(BF16)
            return send(bufs.out.at[1], bufs.got.at[1], head=h2)

        def scatter_last(make, bufs):
            bufs.out[2] = make(h1).astype(BF16)
            return send(bufs.out.at[2], bufs.got.at[2], head=h1)

        def scatter_done(bufs, b, c):
            c.wait_recv()
            part = bufs.got[2].astype(F32)
            b.wait_recv()
            return part + bufs.got[1].astype(F32)

        def feed(slot):
            ag_at[slot][1].wait_recv()
            fw_at[slot].wait_recv()
            at = slice(slot * TILE, (slot + 1) * TILE)
            hid = s.tok[slot].astype(F32)
            for j in range(nh):
                hid = hid + nn(s.at[j, at, :], s.wo[j])
            s.hid[at, :] = hid
            xhat, _ = normalize(hid)
            normed = (xhat * gain2 + bias2).astype(BF16)
            s.n2[at, :] = normed
            act, slope = gelu_both(nn(normed, s.wup[...]))
            s.act[at, :] = act.astype(BF16)
            s.slope[at, :] = slope

        def feed_back(slot):
            at = slice(slot * TILE, (slot + 1) * TILE)
            slope = s.slope[at, :]
            gu = (nt(s.og[slot], s.wdown[...]) * slope).astype(BF16)
            s.gu[at, :] = gu
            s.ra.part[slot] = nt(gu, s.wup[...])

        core = lax.rem(head, 2)
        ra_a = {
            t: prepare(s.ra.out.at[t], s.ra.got.at[t], head=h1) for t in range(nh)
        }
        ra_b = prepare(s.ra.bout, s.ra.bgot, head=h2)

        def to_core(t):
            @pl.when(core != t % 2)
            def _():
                s.ra.out[t] = s.ra.part[t].astype(BF16)
                ra_a[t].start()

        def to_chip(t):
            @pl.when(h2 == t)
            def _():
                ra_a[t].wait_recv()
                s.ra.bout[...] = (s.ra.part[t] + s.ra.got[t].astype(F32)).astype(BF16)
                ra_b.start()

        forward_attended(order[0])
        for i, t in enumerate(order):
            if i + 1 < nh:
                forward_attended(order[i + 1])
            feed(t)

        b2 = lax.rem(bat + 2, nb)
        b3 = lax.rem(b1 + 2, nb)
        there = pl.ds(pl.multiple_of(other * half_rows, LANES), half_rows)
        here = pl.ds(pl.multiple_of(seq * half_rows, LANES), half_rows)

        def y_send(g):
            right = g.right()
            g.ys[...] = nn(g.left[there, :], right).astype(BF16)
            g.y = send(g.ys, g.yr, seq=other)
            g.own[...] = nn(g.left[here, :], right)

        def with_y(g, index):
            at = rows(index, piece)
            return g.own[at, :] + g.yr[at, :].astype(F32)

        def za_send(g):
            g.y.wait_recv()
            for i, index in enumerate((b1, b3)):
                g.zas[i] = with_y(g, index).astype(BF16)
            g.za = send(g.zas, g.zar, batch=b1)

        def zb_send(g):
            g.za.wait_recv()
            g.zbs[...] = (with_y(g, b2) + g.zar[1].astype(F32)).astype(BF16)
            g.zb = send(g.zbs, g.zbr, batch=b2)

        def weight_sum(g):
            total = with_y(g, bat) + g.zar[0].astype(F32)
            g.zb.wait_recv()
            return total + g.zbr[...].astype(F32)

        def zd_send(g):
            g.y.wait_recv()
            g.zd = []
            for i, index in enumerate((b2, b1, b3)):
                g.zds[i] = with_y(g, index).astype(BF16)
                g.zd.append(send(g.zds.at[i], g.zdr.at[i], batch=index))

        def weight_sum_direct(g):
            total = with_y(g, bat)
            for i in (1, 2, 0):
                g.zd[i].wait_recv()
                total = total + g.zdr[i].astype(F32)
            return total

        def both(index):
            return [rows(half * nb + index, piece) for half in range(ns)]

        def first_za(g):
            g.own[...] = nn(g.left[...], g.right())
            for i, index in enumerate((b1, b3)):
                for half, at in enumerate(both(index)):
                    g.zas[i, half] = g.own[at, :].astype(BF16)
            g.za = send(g.zas, g.zar, batch=b1)

        def first_zb(g):
            g.za.wait_recv()
            for half, at in enumerate(both(b2)):
                g.zbs[half] = (g.own[at, :] + g.zar[1, half].astype(F32)).astype(BF16)
            g.zb = send(g.zbs, g.zbr, batch=b2)

        def first_part(g, half):
            at = rows(half * nb + bat, piece)
            return g.own[at, :] + g.zar[0, half].astype(F32) + g.zbr[half].astype(F32)

        def first_y(g):
            g.zb.wait_recv()
            g.ys[...] = first_part(g, other).astype(BF16)
            g.y = send(g.ys, g.yr, seq=other)

        def first_sum(g):
            total = first_part(g, seq)
            g.y.wait_recv()
            return total + g.yr[...].astype(F32)

        def collect(g):
            if hasattr(g, "zdr"):
                return weight_sum_direct(g)
            return weight_sum(g) if g.zbs.shape[0] == piece else first_sum(g)

        def chunks(groups, left, ref):
            width = ref.shape[-1] // len(groups)
            for i, g in enumerate(groups):
                g.left = left
                g.right = lambda i=i: ref[:, i * width : (i + 1) * width]

        steps = {}
        if inner:
            downs, ups, qkvs = (s.d0, s.d1), (s.u0, s.u1), (s.x0, s.x1, s.x2)
            chunks(downs, s.ogt, s.act)
            chunks(ups, s.n2t, s.gu)
            chunks((s.o0,), s.gbt, s.at.at[head])
            chunks(qkvs, s.n1t, s.gqkv)
            steps = {
                0: [(first_za, s.d0), (y_send, s.d1)],
                5: [(first_za, s.u1), (y_send, s.u0)],
                8: [(first_zb, s.d0)],
                9: [(za_send, s.d1)],
                15: [(first_zb, s.u1)],
                17: [(y_send, s.o0)],
                18: [(za_send, s.u0)],
                19: [(y_send, s.x1)],
                20: [(y_send, s.x0)],
                22: [(za_send, s.o0)],
                24: [(zb_send, s.d1)],
                25: [(y_send, s.x2)],
                27: [(za_send, s.x1)],
                28: [(zb_send, s.u0)],
                31: [(za_send, s.x0), (zb_send, s.x1)],
                32: [(zb_send, s.o0)],
                33: [(za_send, s.x2), (first_y, s.u1)],
                34: [(first_y, s.d0)],
                35: [(zb_send, s.x0)],
                37: [(zb_send, s.x2)],
            }

        def run(*numbers):
            for number in numbers:
                for step, group in steps.get(number, ()):
                    step(group)

        run(0)
        for i, t in enumerate(order):
            feed_back(t)
            to_core(t)
            if i > 0:
                to_chip(order[i - 1])
        to_chip(order[-1])
        run(1)
        for t in range(nh):

            @pl.when(head == t)
            def _():
                ra_a[t].wait_recv()

        ra_b.wait_recv()
        run(2)
        grad2 = s.ra.part[head] + s.ra.got[head].astype(F32) + s.ra.bgot[...].astype(F32)
        mine = rows(head)
        xhat2, rstd2 = normalize(s.hid[mine, :])
        s.ns[...] = jnp.zeros_like(s.ns)
        s.ns[2:3, :] = jnp.sum(grad2 * xhat2, axis=0, keepdims=True)
        s.ns[3:4, :] = jnp.sum(grad2, axis=0, keepdims=True)
        grad_hidden = s.og[head].astype(F32) + norm_back(grad2, gain2, xhat2, rstd2)
        s.gh[...] = grad_hidden
        s.gb[head] = grad_hidden.astype(BF16)
        run(3)
        ag_gb = gather_start(s.gb, 2)
        run(4)
        if inner:
            for j in range(nh):
                lo = j * TILE
                s.n2t[:, lo : lo + TILE] = jnp.transpose(s.n2[lo : lo + TILE, :])
        run(5, 6)

        def lower(slot):
            return nn(s.act[rows(slot), :], s.wdown[...])

        rc_a = scatter_beside(lower, s.rc)
        rc_c = scatter_last(lower, s.rc)
        run(7)

        def divide_back(slot):
            at = rows(slot)
            ga = nt(s.gb[slot], s.wopad[...])
            for h in range(H):
                acc = s.acc[h, at, :]
                inv = 1.0 / acc[:, DH : DH + 1]
                gnum = ga[:, h * LANES : (h + 1) * LANES] * inv
                gden = -jnp.sum(gnum * acc, axis=-1, keepdims=True) * inv
                high = gden.astype(BF16).astype(F32)
                gnum = jnp.where(lane == DH, high, jnp.where(lane == DH + 1, gden - high, gnum))
                s.gn[h, at, :] = gnum.astype(BF16)

        divide_back(head)
        for _, c, _, _ in ag_gb:
            c.wait_recv()
        divide_back(h1)
        run(8)
        fw_gb = gather_forward(s.gb, ag_gb)
        divide_back(h2)
        for c in fw_gb:
            c.wait_recv()
        run(9)
        divide_back(h3)
        run(10)

        def feature_back(gfeat, feat, twice):
            x = nn((gfeat * feat.astype(F32)).astype(BF16), s.omt[...])
            return x - twice.astype(F32) * (x[:, DH : DH + 1] * (scale * scale))

        for h in range(H):
            gm = jnp.where(s.mfar[...] > 0.5, s.gn[h].astype(F32), 0.0).astype(BF16)
            s.gm[h] = gm
            glater = tn(gm[BLK:T, :], s.fq[h, BLK:T, :])
            gstate = tn(gm[0:BLK, :], s.fq[h, 0:BLK, :]) + glater * s.link[0:1, :]
            s.grout[h] = gstate[:STATE].astype(BF16)
            glater = glater.astype(BF16)
            v_last = (s.vin[h].astype(F32) * s.mprev[...]).astype(BF16)
            gn0 = s.gn[h, 0:BLK, :]
            q0 = s.q[h, 0:BLK, :]
            fq0 = s.fq[h, 0:BLK, :]
            gw = nt(gn0, s.vin[h])
            w_in = s.win[h]
            use_exact = s.thr[h, 0:BLK, 0:BLK] < 2.5
            gs = jnp.where(
                same_in & use_exact, gw * w_in.astype(F32) * (1.0 / math.sqrt(DH)), 0.0
            ).astype(BF16)
            gp = jnp.where(same_in & jnp.logical_not(use_exact), gw, 0.0).astype(BF16)
            gfeat = tn(gp, fq0) + nn(v_last, glater)
            gk = feature_back(gfeat, s.fin[h], s.kin[h]) + tn(gs, q0)
            gv = tn(w_in, gn0) + s.mprev[...] * nt(s.fin[h], glater)
            s.gkvout[h] = jnp.where(low, gk, pltpu.roll(gv, DH, 1)).astype(BF16)
            s.gfq0[h] = nn(gp, s.fin[h])
            s.gq0[h] = nn(gs, s.kin[h])
        run(11)
        ex_gkv = send(s.gkvout, s.gkvin, seq=other)
        ex_gr = send(s.grout, s.grin.at[:, pl.ds(0, STATE)], seq=other)

        run(12)
        rc_b = scatter_across(s.rc, rc_a)
        run(13)

        def attend_back(h):
            for t in range(nt_tiles):
                lo, hi = t * TILE, (t + 1) * TILE
                w0 = max(0, lo - TILE)
                tiles = (hi - w0) // TILE
                gw = nt(s.gn[h, lo:hi, :], s.v[h, 0:hi, :])
                code = s.code[t, :, (2 - tiles) * TILE :]
                thr = jnp.concatenate([s.thr[h, lo:hi, :]] * tiles, axis=1)
                use_exact = code >= thr
                near = gw[:, w0:]
                gs = jnp.where(
                    use_exact,
                    near * s.w[h, lo:hi, w0:hi].astype(F32) * (1.0 / math.sqrt(DH)),
                    0.0,
                ).astype(BF16)
                gp = jnp.where((code >= 1.0) & (code < thr), near, 0.0)
                if w0 > 0:
                    col = jnp.concatenate([s.segcol[lo:hi, :]] * (w0 // TILE), axis=1)
                    far = jnp.where(col == s.segrow[0:1, 0:w0], gw[:, :w0], 0.0)
                    gp = jnp.concatenate([far, gp], axis=1)
                gp = gp.astype(BF16)
                s.gp[lo:hi, 0:hi] = gp
                s.gs[lo:hi, (2 - tiles) * TILE :] = gs
                gfq = nn(gp, s.fk[h, 0:hi, :])
                gq = nn(gs, s.k[h, w0:hi, :])
                gm = s.gm[h, lo:hi, :]
                if t == 0:
                    top = nn(gm[0:BLK], s.rin[h]) + s.gfq0[h]
                    bottom = nn(gm[BLK:], s.rlater[h])
                    gfq = gfq + jnp.concatenate([top, bottom], axis=0)
                    gq = gq + jnp.concatenate(
                        [s.gq0[h], jnp.zeros((TILE - BLK, LANES), F32)], axis=0
                    )
                else:
                    gfq = gfq + nn(gm, s.rlater[h])
                gq = gq + feature_back(gfq, s.fq[h, lo:hi, :], s.q[h, lo:hi, :])
                s.gq[h, lo:hi, :] = gq
            for t in range(nt_tiles):
                lo, hi = t * TILE, (t + 1) * TILE
                s.gfk[h, lo:hi, :] = tn(s.gp[lo:T, lo:hi], s.fq[h, lo:T, :])
                s.gv[h, lo:hi, :] = tn(s.w[h, lo:T, lo:hi], s.gn[h, lo:T, :])
                gk = tn(s.gs[lo:hi, TILE:], s.q[h, lo:hi, :])
                if t + 1 < nt_tiles:
                    gk = gk + tn(s.gs[hi : hi + TILE, :TILE], s.q[h, hi : hi + TILE, :])
                s.gk[h, lo:hi, :] = gk

        for h in range(H):
            attend_back(h)
            run(14 + min(h, 2))
        if inner:
            for j in range(nh):
                lo = j * TILE
                s.gbt[:, lo : lo + TILE] = jnp.transpose(s.gb[j])
        run(17)

        if inner:
            width = D // (ns * nb * nh)
            start = ((seq * nb + bat) * nh + head) * width
            s.pick[...] = (
                lax.broadcasted_iota(jnp.int32, (D, LANES), 0)
                == lax.broadcasted_iota(jnp.int32, (D, LANES), 1) + start
            ).astype(F32)

        ex_gkv.wait_recv()
        ex_gr.wait_recv()
        run(18)

        def finish(h, carry):
            state = jnp.where(first, s.grin[h].astype(F32), 0.0).astype(BF16)
            gfk = s.gfk[h] + nn(s.v0[h], state)
            fk = s.fk[h]
            gv = s.gv[h] + s.m0[...] * nt(fk, state)
            gk = s.gk[h] + feature_back(gfk, fk, s.k[h])
            s.gk[h] = gk
            s.gv[h] = gv
            back = jnp.where(first, s.gkvin[h].astype(F32), 0.0)
            s.gk[h, T - BLK : T, :] = s.gk[h, T - BLK : T, :] + back
            s.gv[h, T - BLK : T, :] = s.gv[h, T - BLK : T, :] + pltpu.roll(back, DH, 1)
            return carry

        lax.fori_loop(0, H, finish, 0)
        parts = [(n, h) for n in (s.gq, s.gk, s.gv) for h in range(H)]
        for i in range(0, len(parts), 2):
            (na, ha) = parts[i]
            a = na[ha]
            if i + 1 < len(parts):
                (nb_, hb) = parts[i + 1]
                a = jnp.where(low, a, pltpu.roll(nb_[hb], DH, 1))
                s.gqkv[:, i * DH : (i + 2) * DH] = a.astype(BF16)
            else:
                s.gqkv[:, i * DH : (i + 1) * DH] = a[:, :DH].astype(BF16)

        run(19)

        def first_grad(slot):
            return nn(s.gqkv[rows(slot), :], s.wqkv[...])

        rb_a = scatter_beside(first_grad, s.rb)
        run(20)
        rb_b = scatter_across(s.rb, rb_a)
        run(21, 22, 23, 24)
        rb_c = scatter_last(first_grad, s.rb)
        run(25)
        own = first_grad(head)
        run(26)
        own_mixed = s.hid[mine, :] + lower(head)

        run(27, 28)
        grad1 = own + scatter_done(s.rb, rb_b, rb_c)
        run(29)
        xhat1, rstd1 = normalize(s.tok[head].astype(F32))
        s.ns[0:1, :] = jnp.sum(grad1 * xhat1, axis=0, keepdims=True)
        s.ns[1:2, :] = jnp.sum(grad1, axis=0, keepdims=True)
        s.gh[...] = s.gh[...] + norm_back(grad1, gain1, xhat1, rstd1)

        if inner:
            run(30)
            n_h = [send(s.ns, s.nh.at[i], head=d) for i, d in enumerate((h1, h2, h3))]
            run(31)
            total = s.ns[...]
            for i, c in enumerate(n_h):
                c.wait_recv()
                total = total + s.nh[i]
            s.ns2[...] = total
            run(32)
            n_y = send(s.ns2, s.ny, seq=other)
            run(33)
        write(s.gh, gtok_ref.at[0])
        s.omixed[...] = (own_mixed + scatter_done(s.rc, rc_b, rc_c)).astype(BF16)
        write(s.omixed, mixed_ref.at[0])
        if inner:
            run(34)
            n_y.wait_recv()
            run(35)
            s.ns3[...] = s.ns2[...] + s.ny[...]
            n_z = [
                send(s.ns3, s.nz.at[d - 1], batch=lax.rem(bat + d, nb)) for d in range(1, nb)
            ]
            run(36, 37)
            wide = FL // 2
            for out, groups, ref in ((s.odown, downs, odown_ref), (s.oup, ups, oup_ref)):
                for i, g in enumerate(groups):
                    out[:, i * wide : (i + 1) * wide] = collect(g)
                write(out, ref)
            s.otmp[...] = jnp.zeros_like(s.otmp)
            s.otmp[0:piece, 0:E] = collect(s.o0)
            s.oout[...] = jnp.transpose(s.otmp[...])[:E, :piece]
            write(s.oout, oout_ref)
            total = s.ns3[...]
            for i, c in enumerate(n_z):
                c.wait_recv()
                total = total + s.nz[i]
            s.onorm[...] = lax.dot_general(
                total, s.pick[...], (((1,), (0,)), ((), ())),
                precision=lax.Precision.HIGHEST, preferred_element_type=F32,
            )
            write(s.onorm, norm_ref)
            for i, g in enumerate(qkvs):
                s.oqkv[i] = collect(g)
                write(s.oqkv.at[i], oqkv_ref.at[i])
        else:

            def joined(ref):
                return jnp.concatenate([ref[j] for j in range(nh)], axis=0)

            write(s.ns, norm_ref)
            s.odown[...] = tn(joined(s.og), s.act[...])
            write(s.odown, odown_ref)
            s.oup[...] = tn(s.n2[...], s.gu[...])
            write(s.oup, oup_ref)
            s.oout[...] = tn(joined(s.gb), s.at[head])
            write(s.oout, oout_ref)
            s.oqkv[...] = tn(s.n1[...], s.gqkv[...])
            write(s.oqkv, oqkv_ref)
        for c in written:
            c.wait()
        for t in range(nh):

            @pl.when(core != t % 2)
            def _():
                ra_a[t].wait_send()

        ra_b.wait_send()
        for c in sends:
            c.wait_send()

    return kernel


def build(dims):
    nh, ns, nb, T, R, D, E, FL, H, M, inner = dims
    plan = Plan()
    piece = D // (ns * nb)
    half = D // ns
    blocks = ns * T // BLK
    plan.add(
        seg=((1, ns * T), jnp.int32),
        pat=((H, blocks), jnp.int32),
        omega=((DH, M), F32),
        g1=((D,), F32),
        b1=((D,), F32),
        g2=((D,), F32),
        b2=((D,), F32),
        tok=((nh, R, D), BF16),
        og=((nh, R, D), BF16),
        wqkv=((3 * E, D), BF16),
        wo=((nh, E, D), BF16),
        wup=((D, FL), BF16),
        wdown=((FL, D), BF16),
        wpad=((3 * H * LANES, D), BF16),
        wopad=((H * LANES, D), BF16),
        segrow=((8, T), F32),
        segcol=((T, LANES), F32),
        m0=((T, LANES), F32),
        mprev=((BLK, LANES), F32),
        link=((8, M), F32),
        mfar=((T, LANES), F32),
        thr=((H, T, LANES), F32),
        code=((T // TILE, TILE, 2 * TILE), F32),
        omst=((2 * DH, M), BF16),
        omtmp=((LANES, M), F32),
        omt=((M, LANES), BF16),
        n1=((T, D), BF16),
        q=((H, T, LANES), BF16),
        k=((H, T, LANES), BF16),
        v=((H, T, LANES), BF16),
        v0=((H, T, LANES), BF16),
        gn=((H, T, LANES), BF16),
        gm=((H, T, LANES), BF16),
        fq=((H, T, M), BF16),
        fk=((H, T, M), BF16),
        rout=((H, STATE, M), BF16),
        grout=((H, STATE, M), BF16),
        rin=((H, LANES, M), BF16),
        grin=((H, LANES, M), BF16),
        rlater=((H, LANES, M), BF16),
        last=((H, LANES, M), F32),
        kvout=((H, BLK, LANES), BF16),
        kvin=((H, BLK, LANES), BF16),
        gkvout=((H, BLK, LANES), BF16),
        gkvin=((H, BLK, LANES), BF16),
        kin=((H, BLK, LANES), BF16),
        vin=((H, BLK, LANES), BF16),
        fin=((H, BLK, M), BF16),
        win=((H, BLK, BLK), BF16),
        gfq0=((H, BLK, M), F32),
        gq0=((H, BLK, LANES), F32),
        w=((H, T, T), BF16),
        acc=((H, T, LANES), F32),
        at=((nh, T, E), BF16),
        hid=((T, D), F32),
        slope=((T, FL), F32),
        n2=((T, D), BF16),
        act=((T, FL), BF16),
        gu=((T, FL), BF16),
        gh=((R, D), F32),
        gb=((nh, R, D), BF16),
        gp=((T, T), BF16),
        gs=((T, 2 * TILE), BF16),
        gfk=((H, T, M), F32),
        gq=((H, T, LANES), F32),
        gk=((H, T, LANES), F32),
        gv=((H, T, LANES), F32),
        gqkv=((T, 3 * E), BF16),
        ns=((8, D), F32),
    )
    pair = dict(out=((3, R, D), BF16), got=((3, R, D), BF16), mine=((R, D), F32))
    plan.group(rb=pair, rc=pair)
    plan.group(
        ra=dict(
            part=((nh, R, D), F32),
            out=((nh, R, D), BF16),
            got=((nh, R, D), BF16),
            bout=((R, D), BF16),
            bgot=((R, D), BF16),
        )
    )
    if inner:

        def weight(width):
            return dict(
                ys=((half, width), BF16),
                yr=((half, width), BF16),
                own=((half, width), F32),
                zas=((2, piece, width), BF16),
                zar=((2, piece, width), BF16),
                zbs=((piece, width), BF16),
                zbr=((piece, width), BF16),
            )

        def weight_direct(width):
            return dict(
                ys=((half, width), BF16),
                yr=((half, width), BF16),
                own=((half, width), F32),
                zds=((nb - 1, piece, width), BF16),
                zdr=((nb - 1, piece, width), BF16),
            )

        def weight_first(width):
            return dict(
                own=((D, width), F32),
                zas=((2, ns, piece, width), BF16),
                zar=((2, ns, piece, width), BF16),
                zbs=((ns, piece, width), BF16),
                zbr=((ns, piece, width), BF16),
                ys=((piece, width), BF16),
                yr=((piece, width), BF16),
            )

        wide, narrow = FL // 2, E
        plan.group(
            d0=weight_first(wide),
            d1=weight(wide),
            u0=weight(wide),
            u1=weight_first(wide),
            o0=weight(narrow),
            x0=weight(narrow),
            x1=weight(narrow),
            x2=weight(narrow),
        )
        turned = ((D, T), BF16)
        plan.add(
            odown=((piece, FL), F32),
            oup=((piece, FL), F32),
            oout=((E, piece), F32),
            oqkv=((3, piece, E), F32),
            onorm=((8, LANES), F32),
            pick=((D, LANES), F32),
        )
        plan.add(n1t=turned, n2t=turned, ogt=turned, gbt=turned)
        plan.add(
            ns2=((8, D), F32),
            ns3=((8, D), F32),
            nz=((nb - 1, 8, D), F32),
            ny=((8, D), F32),
            nh=((3, 8, D), F32),
            otmp=((LANES, 2 * LANES), F32),
        )
    else:
        plan.add(
            odown=((D, FL), F32), oup=((D, FL), F32), oout=((D, E), F32), oqkv=((D, 3 * E), F32)
        )
    plan.add(omixed=((R, D), BF16))
    plan.semaphores(ssem=96, rsem=96, lsem=32)

    if inner:
        grads = [(3, piece, E), (E, piece), (piece, FL), (piece, FL)]
        norm = (8, LANES)
    else:
        grads = [(D, 3 * E), (D, E), (D, FL), (D, FL)]
        norm = (8, D)
    outs = [((1, R, D), BF16), ((1, R, D), F32), (norm, F32)] + [(g, F32) for g in grads]
    hbm = pl.BlockSpec(memory_space=pltpu.HBM)
    in_specs = [hbm] * 13
    kind, space = (pltpu.VMEM, pltpu.VMEM) if inner else (jax.ShapeDtypeStruct, pltpu.HBM)
    kernel = make_kernel(dims, len(in_specs), len(outs), plan)
    return pl.pallas_call(
        kernel,
        out_shape=[kind(shape, dtype) for shape, dtype in outs],
        in_specs=in_specs,
        out_specs=[pl.BlockSpec(memory_space=space)] * len(outs),
        scratch_shapes=plan.shapes,
        compiler_params=pltpu.CompilerParams(
            collective_id=0, has_side_effects=True, vmem_limit_bytes=(54 if inner else 60) << 20
        ),
        name="block",
    )


def hand_over(width, *arrays):
    count = len(arrays) - 1

    def kernel(*refs):
        ins, norm_ref = refs[:count], refs[count]
        outs, norm_outs = refs[count + 1 : 2 * count + 1], refs[2 * count + 1 :]
        for a, b in zip(ins, outs):
            b[...] = a[...]
        for i, out in enumerate(norm_outs):
            out[...] = norm_ref[i, :width]

    vmem = pl.BlockSpec(memory_space=pltpu.VMEM)
    return pl.pallas_call(
        kernel,
        out_shape=[jax.ShapeDtypeStruct(a.shape, a.dtype) for a in arrays[:-1]]
        + [jax.ShapeDtypeStruct((width,), F32)] * 4,
        in_specs=[vmem] * len(arrays),
        out_specs=[vmem] * (count + 4),
        compiler_params=pltpu.CompilerParams(vmem_limit_bytes=6 << 20),
        name="hand_over",
    )(*arrays)


def per_device(
    mesh_shape,
    tokens,
    seg_ids,
    pattern,
    omega,
    norm1_gain,
    norm1_bias,
    w_qkv,
    w_out,
    norm2_gain,
    norm2_bias,
    w_up,
    w_down,
    out_grad,
):
    nh, ns, nb = mesh_shape
    rows, D = tokens.shape[1:]
    T = seg_ids.shape[1] // ns
    E = w_qkv.shape[2]
    FL = w_up.shape[1]
    piece = D // (ns * nb)
    inner = piece % 16 == 0 and nb == 4
    dims = (nh, ns, nb, T, rows, D, E, FL, E // DH, omega.shape[1], inner)
    w_flat = jnp.transpose(w_qkv, (1, 2, 0)).reshape(3 * E, D)
    arrays = (
        tokens, seg_ids, pattern, omega, norm1_gain, norm1_bias, w_flat, w_out,
        norm2_gain, norm2_bias, w_up, w_down, out_grad,
    )
    arrays = [pltpu.with_memory_space_constraint(a, pltpu.HBM) for a in arrays]
    mixed, grad_tokens, norms, g_qkv, g_out, g_up, g_down = build(dims)(*arrays)
    if inner:
        width = D // (ns * nb * nh)
        mixed, grad_tokens, g_qkv, g_out, g_up, g_down, *norms = hand_over(
            width, mixed, grad_tokens, g_qkv, g_out, g_up, g_down, norms
        )
        g_qkv = jnp.transpose(g_qkv, (1, 0, 2))
        g_down = g_down.T
    else:
        group = ("seq", "batch")
        scatter = functools.partial(lax.psum_scatter, scatter_dimension=0, tiled=True)
        norms = lax.psum_scatter(
            norms[:4], ("seq", "batch", "head"), scatter_dimension=1, tiled=True
        )
        g_qkv = scatter(g_qkv, group).reshape(piece, 3, E)
        g_out = scatter(g_out, group).T
        g_up = scatter(g_up, group)
        g_down = scatter(g_down, group).T
    return (
        mixed, grad_tokens, norms[0], norms[1], g_qkv, g_out, norms[2], norms[3], g_up, g_down,
    )


def solution(mesh):
    placed = (
        P("batch", ("seq", "head"), None),
        P("batch", None),
        P("head", None),
        P(),
        P(),
        P(),
        P(None, None, "head"),
        P("head", None),
        P(),
        P(),
        P(None, "head"),
        P("head", None),
        P("batch", ("seq", "head"), None),
    )
    shape = (mesh.shape["head"], mesh.shape["seq"], mesh.shape["batch"])
    return jax.shard_map(
        functools.partial(per_device, shape),
        mesh=mesh,
        in_specs=placed,
        out_specs=(
            P("batch", ("seq", "head"), None),
            P("batch", ("seq", "head"), None),
            P(("seq", "batch", "head")),
            P(("seq", "batch", "head")),
            P(("seq", "batch"), None, "head"),
            P("head", ("seq", "batch")),
            P(("seq", "batch", "head")),
            P(("seq", "batch", "head")),
            P(("seq", "batch"), "head"),
            P("head", ("seq", "batch")),
        ),
        check_vma=False,
    )
```

```python
import functools
import math
from types import SimpleNamespace

import jax
import jax.numpy as jnp
from jax import lax
from jax.experimental import pallas as pl
from jax.experimental.pallas import tpu as pltpu
from jax.sharding import PartitionSpec as P

DH = 64
BLK = 64
LANES = 128
TILE = 128
STATE = 80
F32 = jnp.float32
BF16 = jnp.bfloat16
MESH = pl.DeviceIdType.MESH


def nn(a, b):
    return lax.dot_general(a, b, (((1,), (0,)), ((), ())), preferred_element_type=F32)


def nt(a, b):
    return lax.dot_general(a, b, (((1,), (1,)), ((), ())), preferred_element_type=F32)


def tn(a, b):
    return lax.dot_general(a, b, (((0,), (0,)), ((), ())), preferred_element_type=F32)


def normalize(x):
    center = x - jnp.mean(x, axis=-1, keepdims=True)
    rstd = lax.rsqrt(jnp.mean(center * center, axis=-1, keepdims=True) + 1e-05)
    return center * rstd, rstd


def norm_back(grad, gain, xhat, rstd):
    g = grad * gain
    return rstd * (
        g - jnp.mean(g, axis=-1, keepdims=True) - xhat * jnp.mean(g * xhat, axis=-1, keepdims=True)
    )


def gelu_both(u):
    k0 = math.sqrt(2.0 / math.pi)
    u2 = u * u
    th = jnp.tanh(k0 * (u + 0.044715 * u2 * u))
    half = 0.5 * (1.0 + th)
    slope = half + 0.5 * u * (1.0 - th * th) * (k0 * (1.0 + 3.0 * 0.044715 * u2))
    return u * half, slope


class Plan:
    def __init__(self):
        self.shapes = []
        self.tree = {}

    def add(self, into=None, **buffers):
        into = self.tree if into is None else into
        for name, (shape, dtype) in buffers.items():
            into[name] = len(self.shapes)
            self.shapes.append(pltpu.VMEM(shape, dtype))

    def group(self, **groups):
        for name, buffers in groups.items():
            self.tree[name] = {}
            self.add(self.tree[name], **buffers)

    def semaphores(self, **counts):
        for name, n in counts.items():
            self.tree[name] = len(self.shapes)
            self.shapes.append(pltpu.SemaphoreType.DMA((n,)))

    def bind(self, refs):
        def walk(tree):
            return SimpleNamespace(
                **{k: walk(v) if isinstance(v, dict) else refs[v] for k, v in tree.items()}
            )

        return walk(self.tree)


def make_kernel(dims, n_in, n_out, plan):
    nh, ns, nb, T, R, D, E, FL, H, M, inner = dims
    nt_tiles = T // TILE
    half_rows = D // ns
    piece = D // (ns * nb)

    def kernel(*refs):
        (
            tok_hbm, seg_hbm, pat_hbm, omega_hbm, g1_hbm, b1_hbm, wqkv_hbm, wout_hbm,
            g2_hbm, b2_hbm, wup_hbm, wdown_hbm, og_hbm,
        ) = refs[:n_in]
        (
            mixed_ref, gtok_ref, norm_ref, oqkv_ref, oout_ref, oup_ref, odown_ref,
        ) = refs[n_in : n_in + n_out]
        s = plan.bind(refs[n_in + n_out :])
        seg_ref, pat_ref, omega_ref = s.seg, s.pat, s.omega
        g1_ref, b1_ref, g2_ref, b2_ref = s.g1, s.b1, s.g2, s.b2
        ssem, rsem, lsem = s.ssem, s.rsem, s.lsem
        used = {"r": 0, "l": 0}
        sends = []

        head = lax.axis_index("head")
        seq = lax.axis_index("seq")
        bat = lax.axis_index("batch")
        h1 = head + 1 - 2 * lax.rem(head, 2)
        h2 = lax.rem(head + 2, nh)
        h3 = lax.rem(h1 + 2, nh)
        other = 1 - seq

        def local(src, dst):
            k = used["l"]
            used["l"] += 1
            c = pltpu.make_async_copy(src, dst, lsem.at[k])
            c.start()
            return c

        written = []

        def write(src, dst):
            if not inner:
                written.append(local(src, dst))

        s.ogtok = s.gh
        if inner:
            s.odown, s.oup, s.oout, s.oqkv = odown_ref, oup_ref, oout_ref, oqkv_ref
            s.onorm, s.omixed, s.ogtok = norm_ref, mixed_ref.at[0], gtok_ref.at[0]

        def send(src, dst, **dev):
            k = used["r"]
            used["r"] += 1
            c = pltpu.make_async_remote_copy(
                src_ref=src, dst_ref=dst, send_sem=ssem.at[k], recv_sem=rsem.at[k],
                device_id=dev, device_id_type=MESH,
            )
            c.start()
            sends.append(c)
            return c

        def prepare(src, dst, **dev):
            k = used["r"]
            used["r"] += 1
            return pltpu.make_async_remote_copy(
                src_ref=src, dst_ref=dst, send_sem=ssem.at[k], recv_sem=rsem.at[k],
                device_id=dev, device_id_type=MESH,
            )

        def rows(slot, n=TILE):
            return pl.ds(pl.multiple_of(slot * n, n), n)

        b1 = bat + 1 - 2 * lax.rem(bat, 2)
        barrier = pltpu.get_barrier_semaphore()
        peers = [dict(head=h1), dict(head=h2), dict(head=h3), dict(seq=other)]
        if inner:
            peers += [dict(batch=lax.rem(bat + d, nb)) for d in range(1, nb)]
        else:
            peers += [dict(batch=b1)]
        for dev in peers:
            pl.semaphore_signal(barrier, inc=1, device_id=dev, device_id_type=MESH)
        c_tok = local(tok_hbm.at[0], s.tok.at[head])
        c_wout = local(wout_hbm, s.wo.at[head])
        c_og = local(og_hbm.at[0], s.og.at[head])
        c_wqkv = local(wqkv_hbm, s.wqkv)
        small = [
            local(a, b)
            for a, b in (
                (seg_hbm, seg_ref), (pat_hbm, pat_ref), (omega_hbm, omega_ref),
                (g1_hbm, g1_ref), (b1_hbm, b1_ref), (g2_hbm, g2_ref), (b2_hbm, b2_ref),
            )
        ]
        c_wup = local(wup_hbm, s.wup)
        c_wdown = local(wdown_hbm, s.wdown)
        pl.semaphore_wait(barrier, len(peers))

        def gather_start(buf, chunks):
            n = buf.shape[1] // chunks
            out = []
            for i in range(chunks):
                part = buf.at[head, pl.ds(i * n, n)]
                across = send(part, part, head=h2)
                beside = send(part, part, head=h1)
                out.append((across, beside, i * n, n))
            return out

        def gather_forward(buf, started):
            out = []
            for across, _, lo, n in started:
                across.wait_recv()
                part = buf.at[h2, pl.ds(lo, n)]
                out.append(send(part, part, head=h1))
            return out

        c_tok.wait()
        ag_tok = gather_start(s.tok, 2)
        c_wout.wait()
        cut = E // 2
        half_wo = pl.ds(pl.multiple_of(lax.rem(bat, 2) * cut, cut), cut)
        part = s.wo.at[head, half_wo]
        wo_across = send(part, part, head=h2)
        wo_beside = send(s.wo.at[head], s.wo.at[head], head=h1)
        c_og.wait()
        ag_og = gather_start(s.og, 1)

        for c in small:
            c.wait()
        lane = lax.broadcasted_iota(jnp.int32, (1, LANES), 1)
        low = lane < DH
        ones_lanes = ((lane == DH) | (lane == DH + 1)).astype(F32)
        seg_all = seg_ref[...].astype(F32)
        first = seq == 0
        seg_half = jnp.where(first, seg_all[:, :T], seg_all[:, T : 2 * T])
        seg_prev = jnp.where(first, -1.0, seg_all[:, T - BLK : T])
        tail_one = jnp.where(first, -1.0, jnp.broadcast_to(seg_all[:, T - 1 : T], (1, LANES)))
        tail_two = jnp.where(
            first, -1.0, jnp.broadcast_to(seg_all[:, T - BLK - 1 : T - BLK], (1, LANES))
        )
        s.segrow[...] = jnp.broadcast_to(seg_half, (8, T))
        s.segcol[...] = jnp.transpose(jnp.broadcast_to(seg_half, (LANES, T)))
        segcol = s.segcol[...]
        row_id = lax.broadcasted_iota(jnp.int32, (T, LANES), 0)
        mask_two = ((segcol == segcol[T - BLK - 1 : T - BLK, :]) & (row_id < T - BLK)).astype(F32)
        prev_col = jnp.transpose(jnp.broadcast_to(seg_prev, (LANES, BLK)))
        s.mprev[...] = (prev_col == tail_one).astype(F32)
        link = (tail_one == tail_two).astype(F32)
        s.link[...] = jnp.broadcast_to(jnp.concatenate([link] * (M // LANES), axis=1), (8, M))
        s.m0[...] = mask_two
        s.mfar[...] = jnp.where(
            row_id < BLK, (segcol == tail_two).astype(F32), (segcol == tail_one).astype(F32)
        )
        nblk = pat_ref.shape[1]
        per_half = T // BLK
        hot = (
            lax.broadcasted_iota(jnp.int32, (T, nblk), 1)
            == lax.broadcasted_iota(jnp.int32, (T, nblk), 0) // BLK + seq * per_half
        ).astype(F32)
        pat = pat_ref[...].astype(F32)
        for h in range(H):
            s.thr[h] = 3.0 - nn(
                (hot * pat[h : h + 1, :]).astype(BF16), jnp.ones((nblk, LANES), BF16)
            )
        wrow = lax.broadcasted_iota(jnp.int32, (TILE, 2 * TILE), 0)
        wcol = lax.broadcasted_iota(jnp.int32, (TILE, 2 * TILE), 1)
        dist = 2 + wrow // BLK - wcol // BLK
        kind = jnp.where(
            dist >= 2,
            1.0,
            jnp.where(dist == 1, 2.0, jnp.where((dist == 0) & (wcol - TILE <= wrow), 3.0, 0.0)),
        )
        for t in range(nt_tiles):
            col = segcol[t * TILE : (t + 1) * TILE, :]
            for side in range(2):
                tile = t - 1 + side
                if tile < 0:
                    continue
                same = col == s.segrow[0:1, tile * TILE : (tile + 1) * TILE]
                s.code[t, :, side * TILE : (side + 1) * TILE] = jnp.where(
                    same, kind[:, side * TILE : (side + 1) * TILE], 0.0
                )
        scale = DH ** (-0.25)
        om = omega_ref[...] * scale
        om_high = om.astype(BF16)
        s.omst[0:DH, :] = om_high
        s.omst[DH : 2 * DH, :] = (om - om_high.astype(F32)).astype(BF16)
        s.omtmp[...] = jnp.zeros((LANES, M), F32)
        s.omtmp[0:DH, :] = om
        s.omtmp[DH : DH + 8, :] = (
            lax.broadcasted_iota(jnp.int32, (8, M), 0) == 0
        ).astype(F32)
        s.omt[...] = jnp.transpose(s.omtmp[...]).astype(BF16)
        c_wqkv.wait()
        for c in range(3):
            for h in range(H):
                src = s.wqkv[c * E + h * DH : c * E + (h + 1) * DH, :]
                base = (c * H + h) * LANES
                s.wpad[base : base + DH, :] = src
                s.wpad[base + DH : base + 2 * DH, :] = src if c < 2 else jnp.zeros_like(src)
        for h in range(H):
            s.wopad[h * LANES : h * LANES + DH, :] = s.wo[head, h * DH : (h + 1) * DH, :]
            s.wopad[h * LANES + DH : (h + 1) * LANES, :] = jnp.zeros((DH, D), BF16)
        for h in range(H):
            s.rin[h, STATE:LANES, :] = jnp.zeros((LANES - STATE, M), BF16)
            s.grin[h, STATE:LANES, :] = jnp.zeros((LANES - STATE, M), BF16)

        def features(twice):
            x = twice.astype(F32)
            square = jnp.sum(x * x, axis=-1, keepdims=True)
            projected = nn(twice, s.omst[...])
            return jnp.exp(projected - square * (scale * scale * 0.25)) * (1.0 / math.sqrt(M))

        gain1, bias1 = g1_ref[...].reshape(1, D), b1_ref[...].reshape(1, D)
        gain2, bias2 = g2_ref[...].reshape(1, D), b2_ref[...].reshape(1, D)

        def project(slot):
            xhat, _ = normalize(s.tok[slot].astype(F32))
            normed = (xhat * gain1 + bias1).astype(BF16)
            at = rows(slot)
            s.n1[at, :] = normed
            for c in range(3):
                out = nt(normed, s.wpad[c * H * LANES : (c + 1) * H * LANES, :])
                for h in range(H):
                    part = out[:, h * LANES : (h + 1) * LANES]
                    if c == 2:
                        s.v[h, at, :] = (part + ones_lanes).astype(BF16)
                    else:
                        low_part = part.astype(BF16)
                        (s.q, s.k)[c][h, at, :] = low_part
                        (s.fq, s.fk)[c][h, at, :] = features(low_part).astype(BF16)

        project(head)
        for _, beside, _, _ in ag_tok:
            beside.wait_recv()
        project(h1)
        fw_tok = gather_forward(s.tok, ag_tok)
        project(h2)
        for c in fw_tok:
            c.wait_recv()
        project(h3)

        for h in range(H):
            kk = s.k[h, T - BLK : T, :].astype(F32)
            vv = s.v[h, T - BLK : T, :].astype(F32)
            s.kvout[h] = jnp.where(low, kk, pltpu.roll(vv, DH, 1)).astype(BF16)
        ex_kv = send(s.kvout, s.kvin, seq=other)
        ex_r = []
        for h in range(H):
            v0 = (s.v[h].astype(F32) * s.m0[...]).astype(BF16)
            s.v0[h] = v0
            s.rout[h] = tn(v0, s.fk[h])[:STATE].astype(BF16)
            ex_r.append(send(s.rout.at[h], s.rin.at[h, pl.ds(0, STATE)], seq=other))

        wo_across.wait_recv()
        part = s.wo.at[h2, half_wo]
        wo_batch = send(part, part, batch=b1)

        def attend(h, carry):
            for t in range(nt_tiles):
                lo, hi = t * TILE, (t + 1) * TILE
                w0 = max(0, lo - TILE)
                fq = s.fq[h, lo:hi, :]
                low_rank = nt(fq, s.fk[h, 0:hi, :])
                exact = jnp.exp(nt(s.q[h, lo:hi, :], s.k[h, w0:hi, :]) * (0.5 / math.sqrt(DH)))
                tiles = (hi - w0) // TILE
                code = s.code[t, :, (2 - tiles) * TILE :]
                thr = jnp.concatenate([s.thr[h, lo:hi, :]] * tiles, axis=1)
                near = jnp.where(
                    code >= thr, exact, jnp.where(code >= 1.0, low_rank[:, w0:], 0.0)
                )
                if w0 > 0:
                    col = jnp.concatenate([s.segcol[lo:hi, :]] * (w0 // TILE), axis=1)
                    far = jnp.where(col == s.segrow[0:1, 0:w0], low_rank[:, :w0], 0.0)
                    near = jnp.concatenate([far, near], axis=1)
                w = near.astype(BF16)
                s.w[h, lo:hi, 0:hi] = w
                s.acc[h, lo:hi, :] = nn(w, s.v[h, 0:hi, :])
            return carry

        lax.fori_loop(0, H, attend, 0)

        if inner:
            for j in range(nh):
                lo = j * TILE
                s.n1t[:, lo : lo + TILE] = jnp.transpose(s.n1[lo : lo + TILE, :])

        ex_kv.wait_recv()

        def unpack(packed):
            x = packed.astype(F32)
            turned = pltpu.roll(x, DH, 1)
            twice = jnp.where(low, x, turned).astype(BF16)
            return twice, jnp.where(low, turned, 0.0)

        same_in = s.segcol[0:BLK, 0:BLK] == seg_prev
        for h in range(H):
            k_in, v_in = unpack(s.kvin[h])
            v_in = (v_in + ones_lanes).astype(BF16)
            f_in = features(k_in).astype(BF16)
            s.kin[h] = k_in
            s.vin[h] = v_in
            s.fin[h] = f_in
            q0 = s.q[h, 0:BLK, :]
            fq0 = s.fq[h, 0:BLK, :]
            exact = jnp.exp(nt(q0, k_in) * (0.5 / math.sqrt(DH)))
            low_rank = nt(fq0, f_in)
            use_exact = s.thr[h, 0:BLK, 0:BLK] < 2.5
            w_in = jnp.where(same_in, jnp.where(use_exact, exact, low_rank), 0.0).astype(BF16)
            s.win[h] = w_in
            s.acc[h, 0:BLK, :] = s.acc[h, 0:BLK, :] + nn(w_in, v_in)
            s.last[h] = tn((v_in.astype(F32) * s.mprev[...]).astype(BF16), f_in)
        for h in range(H):
            ex_r[h].wait_recv()
            state = s.rin[h]
            s.rlater[h] = (state.astype(F32) * s.link[0:1, :] + s.last[h]).astype(BF16)

        def add_far(h, lo, hi, state):
            far = nt(s.fq[h, lo:hi, :], state)
            far = jnp.where(s.mfar[lo:hi, :] > 0.5, far, 0.0)
            s.acc[h, lo:hi, :] = s.acc[h, lo:hi, :] + far

        def divided(h, lo, hi):
            acc = s.acc[h, lo:hi, :]
            inv = 1.0 / acc[:, DH : DH + 1]
            return acc * inv, inv

        order = (0, 2, 1, 3)
        ag_at = {}
        for t in order:
            lo, hi = t * TILE, (t + 1) * TILE
            for h in range(H):
                if t == 0:
                    add_far(h, 0, BLK, s.rin[h])
                add_far(h, max(lo, BLK), hi, s.rlater[h])
            outs = [divided(h, lo, hi)[0] for h in range(H)]
            for h in range(0, H, 2):
                if h + 1 < H:
                    both = jnp.where(low, outs[h], pltpu.roll(outs[h + 1], DH, 1))
                    s.at[head, lo:hi, h * DH : (h + 2) * DH] = both.astype(BF16)
                else:
                    s.at[head, lo:hi, h * DH : (h + 1) * DH] = outs[h][:, :DH].astype(BF16)
            part = s.at.at[head, pl.ds(lo, TILE)]
            ag_at[t] = (send(part, part, head=h2), send(part, part, head=h1))
        wo_batch.wait_recv()
        fw_wo = send(s.wo.at[h2], s.wo.at[h2], head=h1)
        fw_og = gather_forward(s.og, ag_og)
        wo_beside.wait_recv()
        fw_wo.wait_recv()
        for _, c, _, _ in ag_og:
            c.wait_recv()
        for c in fw_og:
            c.wait_recv()
        c_wup.wait()
        c_wdown.wait()
        if inner:
            for j in range(nh):
                lo = j * TILE
                s.ogt[:, lo : lo + TILE] = jnp.transpose(s.og[j])
        fw_at = {}

        def forward_attended(t):
            ag_at[t][0].wait_recv()
            part = s.at.at[h2, pl.ds(t * TILE, TILE)]
            fw_at[t] = send(part, part, head=h1)

        def scatter_beside(make, bufs):
            bufs.out[0] = make(h3).astype(BF16)
            a = send(bufs.out.at[0], bufs.got.at[0], head=h1)
            bufs.mine[...] = make(h2)
            return a

        def scatter_across(bufs, a):
            a.wait_recv()
            bufs.out[1] = (bufs.mine[...] + bufs.got[0].astype(F32)).astype(BF16)
            return send(bufs.out.at[1], bufs.got.at[1], head=h2)

        def scatter_last(make, bufs):
            bufs.out[2] = make(h1).astype(BF16)
            return send(bufs.out.at[2], bufs.got.at[2], head=h1)

        def scatter_done(bufs, b, c):
            c.wait_recv()
            part = bufs.got[2].astype(F32)
            b.wait_recv()
            return part + bufs.got[1].astype(F32)

        def feed(slot):
            ag_at[slot][1].wait_recv()
            fw_at[slot].wait_recv()
            at = slice(slot * TILE, (slot + 1) * TILE)
            hid = s.tok[slot].astype(F32)
            for j in range(nh):
                hid = hid + nn(s.at[j, at, :], s.wo[j])
            s.hid[at, :] = hid
            xhat, _ = normalize(hid)
            normed = (xhat * gain2 + bias2).astype(BF16)
            s.n2[at, :] = normed
            act, slope = gelu_both(nn(normed, s.wup[...]))
            s.act[at, :] = act.astype(BF16)
            s.slope[at, :] = slope

        def feed_back(slot):
            at = slice(slot * TILE, (slot + 1) * TILE)
            slope = s.slope[at, :]
            gu = (nt(s.og[slot], s.wdown[...]) * slope).astype(BF16)
            s.gu[at, :] = gu
            s.ra.part[slot] = nt(gu, s.wup[...])

        core = lax.rem(head, 2)
        ra_a = {
            t: prepare(s.ra.out.at[t], s.ra.got.at[t], head=h1) for t in range(nh)
        }
        ra_b = prepare(s.ra.bout, s.ra.bgot, head=h2)

        def to_core(t):
            @pl.when(core != t % 2)
            def _():
                s.ra.out[t] = s.ra.part[t].astype(BF16)
                ra_a[t].start()

        def to_chip(t):
            @pl.when(h2 == t)
            def _():
                ra_a[t].wait_recv()
                s.ra.bout[...] = (s.ra.part[t] + s.ra.got[t].astype(F32)).astype(BF16)
                ra_b.start()

        forward_attended(order[0])
        for i, t in enumerate(order):
            if i + 1 < nh:
                forward_attended(order[i + 1])
            feed(t)

        b2 = lax.rem(bat + 2, nb)
        b3 = lax.rem(b1 + 2, nb)
        there = pl.ds(pl.multiple_of(other * half_rows, LANES), half_rows)
        here = pl.ds(pl.multiple_of(seq * half_rows, LANES), half_rows)

        def y_send(g):
            right = g.right()
            g.ys[...] = nn(g.left[there, :], right).astype(BF16)
            g.y = send(g.ys, g.yr, seq=other)
            g.own[...] = nn(g.left[here, :], right)

        def with_y(g, index):
            at = rows(index, piece)
            return g.own[at, :] + g.yr[at, :].astype(F32)

        def za_send(g):
            g.y.wait_recv()
            for i, index in enumerate((b1, b3)):
                g.zas[i] = with_y(g, index).astype(BF16)
            g.za = send(g.zas, g.zar, batch=b1)

        def zb_send(g):
            g.za.wait_recv()
            g.zbs[...] = (with_y(g, b2) + g.zar[1].astype(F32)).astype(BF16)
            g.zb = send(g.zbs, g.zbr, batch=b2)

        def weight_sum(g):
            total = with_y(g, bat) + g.zar[0].astype(F32)
            g.zb.wait_recv()
            return total + g.zbr[...].astype(F32)

        def zd_send(g):
            g.y.wait_recv()
            g.zd = []
            for i, index in enumerate((b2, b1, b3)):
                g.zds[i] = with_y(g, index).astype(BF16)
                g.zd.append(send(g.zds.at[i], g.zdr.at[i], batch=index))

        def weight_sum_direct(g):
            total = with_y(g, bat)
            for i in (1, 2, 0):
                g.zd[i].wait_recv()
                total = total + g.zdr[i].astype(F32)
            return total

        def both(index):
            return [rows(half * nb + index, piece) for half in range(ns)]

        def first_za(g):
            g.own[...] = nn(g.left[...], g.right())
            for i, index in enumerate((b1, b3)):
                for half, at in enumerate(both(index)):
                    g.zas[i, half] = g.own[at, :].astype(BF16)
            g.za = send(g.zas, g.zar, batch=b1)

        def first_zb(g):
            g.za.wait_recv()
            for half, at in enumerate(both(b2)):
                g.zbs[half] = (g.own[at, :] + g.zar[1, half].astype(F32)).astype(BF16)
            g.zb = send(g.zbs, g.zbr, batch=b2)

        def first_part(g, half):
            at = rows(half * nb + bat, piece)
            return g.own[at, :] + g.zar[0, half].astype(F32) + g.zbr[half].astype(F32)

        def first_y(g):
            g.zb.wait_recv()
            g.ys[...] = first_part(g, other).astype(BF16)
            g.y = send(g.ys, g.yr, seq=other)

        def first_sum(g):
            total = first_part(g, seq)
            g.y.wait_recv()
            return total + g.yr[...].astype(F32)

        def collect(g):
            if hasattr(g, "zdr"):
                return weight_sum_direct(g)
            return weight_sum(g) if g.zbs.shape[0] == piece else first_sum(g)

        def chunks(groups, left, ref):
            width = ref.shape[-1] // len(groups)
            for i, g in enumerate(groups):
                g.left = left
                g.right = lambda i=i: ref[:, i * width : (i + 1) * width]

        steps = {}
        if inner:
            downs, ups, qkvs = (s.d0, s.d1), (s.u0, s.u1), (s.x0, s.x1, s.x2)
            chunks(downs, s.ogt, s.act)
            chunks(ups, s.n2t, s.gu)
            chunks((s.o0,), s.gbt, s.at.at[head])
            chunks(qkvs, s.n1t, s.gqkv)
            steps = {
                0: [(first_za, s.d0), (y_send, s.d1)],
                5: [(first_za, s.u1), (y_send, s.u0)],
                9: [(first_zb, s.d0)],
                10: [(za_send, s.d1)],
                15: [(first_zb, s.u1)],
                17: [(y_send, s.o0)],
                18: [(za_send, s.u0)],
                19: [(y_send, s.x1)],
                20: [(y_send, s.x0)],
                22: [(za_send, s.o0)],
                24: [(zb_send, s.d1)],
                25: [(y_send, s.x2)],
                27: [(za_send, s.x1), (zb_send, s.u0)],
                31: [(za_send, s.x0), (zb_send, s.x1)],
                32: [(zb_send, s.o0)],
                33: [(za_send, s.x2), (first_y, s.u1)],
                34: [(first_y, s.d0), (zb_send, s.x0)],
                36: [(zb_send, s.x2)],
            }

        def run(*numbers):
            for number in numbers:
                for step, group in steps.get(number, ()):
                    step(group)

        run(0)
        for i, t in enumerate(order):
            feed_back(t)
            to_core(t)
            if i > 0:
                to_chip(order[i - 1])
        to_chip(order[-1])
        run(1)
        for t in range(nh):

            @pl.when(head == t)
            def _():
                ra_a[t].wait_recv()

        ra_b.wait_recv()
        run(2)
        grad2 = s.ra.part[head] + s.ra.got[head].astype(F32) + s.ra.bgot[...].astype(F32)
        mine = rows(head)
        xhat2, rstd2 = normalize(s.hid[mine, :])
        s.ns[...] = jnp.zeros_like(s.ns)
        s.ns[2:3, :] = jnp.sum(grad2 * xhat2, axis=0, keepdims=True)
        s.ns[3:4, :] = jnp.sum(grad2, axis=0, keepdims=True)
        grad_hidden = s.og[head].astype(F32) + norm_back(grad2, gain2, xhat2, rstd2)
        s.gh[...] = grad_hidden
        s.gb[head] = grad_hidden.astype(BF16)
        run(3)
        ag_gb = gather_start(s.gb, 2)
        run(4)
        if inner:
            for j in range(nh):
                lo = j * TILE
                s.n2t[:, lo : lo + TILE] = jnp.transpose(s.n2[lo : lo + TILE, :])
        run(5, 6)

        def lower(slot):
            return nn(s.act[rows(slot), :], s.wdown[...])

        rc_a = scatter_beside(lower, s.rc)
        rc_c = scatter_last(lower, s.rc)
        run(7)

        def divide_back(slot):
            at = rows(slot)
            ga = nt(s.gb[slot], s.wopad[...])
            for h in range(H):
                acc = s.acc[h, at, :]
                inv = 1.0 / acc[:, DH : DH + 1]
                gnum = ga[:, h * LANES : (h + 1) * LANES] * inv
                gden = -jnp.sum(gnum * acc, axis=-1, keepdims=True) * inv
                high = gden.astype(BF16).astype(F32)
                gnum = jnp.where(lane == DH, high, jnp.where(lane == DH + 1, gden - high, gnum))
                s.gn[h, at, :] = gnum.astype(BF16)

        divide_back(head)
        for _, c, _, _ in ag_gb:
            c.wait_recv()
        divide_back(h1)
        run(8)
        fw_gb = gather_forward(s.gb, ag_gb)
        divide_back(h2)
        for c in fw_gb:
            c.wait_recv()
        run(9)
        divide_back(h3)
        run(10)

        def feature_back(gfeat, feat, twice):
            x = nn((gfeat * feat.astype(F32)).astype(BF16), s.omt[...])
            return x - twice.astype(F32) * (x[:, DH : DH + 1] * (scale * scale))

        for h in range(H):
            gm = jnp.where(s.mfar[...] > 0.5, s.gn[h].astype(F32), 0.0).astype(BF16)
            s.gm[h] = gm
            glater = tn(gm[BLK:T, :], s.fq[h, BLK:T, :])
            gstate = tn(gm[0:BLK, :], s.fq[h, 0:BLK, :]) + glater * s.link[0:1, :]
            s.grout[h] = gstate[:STATE].astype(BF16)
            glater = glater.astype(BF16)
            v_last = (s.vin[h].astype(F32) * s.mprev[...]).astype(BF16)
            gn0 = s.gn[h, 0:BLK, :]
            q0 = s.q[h, 0:BLK, :]
            fq0 = s.fq[h, 0:BLK, :]
            gw = nt(gn0, s.vin[h])
            w_in = s.win[h]
            use_exact = s.thr[h, 0:BLK, 0:BLK] < 2.5
            gs = jnp.where(
                same_in & use_exact, gw * w_in.astype(F32) * (1.0 / math.sqrt(DH)), 0.0
            ).astype(BF16)
            gp = jnp.where(same_in & jnp.logical_not(use_exact), gw, 0.0).astype(BF16)
            gfeat = tn(gp, fq0) + nn(v_last, glater)
            gk = feature_back(gfeat, s.fin[h], s.kin[h]) + tn(gs, q0)
            gv = tn(w_in, gn0) + s.mprev[...] * nt(s.fin[h], glater)
            s.gkvout[h] = jnp.where(low, gk, pltpu.roll(gv, DH, 1)).astype(BF16)
            s.gfq0[h] = nn(gp, s.fin[h])
            s.gq0[h] = nn(gs, s.kin[h])
        run(11)
        ex_gkv = send(s.gkvout, s.gkvin, seq=other)
        ex_gr = send(s.grout, s.grin.at[:, pl.ds(0, STATE)], seq=other)

        run(12)
        rc_b = scatter_across(s.rc, rc_a)
        run(13)

        def attend_back(h):
            for t in range(nt_tiles):
                lo, hi = t * TILE, (t + 1) * TILE
                w0 = max(0, lo - TILE)
                tiles = (hi - w0) // TILE
                gw = nt(s.gn[h, lo:hi, :], s.v[h, 0:hi, :])
                code = s.code[t, :, (2 - tiles) * TILE :]
                thr = jnp.concatenate([s.thr[h, lo:hi, :]] * tiles, axis=1)
                use_exact = code >= thr
                near = gw[:, w0:]
                gs = jnp.where(
                    use_exact,
                    near * s.w[h, lo:hi, w0:hi].astype(F32) * (1.0 / math.sqrt(DH)),
                    0.0,
                ).astype(BF16)
                gp = jnp.where((code >= 1.0) & (code < thr), near, 0.0)
                if w0 > 0:
                    col = jnp.concatenate([s.segcol[lo:hi, :]] * (w0 // TILE), axis=1)
                    far = jnp.where(col == s.segrow[0:1, 0:w0], gw[:, :w0], 0.0)
                    gp = jnp.concatenate([far, gp], axis=1)
                gp = gp.astype(BF16)
                s.gp[lo:hi, 0:hi] = gp
                s.gs[lo:hi, (2 - tiles) * TILE :] = gs
                gfq = nn(gp, s.fk[h, 0:hi, :])
                gq = nn(gs, s.k[h, w0:hi, :])
                gm = s.gm[h, lo:hi, :]
                if t == 0:
                    top = nn(gm[0:BLK], s.rin[h]) + s.gfq0[h]
                    bottom = nn(gm[BLK:], s.rlater[h])
                    gfq = gfq + jnp.concatenate([top, bottom], axis=0)
                    gq = gq + jnp.concatenate(
                        [s.gq0[h], jnp.zeros((TILE - BLK, LANES), F32)], axis=0
                    )
                else:
                    gfq = gfq + nn(gm, s.rlater[h])
                gq = gq + feature_back(gfq, s.fq[h, lo:hi, :], s.q[h, lo:hi, :])
                s.gq[h, lo:hi, :] = gq
            for t in range(nt_tiles):
                lo, hi = t * TILE, (t + 1) * TILE
                s.gfk[h, lo:hi, :] = tn(s.gp[lo:T, lo:hi], s.fq[h, lo:T, :])
                s.gv[h, lo:hi, :] = tn(s.w[h, lo:T, lo:hi], s.gn[h, lo:T, :])
                gk = tn(s.gs[lo:hi, TILE:], s.q[h, lo:hi, :])
                if t + 1 < nt_tiles:
                    gk = gk + tn(s.gs[hi : hi + TILE, :TILE], s.q[h, hi : hi + TILE, :])
                s.gk[h, lo:hi, :] = gk

        for h in range(H):
            attend_back(h)
            run(14 + min(h, 2))
        if inner:
            for j in range(nh):
                lo = j * TILE
                s.gbt[:, lo : lo + TILE] = jnp.transpose(s.gb[j])
        run(17)

        if inner:
            width = D // (ns * nb * nh)
            start = ((seq * nb + bat) * nh + head) * width
            s.pick[...] = (
                lax.broadcasted_iota(jnp.int32, (D, LANES), 0)
                == lax.broadcasted_iota(jnp.int32, (D, LANES), 1) + start
            ).astype(F32)

        ex_gkv.wait_recv()
        ex_gr.wait_recv()
        run(18)

        def finish(h, carry):
            state = jnp.where(first, s.grin[h].astype(F32), 0.0).astype(BF16)
            gfk = s.gfk[h] + nn(s.v0[h], state)
            fk = s.fk[h]
            gv = s.gv[h] + s.m0[...] * nt(fk, state)
            gk = s.gk[h] + feature_back(gfk, fk, s.k[h])
            s.gk[h] = gk
            s.gv[h] = gv
            back = jnp.where(first, s.gkvin[h].astype(F32), 0.0)
            s.gk[h, T - BLK : T, :] = s.gk[h, T - BLK : T, :] + back
            s.gv[h, T - BLK : T, :] = s.gv[h, T - BLK : T, :] + pltpu.roll(back, DH, 1)
            return carry

        lax.fori_loop(0, H, finish, 0)
        parts = [(n, h) for n in (s.gq, s.gk, s.gv) for h in range(H)]
        for i in range(0, len(parts), 2):
            (na, ha) = parts[i]
            a = na[ha]
            if i + 1 < len(parts):
                (nb_, hb) = parts[i + 1]
                a = jnp.where(low, a, pltpu.roll(nb_[hb], DH, 1))
                s.gqkv[:, i * DH : (i + 2) * DH] = a.astype(BF16)
            else:
                s.gqkv[:, i * DH : (i + 1) * DH] = a[:, :DH].astype(BF16)

        run(19)

        def first_grad(slot):
            return nn(s.gqkv[rows(slot), :], s.wqkv[...])

        rb_a = scatter_beside(first_grad, s.rb)
        run(20)
        rb_b = scatter_across(s.rb, rb_a)
        run(21, 22, 23, 24)
        rb_c = scatter_last(first_grad, s.rb)
        run(25)
        own = first_grad(head)
        run(26)
        own_mixed = s.hid[mine, :] + lower(head)

        run(27, 28)
        grad1 = own + scatter_done(s.rb, rb_b, rb_c)
        run(29)
        xhat1, rstd1 = normalize(s.tok[head].astype(F32))
        s.ns[0:1, :] = jnp.sum(grad1 * xhat1, axis=0, keepdims=True)
        s.ns[1:2, :] = jnp.sum(grad1, axis=0, keepdims=True)
        s.ogtok[...] = s.gh[...] + norm_back(grad1, gain1, xhat1, rstd1)

        if inner:
            run(30)
            n_h = [send(s.ns, s.nh.at[i], head=d) for i, d in enumerate((h1, h2, h3))]
            run(31)
            total = s.ns[...]
            for i, c in enumerate(n_h):
                c.wait_recv()
                total = total + s.nh[i]
            s.ns2[...] = total
            run(32)
            n_y = send(s.ns2, s.ny, seq=other)
            run(33)
        write(s.gh, gtok_ref.at[0])
        s.omixed[...] = (own_mixed + scatter_done(s.rc, rc_b, rc_c)).astype(BF16)
        write(s.omixed, mixed_ref.at[0])
        if inner:
            run(34)
            n_y.wait_recv()
            run(35)
            s.ns3[...] = s.ns2[...] + s.ny[...]
            n_z = [
                send(s.ns3, s.nz.at[d - 1], batch=lax.rem(bat + d, nb)) for d in range(1, nb)
            ]
            run(36, 37)
            wide = FL // 2
            for out, groups, ref in ((s.odown, downs, odown_ref), (s.oup, ups, oup_ref)):
                for i, g in enumerate(groups):
                    out[:, i * wide : (i + 1) * wide] = collect(g)
                write(out, ref)
            s.otmp[...] = jnp.zeros_like(s.otmp)
            s.otmp[0:piece, 0:E] = collect(s.o0)
            s.oout[...] = jnp.transpose(s.otmp[...])[:E, :piece]
            write(s.oout, oout_ref)
            total = s.ns3[...]
            for i, c in enumerate(n_z):
                c.wait_recv()
                total = total + s.nz[i]
            s.onorm[...] = lax.dot_general(
                total, s.pick[...], (((1,), (0,)), ((), ())),
                precision=lax.Precision.HIGHEST, preferred_element_type=F32,
            )
            write(s.onorm, norm_ref)
            for i, g in enumerate(qkvs):
                s.oqkv[i] = collect(g)
                write(s.oqkv.at[i], oqkv_ref.at[i])
        else:

            def joined(ref):
                return jnp.concatenate([ref[j] for j in range(nh)], axis=0)

            write(s.ns, norm_ref)
            s.odown[...] = tn(joined(s.og), s.act[...])
            write(s.odown, odown_ref)
            s.oup[...] = tn(s.n2[...], s.gu[...])
            write(s.oup, oup_ref)
            s.oout[...] = tn(joined(s.gb), s.at[head])
            write(s.oout, oout_ref)
            s.oqkv[...] = tn(s.n1[...], s.gqkv[...])
            write(s.oqkv, oqkv_ref)
        for c in written:
            c.wait()
        for t in range(nh):

            @pl.when(core != t % 2)
            def _():
                ra_a[t].wait_send()

        ra_b.wait_send()
        for c in sends:
            c.wait_send()

    return kernel


def build(dims):
    nh, ns, nb, T, R, D, E, FL, H, M, inner = dims
    plan = Plan()
    piece = D // (ns * nb)
    half = D // ns
    blocks = ns * T // BLK
    plan.add(
        seg=((1, ns * T), jnp.int32),
        pat=((H, blocks), jnp.int32),
        omega=((DH, M), F32),
        g1=((D,), F32),
        b1=((D,), F32),
        g2=((D,), F32),
        b2=((D,), F32),
        tok=((nh, R, D), BF16),
        og=((nh, R, D), BF16),
        wqkv=((3 * E, D), BF16),
        wo=((nh, E, D), BF16),
        wup=((D, FL), BF16),
        wdown=((FL, D), BF16),
        wpad=((3 * H * LANES, D), BF16),
        wopad=((H * LANES, D), BF16),
        segrow=((8, T), F32),
        segcol=((T, LANES), F32),
        m0=((T, LANES), F32),
        mprev=((BLK, LANES), F32),
        link=((8, M), F32),
        mfar=((T, LANES), F32),
        thr=((H, T, LANES), F32),
        code=((T // TILE, TILE, 2 * TILE), F32),
        omst=((2 * DH, M), BF16),
        omtmp=((LANES, M), F32),
        omt=((M, LANES), BF16),
        n1=((T, D), BF16),
        q=((H, T, LANES), BF16),
        k=((H, T, LANES), BF16),
        v=((H, T, LANES), BF16),
        v0=((H, T, LANES), BF16),
        gn=((H, T, LANES), BF16),
        gm=((H, T, LANES), BF16),
        fq=((H, T, M), BF16),
        fk=((H, T, M), BF16),
        rout=((H, STATE, M), BF16),
        grout=((H, STATE, M), BF16),
        rin=((H, LANES, M), BF16),
        grin=((H, LANES, M), BF16),
        rlater=((H, LANES, M), BF16),
        last=((H, LANES, M), F32),
        kvout=((H, BLK, LANES), BF16),
        kvin=((H, BLK, LANES), BF16),
        gkvout=((H, BLK, LANES), BF16),
        gkvin=((H, BLK, LANES), BF16),
        kin=((H, BLK, LANES), BF16),
        vin=((H, BLK, LANES), BF16),
        fin=((H, BLK, M), BF16),
        win=((H, BLK, BLK), BF16),
        gfq0=((H, BLK, M), F32),
        gq0=((H, BLK, LANES), F32),
        w=((H, T, T), BF16),
        acc=((H, T, LANES), F32),
        at=((nh, T, E), BF16),
        hid=((T, D), F32),
        slope=((T, FL), F32),
        n2=((T, D), BF16),
        act=((T, FL), BF16),
        gu=((T, FL), BF16),
        gh=((R, D), F32),
        gb=((nh, R, D), BF16),
        gp=((T, T), BF16),
        gs=((T, 2 * TILE), BF16),
        gfk=((H, T, M), F32),
        gq=((H, T, LANES), F32),
        gk=((H, T, LANES), F32),
        gv=((H, T, LANES), F32),
        gqkv=((T, 3 * E), BF16),
        ns=((8, D), F32),
    )
    pair = dict(out=((3, R, D), BF16), got=((3, R, D), BF16), mine=((R, D), F32))
    plan.group(rb=pair, rc=pair)
    plan.group(
        ra=dict(
            part=((nh, R, D), F32),
            out=((nh, R, D), BF16),
            got=((nh, R, D), BF16),
            bout=((R, D), BF16),
            bgot=((R, D), BF16),
        )
    )
    if inner:

        def weight(width):
            return dict(
                ys=((half, width), BF16),
                yr=((half, width), BF16),
                own=((half, width), F32),
                zas=((2, piece, width), BF16),
                zar=((2, piece, width), BF16),
                zbs=((piece, width), BF16),
                zbr=((piece, width), BF16),
            )

        def weight_direct(width):
            return dict(
                ys=((half, width), BF16),
                yr=((half, width), BF16),
                own=((half, width), F32),
                zds=((nb - 1, piece, width), BF16),
                zdr=((nb - 1, piece, width), BF16),
            )

        def weight_first(width):
            return dict(
                own=((D, width), F32),
                zas=((2, ns, piece, width), BF16),
                zar=((2, ns, piece, width), BF16),
                zbs=((ns, piece, width), BF16),
                zbr=((ns, piece, width), BF16),
                ys=((piece, width), BF16),
                yr=((piece, width), BF16),
            )

        wide, narrow = FL // 2, E
        plan.group(
            d0=weight_first(wide),
            d1=weight(wide),
            u0=weight(wide),
            u1=weight_first(wide),
            o0=weight(narrow),
            x0=weight(narrow),
            x1=weight(narrow),
            x2=weight(narrow),
        )
        turned = ((D, T), BF16)
        plan.add(
            pick=((D, LANES), F32),
        )
        plan.add(n1t=turned, n2t=turned, ogt=turned, gbt=turned)
        plan.add(
            ns2=((8, D), F32),
            ns3=((8, D), F32),
            nz=((nb - 1, 8, D), F32),
            ny=((8, D), F32),
            nh=((3, 8, D), F32),
            otmp=((LANES, 2 * LANES), F32),
        )
    else:
        plan.add(
            odown=((D, FL), F32),
            oup=((D, FL), F32),
            oout=((D, E), F32),
            oqkv=((D, 3 * E), F32),
            omixed=((R, D), BF16),
        )
    plan.semaphores(ssem=96, rsem=96, lsem=32)

    if inner:
        grads = [(3, piece, E), (E, piece), (piece, FL), (piece, FL)]
        norm = (8, LANES)
    else:
        grads = [(D, 3 * E), (D, E), (D, FL), (D, FL)]
        norm = (8, D)
    outs = [((1, R, D), BF16), ((1, R, D), F32), (norm, F32)] + [(g, F32) for g in grads]
    hbm = pl.BlockSpec(memory_space=pltpu.HBM)
    in_specs = [hbm] * 13
    kind, space = (pltpu.VMEM, pltpu.VMEM) if inner else (jax.ShapeDtypeStruct, pltpu.HBM)
    kernel = make_kernel(dims, len(in_specs), len(outs), plan)
    return pl.pallas_call(
        kernel,
        out_shape=[kind(shape, dtype) for shape, dtype in outs],
        in_specs=in_specs,
        out_specs=[pl.BlockSpec(memory_space=space)] * len(outs),
        scratch_shapes=plan.shapes,
        compiler_params=pltpu.CompilerParams(
            collective_id=0, has_side_effects=True, vmem_limit_bytes=(54 if inner else 60) << 20
        ),
        name="block",
    )


def hand_over(width, *arrays):
    count = len(arrays) - 1

    def kernel(*refs):
        ins, norm_ref = refs[:count], refs[count]
        outs, norm_outs = refs[count + 1 : 2 * count + 1], refs[2 * count + 1 :]
        for a, b in zip(ins, outs):
            b[...] = a[...]
        for i, out in enumerate(norm_outs):
            out[...] = norm_ref[i, :width]

    vmem = pl.BlockSpec(memory_space=pltpu.VMEM)
    return pl.pallas_call(
        kernel,
        out_shape=[jax.ShapeDtypeStruct(a.shape, a.dtype) for a in arrays[:-1]]
        + [jax.ShapeDtypeStruct((width,), F32)] * 4,
        in_specs=[vmem] * len(arrays),
        out_specs=[vmem] * (count + 4),
        compiler_params=pltpu.CompilerParams(vmem_limit_bytes=6 << 20),
        name="hand_over",
    )(*arrays)


def per_device(
    mesh_shape,
    tokens,
    seg_ids,
    pattern,
    omega,
    norm1_gain,
    norm1_bias,
    w_qkv,
    w_out,
    norm2_gain,
    norm2_bias,
    w_up,
    w_down,
    out_grad,
):
    nh, ns, nb = mesh_shape
    rows, D = tokens.shape[1:]
    T = seg_ids.shape[1] // ns
    E = w_qkv.shape[2]
    FL = w_up.shape[1]
    piece = D // (ns * nb)
    inner = piece % 16 == 0 and nb == 4
    dims = (nh, ns, nb, T, rows, D, E, FL, E // DH, omega.shape[1], inner)
    w_flat = jnp.transpose(w_qkv, (1, 2, 0)).reshape(3 * E, D)
    arrays = (
        tokens, seg_ids, pattern, omega, norm1_gain, norm1_bias, w_flat, w_out,
        norm2_gain, norm2_bias, w_up, w_down, out_grad,
    )
    arrays = [pltpu.with_memory_space_constraint(a, pltpu.HBM) for a in arrays]
    mixed, grad_tokens, norms, g_qkv, g_out, g_up, g_down = build(dims)(*arrays)
    if inner:
        width = D // (ns * nb * nh)
        mixed, grad_tokens, g_qkv, g_out, g_up, g_down, *norms = hand_over(
            width, mixed, grad_tokens, g_qkv, g_out, g_up, g_down, norms
        )
        g_qkv = jnp.transpose(g_qkv, (1, 0, 2))
        g_down = g_down.T
    else:
        group = ("seq", "batch")
        scatter = functools.partial(lax.psum_scatter, scatter_dimension=0, tiled=True)
        norms = lax.psum_scatter(
            norms[:4], ("seq", "batch", "head"), scatter_dimension=1, tiled=True
        )
        g_qkv = scatter(g_qkv, group).reshape(piece, 3, E)
        g_out = scatter(g_out, group).T
        g_up = scatter(g_up, group)
        g_down = scatter(g_down, group).T
    return (
        mixed, grad_tokens, norms[0], norms[1], g_qkv, g_out, norms[2], norms[3], g_up, g_down,
    )


def solution(mesh):
    placed = (
        P("batch", ("seq", "head"), None),
        P("batch", None),
        P("head", None),
        P(),
        P(),
        P(),
        P(None, None, "head"),
        P("head", None),
        P(),
        P(),
        P(None, "head"),
        P("head", None),
        P("batch", ("seq", "head"), None),
    )
    shape = (mesh.shape["head"], mesh.shape["seq"], mesh.shape["batch"])
    return jax.shard_map(
        functools.partial(per_device, shape),
        mesh=mesh,
        in_specs=placed,
        out_specs=(
            P("batch", ("seq", "head"), None),
            P("batch", ("seq", "head"), None),
            P(("seq", "batch", "head")),
            P(("seq", "batch", "head")),
            P(("seq", "batch"), None, "head"),
            P("head", ("seq", "batch")),
            P(("seq", "batch", "head")),
            P(("seq", "batch", "head")),
            P(("seq", "batch"), "head"),
            P("head", ("seq", "batch")),
        ),
        check_vma=False,
    )
```

```python
import functools
import math
from types import SimpleNamespace

import jax
import jax.numpy as jnp
from jax import lax
from jax.experimental import pallas as pl
from jax.experimental.pallas import tpu as pltpu
from jax.sharding import PartitionSpec as P

DH = 64
BLK = 64
LANES = 128
TILE = 128
STATE = 80
F32 = jnp.float32
BF16 = jnp.bfloat16
MESH = pl.DeviceIdType.MESH


def nn(a, b):
    return lax.dot_general(a, b, (((1,), (0,)), ((), ())), preferred_element_type=F32)


def nt(a, b):
    return lax.dot_general(a, b, (((1,), (1,)), ((), ())), preferred_element_type=F32)


def tn(a, b):
    return lax.dot_general(a, b, (((0,), (0,)), ((), ())), preferred_element_type=F32)


def normalize(x):
    center = x - jnp.mean(x, axis=-1, keepdims=True)
    rstd = lax.rsqrt(jnp.mean(center * center, axis=-1, keepdims=True) + 1e-05)
    return center * rstd, rstd


def norm_back(grad, gain, xhat, rstd):
    g = grad * gain
    return rstd * (
        g - jnp.mean(g, axis=-1, keepdims=True) - xhat * jnp.mean(g * xhat, axis=-1, keepdims=True)
    )


def gelu_both(u):
    k0 = math.sqrt(2.0 / math.pi)
    u2 = u * u
    th = jnp.tanh(k0 * (u + 0.044715 * u2 * u))
    half = 0.5 * (1.0 + th)
    slope = half + 0.5 * u * (1.0 - th * th) * (k0 * (1.0 + 3.0 * 0.044715 * u2))
    return u * half, slope


class Plan:
    def __init__(self):
        self.shapes = []
        self.tree = {}

    def add(self, into=None, **buffers):
        into = self.tree if into is None else into
        for name, (shape, dtype) in buffers.items():
            into[name] = len(self.shapes)
            self.shapes.append(pltpu.VMEM(shape, dtype))

    def group(self, **groups):
        for name, buffers in groups.items():
            self.tree[name] = {}
            self.add(self.tree[name], **buffers)

    def semaphores(self, **counts):
        for name, n in counts.items():
            self.tree[name] = len(self.shapes)
            self.shapes.append(pltpu.SemaphoreType.DMA((n,)))

    def bind(self, refs):
        def walk(tree):
            return SimpleNamespace(
                **{k: walk(v) if isinstance(v, dict) else refs[v] for k, v in tree.items()}
            )

        return walk(self.tree)


def make_kernel(dims, n_in, n_out, plan):
    nh, ns, nb, T, R, D, E, FL, H, M, inner = dims
    nt_tiles = T // TILE
    half_rows = D // ns
    piece = D // (ns * nb)

    def kernel(*refs):
        (
            tok_hbm, seg_hbm, pat_hbm, omega_hbm, g1_hbm, b1_hbm, wqkv_hbm, wout_hbm,
            g2_hbm, b2_hbm, wup_hbm, wdown_hbm, og_hbm,
        ) = refs[:n_in]
        (
            mixed_ref, gtok_ref, norm_ref, oqkv_ref, oout_ref, oup_ref, odown_ref,
        ) = refs[n_in : n_in + n_out]
        s = plan.bind(refs[n_in + n_out :])
        seg_ref, pat_ref, omega_ref = s.seg, s.pat, s.omega
        g1_ref, b1_ref, g2_ref, b2_ref = s.g1, s.b1, s.g2, s.b2
        ssem, rsem, lsem = s.ssem, s.rsem, s.lsem
        used = {"r": 0, "l": 0}
        sends = []

        head = lax.axis_index("head")
        seq = lax.axis_index("seq")
        bat = lax.axis_index("batch")
        h1 = head + 1 - 2 * lax.rem(head, 2)
        h2 = lax.rem(head + 2, nh)
        h3 = lax.rem(h1 + 2, nh)
        other = 1 - seq

        def local(src, dst):
            k = used["l"]
            used["l"] += 1
            c = pltpu.make_async_copy(src, dst, lsem.at[k])
            c.start()
            return c

        written = []

        def write(src, dst):
            if not inner:
                written.append(local(src, dst))

        s.ogtok = s.gh
        if inner:
            s.odown, s.oup, s.oout, s.oqkv = odown_ref, oup_ref, oout_ref, oqkv_ref
            s.onorm, s.omixed, s.ogtok = norm_ref, mixed_ref.at[0], gtok_ref.at[0]

        def send(src, dst, **dev):
            k = used["r"]
            used["r"] += 1
            c = pltpu.make_async_remote_copy(
                src_ref=src, dst_ref=dst, send_sem=ssem.at[k], recv_sem=rsem.at[k],
                device_id=dev, device_id_type=MESH,
            )
            c.start()
            sends.append(c)
            return c

        def prepare(src, dst, **dev):
            k = used["r"]
            used["r"] += 1
            return pltpu.make_async_remote_copy(
                src_ref=src, dst_ref=dst, send_sem=ssem.at[k], recv_sem=rsem.at[k],
                device_id=dev, device_id_type=MESH,
            )

        def rows(slot, n=TILE):
            return pl.ds(pl.multiple_of(slot * n, n), n)

        b1 = bat + 1 - 2 * lax.rem(bat, 2)
        barrier = pltpu.get_barrier_semaphore()
        peers = [dict(head=h1), dict(head=h2), dict(head=h3), dict(seq=other)]
        if inner:
            peers += [dict(batch=lax.rem(bat + d, nb)) for d in range(1, nb)]
        else:
            peers += [dict(batch=b1)]
        for dev in peers:
            pl.semaphore_signal(barrier, inc=1, device_id=dev, device_id_type=MESH)
        c_tok = local(tok_hbm.at[0], s.tok.at[head])
        c_wout = local(wout_hbm, s.wo.at[head])
        c_og = local(og_hbm.at[0], s.og.at[head])
        c_wqkv = local(wqkv_hbm, s.wqkv)
        small = [
            local(a, b)
            for a, b in (
                (seg_hbm, seg_ref), (pat_hbm, pat_ref), (omega_hbm, omega_ref),
                (g1_hbm, g1_ref), (b1_hbm, b1_ref), (g2_hbm, g2_ref), (b2_hbm, b2_ref),
            )
        ]
        c_wup = local(wup_hbm, s.wup)
        c_wdown = local(wdown_hbm, s.wdown)
        pl.semaphore_wait(barrier, len(peers))

        def gather_start(buf, chunks):
            n = buf.shape[1] // chunks
            out = []
            for i in range(chunks):
                part = buf.at[head, pl.ds(i * n, n)]
                across = send(part, part, head=h2)
                beside = send(part, part, head=h1)
                out.append((across, beside, i * n, n))
            return out

        def gather_forward(buf, started):
            out = []
            for across, _, lo, n in started:
                across.wait_recv()
                part = buf.at[h2, pl.ds(lo, n)]
                out.append(send(part, part, head=h1))
            return out

        c_tok.wait()
        ag_tok = gather_start(s.tok, 4)
        c_wout.wait()
        cut = E // 2
        half_wo = pl.ds(pl.multiple_of(lax.rem(bat, 2) * cut, cut), cut)
        part = s.wo.at[head, half_wo]
        wo_across = send(part, part, head=h2)
        wo_beside = send(s.wo.at[head], s.wo.at[head], head=h1)
        c_og.wait()
        ag_og = gather_start(s.og, 1)

        for c in small:
            c.wait()
        lane = lax.broadcasted_iota(jnp.int32, (1, LANES), 1)
        low = lane < DH
        ones_lanes = ((lane == DH) | (lane == DH + 1)).astype(F32)
        seg_all = seg_ref[...].astype(F32)
        first = seq == 0
        seg_half = jnp.where(first, seg_all[:, :T], seg_all[:, T : 2 * T])
        seg_prev = jnp.where(first, -1.0, seg_all[:, T - BLK : T])
        tail_one = jnp.where(first, -1.0, jnp.broadcast_to(seg_all[:, T - 1 : T], (1, LANES)))
        tail_two = jnp.where(
            first, -1.0, jnp.broadcast_to(seg_all[:, T - BLK - 1 : T - BLK], (1, LANES))
        )
        s.segrow[...] = jnp.broadcast_to(seg_half, (8, T))
        s.segcol[...] = jnp.transpose(jnp.broadcast_to(seg_half, (LANES, T)))
        segcol = s.segcol[...]
        row_id = lax.broadcasted_iota(jnp.int32, (T, LANES), 0)
        mask_two = ((segcol == segcol[T - BLK - 1 : T - BLK, :]) & (row_id < T - BLK)).astype(F32)
        prev_col = jnp.transpose(jnp.broadcast_to(seg_prev, (LANES, BLK)))
        s.mprev[...] = (prev_col == tail_one).astype(F32)
        link = (tail_one == tail_two).astype(F32)
        s.link[...] = jnp.broadcast_to(jnp.concatenate([link] * (M // LANES), axis=1), (8, M))
        s.m0[...] = mask_two
        s.mfar[...] = jnp.where(
            row_id < BLK, (segcol == tail_two).astype(F32), (segcol == tail_one).astype(F32)
        )
        nblk = pat_ref.shape[1]
        per_half = T // BLK
        hot = (
            lax.broadcasted_iota(jnp.int32, (T, nblk), 1)
            == lax.broadcasted_iota(jnp.int32, (T, nblk), 0) // BLK + seq * per_half
        ).astype(F32)
        pat = pat_ref[...].astype(F32)
        for h in range(H):
            s.thr[h] = 3.0 - nn(
                (hot * pat[h : h + 1, :]).astype(BF16), jnp.ones((nblk, LANES), BF16)
            )
        wrow = lax.broadcasted_iota(jnp.int32, (TILE, 2 * TILE), 0)
        wcol = lax.broadcasted_iota(jnp.int32, (TILE, 2 * TILE), 1)
        dist = 2 + wrow // BLK - wcol // BLK
        kind = jnp.where(
            dist >= 2,
            1.0,
            jnp.where(dist == 1, 2.0, jnp.where((dist == 0) & (wcol - TILE <= wrow), 3.0, 0.0)),
        )
        for t in range(nt_tiles):
            col = segcol[t * TILE : (t + 1) * TILE, :]
            for side in range(2):
                tile = t - 1 + side
                if tile < 0:
                    continue
                same = col == s.segrow[0:1, tile * TILE : (tile + 1) * TILE]
                s.code[t, :, side * TILE : (side + 1) * TILE] = jnp.where(
                    same, kind[:, side * TILE : (side + 1) * TILE], 0.0
                )
        scale = DH ** (-0.25)
        om = omega_ref[...] * scale
        om_high = om.astype(BF16)
        s.omst[0:DH, :] = om_high
        s.omst[DH : 2 * DH, :] = (om - om_high.astype(F32)).astype(BF16)
        s.omtmp[...] = jnp.zeros((LANES, M), F32)
        s.omtmp[0:DH, :] = om
        s.omtmp[DH : DH + 8, :] = (
            lax.broadcasted_iota(jnp.int32, (8, M), 0) == 0
        ).astype(F32)
        s.omt[...] = jnp.transpose(s.omtmp[...]).astype(BF16)
        c_wqkv.wait()
        for c in range(3):
            for h in range(H):
                src = s.wqkv[c * E + h * DH : c * E + (h + 1) * DH, :]
                base = (c * H + h) * LANES
                s.wpad[base : base + DH, :] = src
                s.wpad[base + DH : base + 2 * DH, :] = src if c < 2 else jnp.zeros_like(src)
        for h in range(H):
            s.wopad[h * LANES : h * LANES + DH, :] = s.wo[head, h * DH : (h + 1) * DH, :]
            s.wopad[h * LANES + DH : (h + 1) * LANES, :] = jnp.zeros((DH, D), BF16)
        for h in range(H):
            s.rin[h, STATE:LANES, :] = jnp.zeros((LANES - STATE, M), BF16)
            s.grin[h, STATE:LANES, :] = jnp.zeros((LANES - STATE, M), BF16)

        def features(twice):
            x = twice.astype(F32)
            square = jnp.sum(x * x, axis=-1, keepdims=True)
            projected = nn(twice, s.omst[...])
            return jnp.exp(projected - square * (scale * scale * 0.25)) * (1.0 / math.sqrt(M))

        gain1, bias1 = g1_ref[...].reshape(1, D), b1_ref[...].reshape(1, D)
        gain2, bias2 = g2_ref[...].reshape(1, D), b2_ref[...].reshape(1, D)

        def project(slot):
            xhat, _ = normalize(s.tok[slot].astype(F32))
            normed = (xhat * gain1 + bias1).astype(BF16)
            at = rows(slot)
            s.n1[at, :] = normed
            for c in range(3):
                out = nt(normed, s.wpad[c * H * LANES : (c + 1) * H * LANES, :])
                for h in range(H):
                    part = out[:, h * LANES : (h + 1) * LANES]
                    if c == 2:
                        s.v[h, at, :] = (part + ones_lanes).astype(BF16)
                    else:
                        low_part = part.astype(BF16)
                        (s.q, s.k)[c][h, at, :] = low_part
                        (s.fq, s.fk)[c][h, at, :] = features(low_part).astype(BF16)

        project(head)
        for _, beside, _, _ in ag_tok:
            beside.wait_recv()
        project(h1)
        fw_tok = gather_forward(s.tok, ag_tok)
        project(h2)
        for c in fw_tok:
            c.wait_recv()
        project(h3)

        for h in range(H):
            kk = s.k[h, T - BLK : T, :].astype(F32)
            vv = s.v[h, T - BLK : T, :].astype(F32)
            s.kvout[h] = jnp.where(low, kk, pltpu.roll(vv, DH, 1)).astype(BF16)
        ex_kv = send(s.kvout, s.kvin, seq=other)
        ex_r = []
        for h in range(H):
            v0 = (s.v[h].astype(F32) * s.m0[...]).astype(BF16)
            s.v0[h] = v0
            s.rout[h] = tn(v0, s.fk[h])[:STATE].astype(BF16)
            ex_r.append(send(s.rout.at[h], s.rin.at[h, pl.ds(0, STATE)], seq=other))

        wo_across.wait_recv()
        part = s.wo.at[h2, half_wo]
        wo_batch = send(part, part, batch=b1)

        def attend(h, carry):
            for t in range(nt_tiles):
                lo, hi = t * TILE, (t + 1) * TILE
                w0 = max(0, lo - TILE)
                fq = s.fq[h, lo:hi, :]
                low_rank = nt(fq, s.fk[h, 0:hi, :])
                exact = jnp.exp(nt(s.q[h, lo:hi, :], s.k[h, w0:hi, :]) * (0.5 / math.sqrt(DH)))
                tiles = (hi - w0) // TILE
                code = s.code[t, :, (2 - tiles) * TILE :]
                thr = jnp.concatenate([s.thr[h, lo:hi, :]] * tiles, axis=1)
                near = jnp.where(
                    code >= thr, exact, jnp.where(code >= 1.0, low_rank[:, w0:], 0.0)
                )
                if w0 > 0:
                    col = jnp.concatenate([s.segcol[lo:hi, :]] * (w0 // TILE), axis=1)
                    far = jnp.where(col == s.segrow[0:1, 0:w0], low_rank[:, :w0], 0.0)
                    near = jnp.concatenate([far, near], axis=1)
                w = near.astype(BF16)
                s.w[h, lo:hi, 0:hi] = w
                s.acc[h, lo:hi, :] = nn(w, s.v[h, 0:hi, :])
            return carry

        lax.fori_loop(0, H, attend, 0)

        if inner:
            for j in range(nh):
                lo = j * TILE
                s.n1t[:, lo : lo + TILE] = jnp.transpose(s.n1[lo : lo + TILE, :])

        ex_kv.wait_recv()

        def unpack(packed):
            x = packed.astype(F32)
            turned = pltpu.roll(x, DH, 1)
            twice = jnp.where(low, x, turned).astype(BF16)
            return twice, jnp.where(low, turned, 0.0)

        same_in = s.segcol[0:BLK, 0:BLK] == seg_prev
        for h in range(H):
            k_in, v_in = unpack(s.kvin[h])
            v_in = (v_in + ones_lanes).astype(BF16)
            f_in = features(k_in).astype(BF16)
            s.kin[h] = k_in
            s.vin[h] = v_in
            s.fin[h] = f_in
            q0 = s.q[h, 0:BLK, :]
            fq0 = s.fq[h, 0:BLK, :]
            exact = jnp.exp(nt(q0, k_in) * (0.5 / math.sqrt(DH)))
            low_rank = nt(fq0, f_in)
            use_exact = s.thr[h, 0:BLK, 0:BLK] < 2.5
            w_in = jnp.where(same_in, jnp.where(use_exact, exact, low_rank), 0.0).astype(BF16)
            s.win[h] = w_in
            s.acc[h, 0:BLK, :] = s.acc[h, 0:BLK, :] + nn(w_in, v_in)
            s.last[h] = tn((v_in.astype(F32) * s.mprev[...]).astype(BF16), f_in)
        for h in range(H):
            ex_r[h].wait_recv()
            state = s.rin[h]
            s.rlater[h] = (state.astype(F32) * s.link[0:1, :] + s.last[h]).astype(BF16)

        def add_far(h, lo, hi, state):
            far = nt(s.fq[h, lo:hi, :], state)
            far = jnp.where(s.mfar[lo:hi, :] > 0.5, far, 0.0)
            s.acc[h, lo:hi, :] = s.acc[h, lo:hi, :] + far

        def divided(h, lo, hi):
            acc = s.acc[h, lo:hi, :]
            inv = 1.0 / acc[:, DH : DH + 1]
            return acc * inv, inv

        order = (0, 2, 1, 3)
        ag_at = {}
        for t in order:
            lo, hi = t * TILE, (t + 1) * TILE
            for h in range(H):
                if t == 0:
                    add_far(h, 0, BLK, s.rin[h])
                add_far(h, max(lo, BLK), hi, s.rlater[h])
            outs = [divided(h, lo, hi)[0] for h in range(H)]
            for h in range(0, H, 2):
                if h + 1 < H:
                    both = jnp.where(low, outs[h], pltpu.roll(outs[h + 1], DH, 1))
                    s.at[head, lo:hi, h * DH : (h + 2) * DH] = both.astype(BF16)
                else:
                    s.at[head, lo:hi, h * DH : (h + 1) * DH] = outs[h][:, :DH].astype(BF16)
            part = s.at.at[head, pl.ds(lo, TILE)]
            ag_at[t] = (send(part, part, head=h2), send(part, part, head=h1))
        wo_batch.wait_recv()
        fw_wo = send(s.wo.at[h2], s.wo.at[h2], head=h1)
        fw_og = gather_forward(s.og, ag_og)
        wo_beside.wait_recv()
        fw_wo.wait_recv()
        for _, c, _, _ in ag_og:
            c.wait_recv()
        for c in fw_og:
            c.wait_recv()
        c_wup.wait()
        c_wdown.wait()
        if inner:
            for j in range(nh):
                lo = j * TILE
                s.ogt[:, lo : lo + TILE] = jnp.transpose(s.og[j])
        fw_at = {}

        def forward_attended(t):
            ag_at[t][0].wait_recv()
            part = s.at.at[h2, pl.ds(t * TILE, TILE)]
            fw_at[t] = send(part, part, head=h1)

        def scatter_beside(make, bufs):
            bufs.out[0] = make(h3).astype(BF16)
            a = send(bufs.out.at[0], bufs.got.at[0], head=h1)
            bufs.mine[...] = make(h2)
            return a

        def scatter_across(bufs, a):
            a.wait_recv()
            bufs.out[1] = (bufs.mine[...] + bufs.got[0].astype(F32)).astype(BF16)
            return send(bufs.out.at[1], bufs.got.at[1], head=h2)

        def scatter_last(make, bufs):
            bufs.out[2] = make(h1).astype(BF16)
            return send(bufs.out.at[2], bufs.got.at[2], head=h1)

        def scatter_done(bufs, b, c):
            c.wait_recv()
            part = bufs.got[2].astype(F32)
            b.wait_recv()
            return part + bufs.got[1].astype(F32)

        def feed(slot):
            ag_at[slot][1].wait_recv()
            fw_at[slot].wait_recv()
            at = slice(slot * TILE, (slot + 1) * TILE)
            hid = s.tok[slot].astype(F32)
            for j in range(nh):
                hid = hid + nn(s.at[j, at, :], s.wo[j])
            s.hid[at, :] = hid
            xhat, _ = normalize(hid)
            normed = (xhat * gain2 + bias2).astype(BF16)
            s.n2[at, :] = normed
            act, slope = gelu_both(nn(normed, s.wup[...]))
            s.act[at, :] = act.astype(BF16)
            s.slope[at, :] = slope

        def feed_back(slot):
            at = slice(slot * TILE, (slot + 1) * TILE)
            slope = s.slope[at, :]
            gu = (nt(s.og[slot], s.wdown[...]) * slope).astype(BF16)
            s.gu[at, :] = gu
            s.ra.part[slot] = nt(gu, s.wup[...])

        core = lax.rem(head, 2)
        ra_a = {
            t: prepare(s.ra.out.at[t], s.ra.got.at[t], head=h1) for t in range(nh)
        }
        ra_b = prepare(s.ra.bout, s.ra.bgot, head=h2)

        def to_core(t):
            @pl.when(core != t % 2)
            def _():
                s.ra.out[t] = s.ra.part[t].astype(BF16)
                ra_a[t].start()

        def to_chip(t):
            @pl.when(h2 == t)
            def _():
                ra_a[t].wait_recv()
                s.ra.bout[...] = (s.ra.part[t] + s.ra.got[t].astype(F32)).astype(BF16)
                ra_b.start()

        forward_attended(order[0])
        for i, t in enumerate(order):
            if i + 1 < nh:
                forward_attended(order[i + 1])
            feed(t)

        b2 = lax.rem(bat + 2, nb)
        b3 = lax.rem(b1 + 2, nb)
        there = pl.ds(pl.multiple_of(other * half_rows, LANES), half_rows)
        here = pl.ds(pl.multiple_of(seq * half_rows, LANES), half_rows)

        def y_send(g):
            right = g.right()
            g.ys[...] = nn(g.left[there, :], right).astype(BF16)
            g.y = send(g.ys, g.yr, seq=other)
            g.own[...] = nn(g.left[here, :], right)

        def with_y(g, index):
            at = rows(index, piece)
            return g.own[at, :] + g.yr[at, :].astype(F32)

        def za_send(g):
            g.y.wait_recv()
            for i, index in enumerate((b1, b3)):
                g.zas[i] = with_y(g, index).astype(BF16)
            g.za = send(g.zas, g.zar, batch=b1)

        def zb_send(g):
            g.za.wait_recv()
            g.zbs[...] = (with_y(g, b2) + g.zar[1].astype(F32)).astype(BF16)
            g.zb = send(g.zbs, g.zbr, batch=b2)

        def weight_sum(g):
            total = with_y(g, bat) + g.zar[0].astype(F32)
            g.zb.wait_recv()
            return total + g.zbr[...].astype(F32)

        def zd_send(g):
            g.y.wait_recv()
            g.zd = []
            for i, index in enumerate((b2, b1, b3)):
                g.zds[i] = with_y(g, index).astype(BF16)
                g.zd.append(send(g.zds.at[i], g.zdr.at[i], batch=index))

        def weight_sum_direct(g):
            total = with_y(g, bat)
            for i in (1, 2, 0):
                g.zd[i].wait_recv()
                total = total + g.zdr[i].astype(F32)
            return total

        def both(index):
            return [rows(half * nb + index, piece) for half in range(ns)]

        def first_za(g):
            g.own[...] = nn(g.left[...], g.right())
            for i, index in enumerate((b1, b3)):
                for half, at in enumerate(both(index)):
                    g.zas[i, half] = g.own[at, :].astype(BF16)
            g.za = send(g.zas, g.zar, batch=b1)

        def first_zb(g):
            g.za.wait_recv()
            for half, at in enumerate(both(b2)):
                g.zbs[half] = (g.own[at, :] + g.zar[1, half].astype(F32)).astype(BF16)
            g.zb = send(g.zbs, g.zbr, batch=b2)

        def first_part(g, half):
            at = rows(half * nb + bat, piece)
            return g.own[at, :] + g.zar[0, half].astype(F32) + g.zbr[half].astype(F32)

        def first_y(g):
            g.zb.wait_recv()
            g.ys[...] = first_part(g, other).astype(BF16)
            g.y = send(g.ys, g.yr, seq=other)

        def first_sum(g):
            total = first_part(g, seq)
            g.y.wait_recv()
            return total + g.yr[...].astype(F32)

        def collect(g):
            if hasattr(g, "zdr"):
                return weight_sum_direct(g)
            return weight_sum(g) if g.zbs.shape[0] == piece else first_sum(g)

        def chunks(groups, left, ref):
            width = ref.shape[-1] // len(groups)
            for i, g in enumerate(groups):
                g.left = left
                g.right = lambda i=i: ref[:, i * width : (i + 1) * width]

        steps = {}
        if inner:
            downs, ups, qkvs = (s.d0, s.d1), (s.u0, s.u1), (s.x0, s.x1, s.x2)
            chunks(downs, s.ogt, s.act)
            chunks(ups, s.n2t, s.gu)
            chunks((s.o0,), s.gbt, s.at.at[head])
            chunks(qkvs, s.n1t, s.gqkv)
            steps = {
                0: [(first_za, s.d0), (y_send, s.d1)],
                5: [(first_za, s.u1), (y_send, s.u0)],
                9: [(first_zb, s.d0)],
                10: [(za_send, s.d1)],
                15: [(first_zb, s.u1)],
                17: [(y_send, s.o0)],
                18: [(za_send, s.u0)],
                19: [(y_send, s.x1)],
                20: [(y_send, s.x0)],
                21: [(zb_send, s.d1)],
                22: [(za_send, s.o0)],
                25: [(y_send, s.x2)],
                27: [(za_send, s.x1), (zb_send, s.u0)],
                31: [(za_send, s.x0), (zb_send, s.x1)],
                32: [(zb_send, s.o0)],
                33: [(za_send, s.x2), (first_y, s.u1)],
                34: [(first_y, s.d0), (zb_send, s.x0)],
                36: [(zb_send, s.x2)],
            }

        def run(*numbers):
            for number in numbers:
                for step, group in steps.get(number, ()):
                    step(group)

        run(0)
        for i, t in enumerate(order):
            feed_back(t)
            to_core(t)
            if i > 0:
                to_chip(order[i - 1])
        to_chip(order[-1])
        run(1)
        for t in range(nh):

            @pl.when(head == t)
            def _():
                ra_a[t].wait_recv()

        ra_b.wait_recv()
        run(2)
        grad2 = s.ra.part[head] + s.ra.got[head].astype(F32) + s.ra.bgot[...].astype(F32)
        mine = rows(head)
        xhat2, rstd2 = normalize(s.hid[mine, :])
        s.ns[...] = jnp.zeros_like(s.ns)
        s.ns[2:3, :] = jnp.sum(grad2 * xhat2, axis=0, keepdims=True)
        s.ns[3:4, :] = jnp.sum(grad2, axis=0, keepdims=True)
        grad_hidden = s.og[head].astype(F32) + norm_back(grad2, gain2, xhat2, rstd2)
        s.gh[...] = grad_hidden
        s.gb[head] = grad_hidden.astype(BF16)
        run(3)
        ag_gb = gather_start(s.gb, 4)
        run(4)
        if inner:
            for j in range(nh):
                lo = j * TILE
                s.n2t[:, lo : lo + TILE] = jnp.transpose(s.n2[lo : lo + TILE, :])
        run(5, 6)

        def lower(slot):
            return nn(s.act[rows(slot), :], s.wdown[...])

        rc_a = scatter_beside(lower, s.rc)
        rc_c = scatter_last(lower, s.rc)
        run(7)

        def divide_back(slot):
            at = rows(slot)
            ga = nt(s.gb[slot], s.wopad[...])
            for h in range(H):
                acc = s.acc[h, at, :]
                inv = 1.0 / acc[:, DH : DH + 1]
                gnum = ga[:, h * LANES : (h + 1) * LANES] * inv
                gden = -jnp.sum(gnum * acc, axis=-1, keepdims=True) * inv
                high = gden.astype(BF16).astype(F32)
                gnum = jnp.where(lane == DH, high, jnp.where(lane == DH + 1, gden - high, gnum))
                s.gn[h, at, :] = gnum.astype(BF16)

        divide_back(head)
        for _, c, _, _ in ag_gb:
            c.wait_recv()
        divide_back(h1)
        run(8)
        fw_gb = gather_forward(s.gb, ag_gb)
        divide_back(h2)
        for c in fw_gb:
            c.wait_recv()
        run(9)
        divide_back(h3)
        run(10)

        def feature_back(gfeat, feat, twice):
            x = nn((gfeat * feat.astype(F32)).astype(BF16), s.omt[...])
            return x - twice.astype(F32) * (x[:, DH : DH + 1] * (scale * scale))

        for h in range(H):
            gm = jnp.where(s.mfar[...] > 0.5, s.gn[h].astype(F32), 0.0).astype(BF16)
            s.gm[h] = gm
            glater = tn(gm[BLK:T, :], s.fq[h, BLK:T, :])
            gstate = tn(gm[0:BLK, :], s.fq[h, 0:BLK, :]) + glater * s.link[0:1, :]
            s.grout[h] = gstate[:STATE].astype(BF16)
            glater = glater.astype(BF16)
            v_last = (s.vin[h].astype(F32) * s.mprev[...]).astype(BF16)
            gn0 = s.gn[h, 0:BLK, :]
            q0 = s.q[h, 0:BLK, :]
            fq0 = s.fq[h, 0:BLK, :]
            gw = nt(gn0, s.vin[h])
            w_in = s.win[h]
            use_exact = s.thr[h, 0:BLK, 0:BLK] < 2.5
            gs = jnp.where(
                same_in & use_exact, gw * w_in.astype(F32) * (1.0 / math.sqrt(DH)), 0.0
            ).astype(BF16)
            gp = jnp.where(same_in & jnp.logical_not(use_exact), gw, 0.0).astype(BF16)
            gfeat = tn(gp, fq0) + nn(v_last, glater)
            gk = feature_back(gfeat, s.fin[h], s.kin[h]) + tn(gs, q0)
            gv = tn(w_in, gn0) + s.mprev[...] * nt(s.fin[h], glater)
            s.gkvout[h] = jnp.where(low, gk, pltpu.roll(gv, DH, 1)).astype(BF16)
            s.gfq0[h] = nn(gp, s.fin[h])
            s.gq0[h] = nn(gs, s.kin[h])
        run(11)
        ex_gkv = send(s.gkvout, s.gkvin, seq=other)
        ex_gr = send(s.grout, s.grin.at[:, pl.ds(0, STATE)], seq=other)

        run(12)
        rc_b = scatter_across(s.rc, rc_a)
        run(13)

        def attend_back(h):
            for t in range(nt_tiles):
                lo, hi = t * TILE, (t + 1) * TILE
                w0 = max(0, lo - TILE)
                tiles = (hi - w0) // TILE
                gw = nt(s.gn[h, lo:hi, :], s.v[h, 0:hi, :])
                code = s.code[t, :, (2 - tiles) * TILE :]
                thr = jnp.concatenate([s.thr[h, lo:hi, :]] * tiles, axis=1)
                use_exact = code >= thr
                near = gw[:, w0:]
                gs = jnp.where(
                    use_exact,
                    near * s.w[h, lo:hi, w0:hi].astype(F32) * (1.0 / math.sqrt(DH)),
                    0.0,
                ).astype(BF16)
                gp = jnp.where((code >= 1.0) & (code < thr), near, 0.0)
                if w0 > 0:
                    col = jnp.concatenate([s.segcol[lo:hi, :]] * (w0 // TILE), axis=1)
                    far = jnp.where(col == s.segrow[0:1, 0:w0], gw[:, :w0], 0.0)
                    gp = jnp.concatenate([far, gp], axis=1)
                gp = gp.astype(BF16)
                s.gp[lo:hi, 0:hi] = gp
                s.gs[lo:hi, (2 - tiles) * TILE :] = gs
                gfq = nn(gp, s.fk[h, 0:hi, :])
                gq = nn(gs, s.k[h, w0:hi, :])
                gm = s.gm[h, lo:hi, :]
                if t == 0:
                    top = nn(gm[0:BLK], s.rin[h]) + s.gfq0[h]
                    bottom = nn(gm[BLK:], s.rlater[h])
                    gfq = gfq + jnp.concatenate([top, bottom], axis=0)
                    gq = gq + jnp.concatenate(
                        [s.gq0[h], jnp.zeros((TILE - BLK, LANES), F32)], axis=0
                    )
                else:
                    gfq = gfq + nn(gm, s.rlater[h])
                gq = gq + feature_back(gfq, s.fq[h, lo:hi, :], s.q[h, lo:hi, :])
                s.gq[h, lo:hi, :] = gq
            for t in range(nt_tiles):
                lo, hi = t * TILE, (t + 1) * TILE
                s.gfk[h, lo:hi, :] = tn(s.gp[lo:T, lo:hi], s.fq[h, lo:T, :])
                s.gv[h, lo:hi, :] = tn(s.w[h, lo:T, lo:hi], s.gn[h, lo:T, :])
                gk = tn(s.gs[lo:hi, TILE:], s.q[h, lo:hi, :])
                if t + 1 < nt_tiles:
                    gk = gk + tn(s.gs[hi : hi + TILE, :TILE], s.q[h, hi : hi + TILE, :])
                s.gk[h, lo:hi, :] = gk

        for h in range(H):
            attend_back(h)
            run(14 + min(h, 2))
        if inner:
            for j in range(nh):
                lo = j * TILE
                s.gbt[:, lo : lo + TILE] = jnp.transpose(s.gb[j])
        run(17)

        if inner:
            width = D // (ns * nb * nh)
            start = ((seq * nb + bat) * nh + head) * width
            s.pick[...] = (
                lax.broadcasted_iota(jnp.int32, (D, LANES), 0)
                == lax.broadcasted_iota(jnp.int32, (D, LANES), 1) + start
            ).astype(F32)

        ex_gkv.wait_recv()
        ex_gr.wait_recv()
        run(18)

        def finish(h, carry):
            state = jnp.where(first, s.grin[h].astype(F32), 0.0).astype(BF16)
            gfk = s.gfk[h] + nn(s.v0[h], state)
            fk = s.fk[h]
            gv = s.gv[h] + s.m0[...] * nt(fk, state)
            gk = s.gk[h] + feature_back(gfk, fk, s.k[h])
            s.gk[h] = gk
            s.gv[h] = gv
            back = jnp.where(first, s.gkvin[h].astype(F32), 0.0)
            s.gk[h, T - BLK : T, :] = s.gk[h, T - BLK : T, :] + back
            s.gv[h, T - BLK : T, :] = s.gv[h, T - BLK : T, :] + pltpu.roll(back, DH, 1)
            return carry

        lax.fori_loop(0, H, finish, 0)
        parts = [(n, h) for n in (s.gq, s.gk, s.gv) for h in range(H)]
        for i in range(0, len(parts), 2):
            (na, ha) = parts[i]
            a = na[ha]
            if i + 1 < len(parts):
                (nb_, hb) = parts[i + 1]
                a = jnp.where(low, a, pltpu.roll(nb_[hb], DH, 1))
                s.gqkv[:, i * DH : (i + 2) * DH] = a.astype(BF16)
            else:
                s.gqkv[:, i * DH : (i + 1) * DH] = a[:, :DH].astype(BF16)

        run(19)

        def first_grad(slot):
            return nn(s.gqkv[rows(slot), :], s.wqkv[...])

        rb_a = scatter_beside(first_grad, s.rb)
        run(20)
        rb_b = scatter_across(s.rb, rb_a)
        run(21, 22, 23, 24)
        rb_c = scatter_last(first_grad, s.rb)
        run(25)
        own = first_grad(head)
        run(26)
        own_mixed = s.hid[mine, :] + lower(head)

        run(27, 28)
        grad1 = own + scatter_done(s.rb, rb_b, rb_c)
        run(29)
        xhat1, rstd1 = normalize(s.tok[head].astype(F32))
        s.ns[0:1, :] = jnp.sum(grad1 * xhat1, axis=0, keepdims=True)
        s.ns[1:2, :] = jnp.sum(grad1, axis=0, keepdims=True)
        s.ogtok[...] = s.gh[...] + norm_back(grad1, gain1, xhat1, rstd1)

        if inner:
            run(30)
            n_h = [send(s.ns, s.nh.at[i], head=d) for i, d in enumerate((h1, h2, h3))]
            run(31)
            total = s.ns[...]
            for i, c in enumerate(n_h):
                c.wait_recv()
                total = total + s.nh[i]
            s.ns2[...] = total
            run(32)
            n_y = send(s.ns2, s.ny, seq=other)
            run(33)
        write(s.gh, gtok_ref.at[0])
        s.omixed[...] = (own_mixed + scatter_done(s.rc, rc_b, rc_c)).astype(BF16)
        write(s.omixed, mixed_ref.at[0])
        if inner:
            run(34)
            n_y.wait_recv()
            run(35)
            s.ns3[...] = s.ns2[...] + s.ny[...]
            n_z = [
                send(s.ns3, s.nz.at[d - 1], batch=lax.rem(bat + d, nb)) for d in range(1, nb)
            ]
            run(36, 37)
            wide = FL // 2
            for out, groups, ref in ((s.odown, downs, odown_ref), (s.oup, ups, oup_ref)):
                for i, g in enumerate(groups):
                    out[:, i * wide : (i + 1) * wide] = collect(g)
                write(out, ref)
            s.otmp[...] = jnp.zeros_like(s.otmp)
            s.otmp[0:piece, 0:E] = collect(s.o0)
            s.oout[...] = jnp.transpose(s.otmp[...])[:E, :piece]
            write(s.oout, oout_ref)
            total = s.ns3[...]
            for i, c in enumerate(n_z):
                c.wait_recv()
                total = total + s.nz[i]
            s.onorm[...] = lax.dot_general(
                total, s.pick[...], (((1,), (0,)), ((), ())),
                precision=lax.Precision.HIGHEST, preferred_element_type=F32,
            )
            write(s.onorm, norm_ref)
            for i, g in enumerate(qkvs):
                s.oqkv[i] = collect(g)
                write(s.oqkv.at[i], oqkv_ref.at[i])
        else:

            def joined(ref):
                return jnp.concatenate([ref[j] for j in range(nh)], axis=0)

            write(s.ns, norm_ref)
            s.odown[...] = tn(joined(s.og), s.act[...])
            write(s.odown, odown_ref)
            s.oup[...] = tn(s.n2[...], s.gu[...])
            write(s.oup, oup_ref)
            s.oout[...] = tn(joined(s.gb), s.at[head])
            write(s.oout, oout_ref)
            s.oqkv[...] = tn(s.n1[...], s.gqkv[...])
            write(s.oqkv, oqkv_ref)
        for c in written:
            c.wait()
        for t in range(nh):

            @pl.when(core != t % 2)
            def _():
                ra_a[t].wait_send()

        ra_b.wait_send()
        for c in sends:
            c.wait_send()

    return kernel


def build(dims):
    nh, ns, nb, T, R, D, E, FL, H, M, inner = dims
    plan = Plan()
    piece = D // (ns * nb)
    half = D // ns
    blocks = ns * T // BLK
    plan.add(
        seg=((1, ns * T), jnp.int32),
        pat=((H, blocks), jnp.int32),
        omega=((DH, M), F32),
        g1=((D,), F32),
        b1=((D,), F32),
        g2=((D,), F32),
        b2=((D,), F32),
        tok=((nh, R, D), BF16),
        og=((nh, R, D), BF16),
        wqkv=((3 * E, D), BF16),
        wo=((nh, E, D), BF16),
        wup=((D, FL), BF16),
        wdown=((FL, D), BF16),
        wpad=((3 * H * LANES, D), BF16),
        wopad=((H * LANES, D), BF16),
        segrow=((8, T), F32),
        segcol=((T, LANES), F32),
        m0=((T, LANES), F32),
        mprev=((BLK, LANES), F32),
        link=((8, M), F32),
        mfar=((T, LANES), F32),
        thr=((H, T, LANES), F32),
        code=((T // TILE, TILE, 2 * TILE), F32),
        omst=((2 * DH, M), BF16),
        omtmp=((LANES, M), F32),
        omt=((M, LANES), BF16),
        n1=((T, D), BF16),
        q=((H, T, LANES), BF16),
        k=((H, T, LANES), BF16),
        v=((H, T, LANES), BF16),
        v0=((H, T, LANES), BF16),
        gn=((H, T, LANES), BF16),
        gm=((H, T, LANES), BF16),
        fq=((H, T, M), BF16),
        fk=((H, T, M), BF16),
        rout=((H, STATE, M), BF16),
        grout=((H, STATE, M), BF16),
        rin=((H, LANES, M), BF16),
        grin=((H, LANES, M), BF16),
        rlater=((H, LANES, M), BF16),
        last=((H, LANES, M), F32),
        kvout=((H, BLK, LANES), BF16),
        kvin=((H, BLK, LANES), BF16),
        gkvout=((H, BLK, LANES), BF16),
        gkvin=((H, BLK, LANES), BF16),
        kin=((H, BLK, LANES), BF16),
        vin=((H, BLK, LANES), BF16),
        fin=((H, BLK, M), BF16),
        win=((H, BLK, BLK), BF16),
        gfq0=((H, BLK, M), F32),
        gq0=((H, BLK, LANES), F32),
        w=((H, T, T), BF16),
        acc=((H, T, LANES), F32),
        at=((nh, T, E), BF16),
        hid=((T, D), F32),
        slope=((T, FL), F32),
        n2=((T, D), BF16),
        act=((T, FL), BF16),
        gu=((T, FL), BF16),
        gh=((R, D), F32),
        gb=((nh, R, D), BF16),
        gp=((T, T), BF16),
        gs=((T, 2 * TILE), BF16),
        gfk=((H, T, M), F32),
        gq=((H, T, LANES), F32),
        gk=((H, T, LANES), F32),
        gv=((H, T, LANES), F32),
        gqkv=((T, 3 * E), BF16),
        ns=((8, D), F32),
    )
    pair = dict(out=((3, R, D), BF16), got=((3, R, D), BF16), mine=((R, D), F32))
    plan.group(rb=pair, rc=pair)
    plan.group(
        ra=dict(
            part=((nh, R, D), F32),
            out=((nh, R, D), BF16),
            got=((nh, R, D), BF16),
            bout=((R, D), BF16),
            bgot=((R, D), BF16),
        )
    )
    if inner:

        def weight(width):
            return dict(
                ys=((half, width), BF16),
                yr=((half, width), BF16),
                own=((half, width), F32),
                zas=((2, piece, width), BF16),
                zar=((2, piece, width), BF16),
                zbs=((piece, width), BF16),
                zbr=((piece, width), BF16),
            )

        def weight_direct(width):
            return dict(
                ys=((half, width), BF16),
                yr=((half, width), BF16),
                own=((half, width), F32),
                zds=((nb - 1, piece, width), BF16),
                zdr=((nb - 1, piece, width), BF16),
            )

        def weight_first(width):
            return dict(
                own=((D, width), F32),
                zas=((2, ns, piece, width), BF16),
                zar=((2, ns, piece, width), BF16),
                zbs=((ns, piece, width), BF16),
                zbr=((ns, piece, width), BF16),
                ys=((piece, width), BF16),
                yr=((piece, width), BF16),
            )

        wide, narrow = FL // 2, E
        plan.group(
            d0=weight_first(wide),
            d1=weight(wide),
            u0=weight(wide),
            u1=weight_first(wide),
            o0=weight(narrow),
            x0=weight(narrow),
            x1=weight(narrow),
            x2=weight(narrow),
        )
        turned = ((D, T), BF16)
        plan.add(
            pick=((D, LANES), F32),
        )
        plan.add(n1t=turned, n2t=turned, ogt=turned, gbt=turned)
        plan.add(
            ns2=((8, D), F32),
            ns3=((8, D), F32),
            nz=((nb - 1, 8, D), F32),
            ny=((8, D), F32),
            nh=((3, 8, D), F32),
            otmp=((LANES, 2 * LANES), F32),
        )
    else:
        plan.add(
            odown=((D, FL), F32),
            oup=((D, FL), F32),
            oout=((D, E), F32),
            oqkv=((D, 3 * E), F32),
            omixed=((R, D), BF16),
        )
    plan.semaphores(ssem=96, rsem=96, lsem=32)

    if inner:
        grads = [(3, piece, E), (E, piece), (piece, FL), (piece, FL)]
        norm = (8, LANES)
    else:
        grads = [(D, 3 * E), (D, E), (D, FL), (D, FL)]
        norm = (8, D)
    outs = [((1, R, D), BF16), ((1, R, D), F32), (norm, F32)] + [(g, F32) for g in grads]
    hbm = pl.BlockSpec(memory_space=pltpu.HBM)
    in_specs = [hbm] * 13
    kind, space = (pltpu.VMEM, pltpu.VMEM) if inner else (jax.ShapeDtypeStruct, pltpu.HBM)
    kernel = make_kernel(dims, len(in_specs), len(outs), plan)
    return pl.pallas_call(
        kernel,
        out_shape=[kind(shape, dtype) for shape, dtype in outs],
        in_specs=in_specs,
        out_specs=[pl.BlockSpec(memory_space=space)] * len(outs),
        scratch_shapes=plan.shapes,
        compiler_params=pltpu.CompilerParams(
            collective_id=0, has_side_effects=True, vmem_limit_bytes=(54 if inner else 60) << 20
        ),
        name="block",
    )


def hand_over(width, *arrays):
    count = len(arrays) - 1

    def kernel(*refs):
        ins, norm_ref = refs[:count], refs[count]
        outs, norm_outs = refs[count + 1 : 2 * count + 1], refs[2 * count + 1 :]
        for a, b in zip(ins, outs):
            b[...] = a[...]
        for i, out in enumerate(norm_outs):
            out[...] = norm_ref[i, :width]

    vmem = pl.BlockSpec(memory_space=pltpu.VMEM)
    return pl.pallas_call(
        kernel,
        out_shape=[jax.ShapeDtypeStruct(a.shape, a.dtype) for a in arrays[:-1]]
        + [jax.ShapeDtypeStruct((width,), F32)] * 4,
        in_specs=[vmem] * len(arrays),
        out_specs=[vmem] * (count + 4),
        compiler_params=pltpu.CompilerParams(vmem_limit_bytes=6 << 20),
        name="hand_over",
    )(*arrays)


def per_device(
    mesh_shape,
    tokens,
    seg_ids,
    pattern,
    omega,
    norm1_gain,
    norm1_bias,
    w_qkv,
    w_out,
    norm2_gain,
    norm2_bias,
    w_up,
    w_down,
    out_grad,
):
    nh, ns, nb = mesh_shape
    rows, D = tokens.shape[1:]
    T = seg_ids.shape[1] // ns
    E = w_qkv.shape[2]
    FL = w_up.shape[1]
    piece = D // (ns * nb)
    inner = piece % 16 == 0 and nb == 4
    dims = (nh, ns, nb, T, rows, D, E, FL, E // DH, omega.shape[1], inner)
    w_flat = jnp.transpose(w_qkv, (1, 2, 0)).reshape(3 * E, D)
    arrays = (
        tokens, seg_ids, pattern, omega, norm1_gain, norm1_bias, w_flat, w_out,
        norm2_gain, norm2_bias, w_up, w_down, out_grad,
    )
    arrays = [pltpu.with_memory_space_constraint(a, pltpu.HBM) for a in arrays]
    mixed, grad_tokens, norms, g_qkv, g_out, g_up, g_down = build(dims)(*arrays)
    if inner:
        width = D // (ns * nb * nh)
        mixed, grad_tokens, g_qkv, g_out, g_up, g_down, *norms = hand_over(
            width, mixed, grad_tokens, g_qkv, g_out, g_up, g_down, norms
        )
        g_qkv = jnp.transpose(g_qkv, (1, 0, 2))
        g_down = g_down.T
    else:
        group = ("seq", "batch")
        scatter = functools.partial(lax.psum_scatter, scatter_dimension=0, tiled=True)
        norms = lax.psum_scatter(
            norms[:4], ("seq", "batch", "head"), scatter_dimension=1, tiled=True
        )
        g_qkv = scatter(g_qkv, group).reshape(piece, 3, E)
        g_out = scatter(g_out, group).T
        g_up = scatter(g_up, group)
        g_down = scatter(g_down, group).T
    return (
        mixed, grad_tokens, norms[0], norms[1], g_qkv, g_out, norms[2], norms[3], g_up, g_down,
    )


def solution(mesh):
    placed = (
        P("batch", ("seq", "head"), None),
        P("batch", None),
        P("head", None),
        P(),
        P(),
        P(),
        P(None, None, "head"),
        P("head", None),
        P(),
        P(),
        P(None, "head"),
        P("head", None),
        P("batch", ("seq", "head"), None),
    )
    shape = (mesh.shape["head"], mesh.shape["seq"], mesh.shape["batch"])
    return jax.shard_map(
        functools.partial(per_device, shape),
        mesh=mesh,
        in_specs=placed,
        out_specs=(
            P("batch", ("seq", "head"), None),
            P("batch", ("seq", "head"), None),
            P(("seq", "batch", "head")),
            P(("seq", "batch", "head")),
            P(("seq", "batch"), None, "head"),
            P("head", ("seq", "batch")),
            P(("seq", "batch", "head")),
            P(("seq", "batch", "head")),
            P(("seq", "batch"), "head"),
            P("head", ("seq", "batch")),
        ),
        check_vma=False,
    )
```
